32 devices in a mesh: space: 8 (over y, x, core), frame: 4 (over z).
Axes of the slice: x: 2, y: 2, z: 4, core: 2. Of those that a mesh axis runs over, the one named last changes fastest.
Arguments:
- features: bfloat16 [4, 32, 8, 8, 512], P('frame', 'space'), may hold values from -6 to 6
- occupancy: int32 [4, 32, 512], P('frame', 'space'), may hold values 0 or 1
- w_spatial: bfloat16 [2, 27, 64, 64], replicated, may hold values from -0.21875 to 0.21875
- b_spatial: float32 [2, 64], replicated, may hold values from -3 to 3
- w_temporal: bfloat16 [3, 64, 64], replicated, may hold values from -0.75 to 0.75
- face_send: int32 [4, 16], P('frame', 'space'), may hold values from -1 to 19, as said below
- face_source: int32 [4, 32, 6], P('frame', 'space'), may hold values from -1 to 25, as said below
- send_ahead: int32 [4, 24], P('frame', 'space'), may hold values from 0 to 3, as said below
- from_prior: int32 [4, 32], P('frame', 'space'), may hold values from -1 to 2, as said below
- send_back: int32 [4, 24], P('frame', 'space'), may hold values from 0 to 3, as said below
- from_later: int32 [4, 32], P('frame', 'space'), may hold values from -1 to 2, as said below
Outputs:
- section_out: bfloat16 [4, 32, 8, 8, 512], P('frame', 'space')
The draws below stay inside these ranges and needn't reach their ends.
Inputs may be any that keep to these rules, and one draw needn't show every extreme that they name: `face_send`: entries 0 to 0 of a device's row are the faces it sends to the device one lower in space, as brick * 6 + 0 of 1 distinct own bricks; entries 1 to 1 those it sends to the device one higher, as brick * 6 + 1 of 1 distinct own bricks; all -1 toward a side where the axis ends. `face_source`: entry (b, f) names an entry of the device's table: k < 1 a face from the device below (only for f = 0), 1 + k one from the device above (only for f = 1), 2 + 6 j + g face g of brick j of the same device, the opposite of f; or -1. Every received face is named exactly once; local pairs are mutual. `send_ahead`: each device's 3 entries are distinct bricks of that device. `from_prior`: -1 for every brick of frame 0; in other frames exactly 3 bricks of each device name a slot, each slot once. `send_back`: each device's 3 entries are distinct bricks of that device. `from_later`: -1 for every brick of the last frame; in other frames exactly 3 bricks of each device name a slot, each slot once.
All inputs are finite; a program needn't handle non-finite values. No bound on the sum of `occupancy` on one device may be relied on, other than what follows from the above.
Results may differ from the reference program's by a relative error of at most 0.0049.
Values may be sent and summed in bfloat16 or wider, within the bound.
No kernel may reach another device: no remote copies, remote signals or barrier semaphores. Data moves between devices by JAX's collectives and lax.ppermute only.
A program may use at most 64 MiB of HBM per device.

```python
import jax
import jax.numpy as jnp
from jax import lax

CH = 64
EDGE = 8
LAYERS = 2
BR = 4
SLABS = 1
MATCH = 3
FRAMES = 4
BRICKS = 32
N_SPACE = 8


def last_first(sub_key):
    order = jax.random.permutation(sub_key, BR).astype(jnp.int32)
    where_last = jnp.argmax(order == BR - 1).astype(jnp.int32)
    order = order.at[where_last].set(order[0])
    return order.at[0].set(BR - 1)


def rim_tables(key):
    base_key = jax.random.fold_in(key, 31)

    def one_device(own_id, orders):
        down_bricks = orders[0, :SLABS].astype(jnp.int32)
        up_bricks = orders[1, :SLABS].astype(jnp.int32)
        slot_ids = jnp.arange(SLABS, dtype=jnp.int32)
        local_base = 2 * SLABS
        naming = jnp.full((BR * 6,), -1, jnp.int32)
        naming = naming.at[jnp.where(own_id > 0, down_bricks * 6, BR * 6)].set(slot_ids, mode='drop')
        naming = naming.at[jnp.where(own_id < N_SPACE - 1, up_bricks * 6 + 1, BR * 6)].set(SLABS + slot_ids, mode='drop')
        pair_count = BR // 4
        for order_row, low_face in ((2, 2), (3, 4)):
            chosen = orders[order_row].astype(jnp.int32)
            first = chosen[0:2 * pair_count:2]
            second = chosen[1:2 * pair_count:2]
            naming = naming.at[second * 6 + low_face].set(local_base + first * 6 + low_face + 1)
            naming = naming.at[first * 6 + low_face + 1].set(local_base + second * 6 + low_face)
        send_low = jnp.where(own_id > 0, down_bricks * 6, -1)
        send_high = jnp.where(own_id < N_SPACE - 1, up_bricks * 6 + 1, -1)
        return (jnp.concatenate([send_low, send_high]), naming.reshape(BR, 6))

    def one_frame(frame_key):
        orders = jax.vmap(last_first)(jax.random.split(frame_key, N_SPACE * 4)).reshape(N_SPACE, 4, BR)
        return jax.vmap(one_device)(jnp.arange(N_SPACE, dtype=jnp.int32), orders)
    sending, naming = jax.vmap(one_frame)(jax.random.split(base_key, FRAMES))
    return (sending.reshape(FRAMES, N_SPACE * 2 * SLABS).astype(jnp.int32), naming.reshape(FRAMES, N_SPACE * BR, 6).astype(jnp.int32))


def frame_links(key, salt_value):
    base_key = jax.random.fold_in(key, salt_value)
    shuffles = jax.vmap(last_first)(jax.random.split(base_key, FRAMES * N_SPACE * 2)).reshape(FRAMES, N_SPACE, 2, BR)
    senders = shuffles[:, :, 0, :MATCH].astype(jnp.int32)
    takers = shuffles[:, :, 1, :MATCH]
    matches = (takers[:, :, :, None] == jnp.arange(BR)[None, None, None, :]).astype(jnp.int32)
    slot_ids = jnp.sum(matches * (jnp.arange(MATCH, dtype=jnp.int32) + 1)[None, None, :, None], axis=2) - 1
    return (senders, slot_ids.astype(jnp.int32))


def draw_face_send(key, part):
    return rim_tables(key)[0]


def draw_face_source(key, part):
    return rim_tables(key)[1]


def draw_send_ahead(key, part):
    senders, slot_ids = frame_links(key, 11)
    return senders.reshape(FRAMES, N_SPACE * MATCH)


def draw_from_prior(key, part):
    senders, slot_ids = frame_links(key, 11)
    first = (jnp.arange(FRAMES) == 0)[:, None, None]
    return jnp.where(first, -1, slot_ids).reshape(FRAMES, N_SPACE * BR).astype(jnp.int32)


def draw_send_back(key, part):
    senders, slot_ids = frame_links(key, 12)
    return senders.reshape(FRAMES, N_SPACE * MATCH)


def draw_from_later(key, part):
    senders, slot_ids = frame_links(key, 12)
    final = (jnp.arange(FRAMES) == FRAMES - 1)[:, None, None]
    return jnp.where(final, -1, slot_ids).reshape(FRAMES, N_SPACE * BR).astype(jnp.int32)


def with_ends(drawn, rng, low, high):
    dims = drawn.shape
    index_at = [jax.random.randint(jax.random.fold_in(rng, axis), (), 0, dims[axis]) for axis in range(len(dims))]
    drawn = drawn.at[tuple(index_at)].set(low)
    longest = dims.index(max(dims))
    index_at[longest] = (index_at[longest] + 1) % dims[longest]
    return drawn.at[tuple(index_at)].set(high)


def levels(rng, extent, cuts, smallest, top_value):
    factor_of = 1.0
    for position, parts in cuts:
        steps = jax.random.uniform(jax.random.fold_in(jax.random.fold_in(rng, 6), position), (parts,), jnp.float32, smallest / len(cuts), top_value / len(cuts))
        factor_of = factor_of * jnp.repeat(jnp.exp(steps), extent[position] // parts).reshape((-1,) + (1,) * (len(extent) - 1 - position))
    return factor_of


def normal_values(key, extent, deviation, bound, cuts=(), kind=jnp.bfloat16):
    entries = jax.random.normal(key, extent, jnp.float32) * deviation
    if len(cuts) > 0:
        entries = levels(key, extent, cuts, -0.22, 0.18) * entries
    return jnp.clip(entries, min=-bound, max=bound).astype(kind)


def setup_inputs(seed: int = 0) -> dict:
    streams_of = jax.random.split(jax.random.key(seed), 12)
    features = normal_values(streams_of[0], (FRAMES, BRICKS, EDGE, EDGE, EDGE * CH), 1.0, 6.0, ((0, 4), (1, 8)))
    occupancy = with_ends((jax.random.randint(streams_of[1], (FRAMES, BRICKS, EDGE * EDGE * EDGE), 0, 4) < 3).astype(jnp.int32), jax.random.fold_in(streams_of[1], 1), 0, 1)
    w_spatial = normal_values(streams_of[2], (LAYERS, 27, CH, CH), (12 * CH) ** -0.5, 0.21875)
    b_spatial = normal_values(streams_of[3], (LAYERS, CH), 0.5, 3.0, (), jnp.float32)
    w_temporal = normal_values(streams_of[4], (3, CH, CH), CH ** -0.5, 0.75)
    face_send = draw_face_send(jax.random.fold_in(streams_of[11], 71), 0)
    face_source = draw_face_source(jax.random.fold_in(streams_of[11], 71), 0)
    send_ahead = draw_send_ahead(jax.random.fold_in(streams_of[11], 71), 0)
    from_prior = draw_from_prior(jax.random.fold_in(streams_of[11], 71), 0)
    send_back = draw_send_back(jax.random.fold_in(streams_of[11], 71), 0)
    from_later = draw_from_later(jax.random.fold_in(streams_of[11], 71), 0)
    return {"features": features, "occupancy": occupancy, "w_spatial": w_spatial, "b_spatial": b_spatial, "w_temporal": w_temporal, "face_send": face_send, "face_source": face_source, "send_ahead": send_ahead, "from_prior": from_prior, "send_back": send_back, "from_later": from_later}


def voxel_mask(occupied, edge_len, channels):
    bricks = occupied.shape[0]
    shaped = occupied.astype(jnp.float32).reshape(bricks, edge_len, edge_len, edge_len, 1)
    return jnp.broadcast_to(shaped, (bricks, edge_len, edge_len, edge_len, channels)).reshape(bricks, edge_len, edge_len, edge_len * channels)


def face_layers(field_data, edge_len, channels):
    bricks = field_data.shape[0]
    volume = field_data.reshape(bricks, edge_len, edge_len, edge_len, channels)
    planes = [volume[:, :, :, 0], volume[:, :, :, edge_len - 1], volume[:, :, 0], volume[:, :, edge_len - 1], volume[:, 0], volume[:, edge_len - 1]]
    stacked = jnp.stack([single.reshape(bricks, edge_len, edge_len * channels) for single in planes], axis=1)
    return stacked.reshape(bricks * 6, edge_len, edge_len * channels)


def padded_block(field_data, rim_faces, edge_len, channels):
    bricks = field_data.shape[0]
    wide_cols = (edge_len + 2) * channels
    inner = slice(1, edge_len + 1)
    middle = slice(channels, (edge_len + 1) * channels)
    padded = jnp.zeros((bricks, edge_len + 2, edge_len + 2, wide_cols), jnp.bfloat16)
    padded = padded.at[:, inner, inner, middle].set(field_data)
    padded = padded.at[:, inner, inner, 0:channels].set(rim_faces[:, 0].reshape(bricks, edge_len, edge_len, channels))
    padded = padded.at[:, inner, inner, (edge_len + 1) * channels:wide_cols].set(rim_faces[:, 1].reshape(bricks, edge_len, edge_len, channels))
    padded = padded.at[:, inner, 0, middle].set(rim_faces[:, 2])
    padded = padded.at[:, inner, edge_len + 1, middle].set(rim_faces[:, 3])
    padded = padded.at[:, 0, inner, middle].set(rim_faces[:, 4])
    padded = padded.at[:, edge_len + 1, inner, middle].set(rim_faces[:, 5])
    return padded


def conv_exact(padded, weights, bias_row, keep_mask, edge_len, channels, group_size):
    bricks = padded.shape[0]

    def one_group(pieces):
        piece_block, piece_mask = pieces
        shifted = []
        for depth_off in range(3):
            for row_off in range(3):
                for col_off in range(3):
                    shifted.append(piece_block[:, depth_off:depth_off + edge_len, row_off:row_off + edge_len, col_off * channels:col_off * channels + edge_len * channels])
        columns = jnp.stack(shifted, axis=1).reshape(group_size, 27, edge_len, edge_len, edge_len, channels)
        summed = jnp.einsum("btzyxc,tcd->bzyxd", columns.astype(jnp.float32), weights.astype(jnp.float32))
        summed = summed.reshape(group_size, edge_len, edge_len, edge_len * channels) + jnp.tile(bias_row, edge_len)
        return (jnp.maximum(summed, 0.0) * piece_mask).astype(jnp.bfloat16)

    grouped = lax.map(one_group, (padded.reshape((bricks // group_size, group_size) + padded.shape[1:]), keep_mask.reshape((bricks // group_size, group_size) + keep_mask.shape[1:])))
    return grouped.reshape(bricks, edge_len, edge_len, edge_len * channels)


def reference(features, occupancy, w_spatial, b_spatial, w_temporal, face_send, face_source, send_ahead, from_prior, send_back, from_later):
    frames = features.shape[0]
    all_bricks = features.shape[1]
    edge_len = features.shape[2]
    channels = w_spatial.shape[-1]
    peers = N_SPACE
    per_dev = all_bricks // peers
    slab_count = face_send.shape[1] // (2 * peers)

    def pick_rows(table, names):
        return jnp.where((names >= 0)[:, None, None], table[jnp.clip(names, 0)], 0)

    def pick_rims(table, names):
        return jnp.where((names >= 0)[:, :, None, None], table[jnp.clip(names, 0)], 0)

    def spatial(packed):
        frame_feats, frame_occ, send_plan, slot_names = packed
        keep_mask = voxel_mask(frame_occ, edge_len, channels)
        inputs = (frame_feats.astype(jnp.float32) * keep_mask).astype(jnp.bfloat16)
        hidden = inputs
        plan_rows = send_plan.reshape(peers, 2 * slab_count)
        local_src = slot_names.reshape(peers, per_dev, 6)
        for layer_index in range(LAYERS):
            face_dev = face_layers(hidden, edge_len, channels).reshape(peers, per_dev * 6, edge_len, edge_len * channels)
            outbound = jax.vmap(pick_rows)(face_dev, plan_rows)
            empty = jnp.zeros_like(outbound[:1, :slab_count])
            from_lower = jnp.concatenate([empty, outbound[:-1, slab_count:]], axis=0)
            from_upper = jnp.concatenate([outbound[1:, :slab_count], empty], axis=0)
            table = jnp.concatenate([from_lower, from_upper, face_dev], axis=1)
            rim_faces = jax.vmap(pick_rims)(table, local_src).reshape(all_bricks, 6, edge_len, edge_len * channels)
            padded = padded_block(hidden, rim_faces, edge_len, channels)
            hidden = conv_exact(padded, w_spatial[layer_index], b_spatial[layer_index], keep_mask, edge_len, channels, 16)
        return inputs, hidden

    inputs_all, hidden_all = lax.map(spatial, (features, occupancy, face_send, face_source))
    device_base = (jnp.arange(peers, dtype=jnp.int32) * per_dev)[:, None]

    def temporal(frame_id):
        hidden = hidden_all[frame_id]
        before_id = jnp.maximum(frame_id - 1, 0)
        after_id = jnp.minimum(frame_id + 1, frames - 1)
        ahead_rows = device_base + send_ahead[before_id].reshape(peers, MATCH)
        prior_slots = from_prior[frame_id].reshape(peers, per_dev)
        chosen = jnp.take_along_axis(ahead_rows, jnp.clip(prior_slots, 0), axis=1).reshape(all_bricks)
        usable = (prior_slots.reshape(all_bricks) >= 0) & (frame_id > 0)
        from_before = jnp.where(usable[:, None, None, None], hidden_all[before_id][chosen], 0)
        back_rows = device_base + send_back[after_id].reshape(peers, MATCH)
        later_slots = from_later[frame_id].reshape(peers, per_dev)
        chosen_after = jnp.take_along_axis(back_rows, jnp.clip(later_slots, 0), axis=1).reshape(all_bricks)
        usable_after = (later_slots.reshape(all_bricks) >= 0) & (frame_id < frames - 1)
        from_after = jnp.where(usable_after[:, None, None, None], hidden_all[after_id][chosen_after], 0)
        temporal_sum = jnp.dot(from_before.reshape(-1, channels), w_temporal[0], preferred_element_type=jnp.float32)
        temporal_sum = temporal_sum + jnp.dot(hidden.reshape(-1, channels), w_temporal[1], preferred_element_type=jnp.float32)
        temporal_sum = temporal_sum + jnp.dot(from_after.reshape(-1, channels), w_temporal[2], preferred_element_type=jnp.float32)
        keep_mask = voxel_mask(occupancy[frame_id], edge_len, channels)
        total_sum = inputs_all[frame_id].astype(jnp.float32) + temporal_sum.reshape(all_bricks, edge_len, edge_len, edge_len * channels)
        return (keep_mask * total_sum).astype(jnp.bfloat16)

    return lax.map(temporal, jnp.arange(frames, dtype=jnp.int32))
```

```python
import functools

import jax
import jax.numpy as jnp
from jax import lax
from jax.experimental import pallas as pl
from jax.experimental.pallas import tpu as pltpu
from jax.sharding import PartitionSpec as P

F32 = jnp.float32
BF16 = jnp.bfloat16
LANES = 128
AXES = ("space", "frame")


def swap_pairs(peers, frames):
    def at(s, t):
        return s * frames + t

    def second(i, n):
        return ((i + 1) ^ 1) - 1 if 0 < i < n - 1 else -1

    space_first, space_second, frame_first, frame_second = [], [], [], []
    for s in range(peers):
        for t in range(frames):
            space_first.append((at(s, t), at(s ^ 1, t)))
            other = second(s, peers)
            space_second.append((at(s, t), at(other, t) if other >= 0 else at(s, t ^ 1)))
            frame_first.append((at(s, t), at(s, t ^ 1)))
            other = second(t, frames)
            frame_second.append((at(s, t), at(s, other) if other >= 0 else at(s ^ 1, t)))
    return space_first, space_second, frame_first, frame_second


def iota(shape, dim):
    return lax.broadcasted_iota(jnp.int32, shape, dim)


def half(tile):
    return pltpu.roll(tile, LANES // 2, 1)


class Tables:
    def __init__(self, send_ref, source_ref, bricks, slabs):
        self.send_ref, self.source_ref = send_ref, source_ref
        self.bricks, self.slabs = bricks, slabs

    def sent(self, side, k):
        entry = self.send_ref[0, side * self.slabs + k]
        return jnp.where(entry < 0, self.bricks, entry // 6)

    def raw(self, brick, face):
        inside = jnp.minimum(brick, self.bricks - 1)
        return jnp.where(brick < self.bricks, self.source_ref[0, inside, face], -1)

    def local(self, brick, face):
        entry = self.raw(brick, face)
        base = 2 * self.slabs
        return jnp.where(entry >= base, (entry - base) // 6, self.bricks)

    def remote(self, brick, face):
        entry = self.raw(brick, face)
        low = face * self.slabs
        return (entry >= low) & (entry < low + self.slabs)

    def rim(self, brick, face):
        entry = self.raw(brick, face)
        low = face * self.slabs
        has = self.send_ref[0, face * self.slabs] >= 0
        arrived = jnp.where(has, self.bricks + 1 + entry - low, self.bricks)
        return jnp.where(self.remote(brick, face), arrived, self.local(brick, face))


def pack_kernel(send_ref, source_ref, feat_ref, occ_ref, rt_ref, mask_ref, pa_ref, pb_ref):
    _, bricks, edge, _, wide = feat_ref.shape
    channels = wide // edge
    slabs = send_ref.shape[1] // 2
    per_tile = LANES // (edge * edge)
    rows8, lanes8 = iota((8, LANES), 0), iota((8, LANES), 1)
    low = lanes8 < channels
    occ = occ_ref[0].astype(F32)
    picked = []
    for z in range(edge):
        keep = (lanes8 // edge) == (z % per_tile) * edge + rows8
        first = (z // per_tile) * LANES
        for b in range(bricks):
            row = jnp.broadcast_to(occ[b : b + 1, first : first + LANES], (8, LANES))
            picked.append(jnp.where(keep, row, 0.0))
    spread = (iota((LANES, wide), 0) % edge == iota((LANES, wide), 1) // channels).astype(F32)
    mask = jnp.dot(
        jnp.concatenate(picked, axis=0).astype(BF16),
        spread.astype(BF16),
        preferred_element_type=F32,
    )
    mask_ref[...] = mask
    tiles = wide // LANES
    for z in range(edge):
        for b in range(bricks):
            at = (z * bricks + b) * edge
            block = feat_ref[0, b, z].astype(F32) * mask[at : at + edge]
            for k in range(tiles):
                cols = slice(k * LANES, (k + 1) * LANES)
                rt_ref[b, z, :, cols] = half(block[:, cols])
    rt_ref[bricks] = jnp.zeros_like(rt_ref[bricks])

    tables = Tables(send_ref, source_ref, bricks, slabs)
    first = slice(0, LANES)
    last = slice(wide - LANES, wide)
    zero = jnp.zeros((8, LANES), F32)

    def window(side, k):
        brick = tables.sent(side, k)
        inside = jnp.minimum(brick, bricks - 1)
        own = last if side else first
        flag = jnp.where(tables.remote(brick, side), 1.0, 0.0)
        near = tables.local(brick, side)
        y_low, y_high = tables.local(brick, 2), tables.local(brick, 3)
        z_low, z_high = tables.local(brick, 4), tables.local(brick, 5)

        def pair(tile, outer, spare):
            if side:
                return [jnp.where(low, spare, tile), jnp.where(low, tile, outer)]
            return [jnp.where(low, outer, tile), jnp.where(low, tile, spare)]

        planes = [pair(rt_ref[z_low, edge - 1, :, own], flag + zero, zero)]
        for z in range(edge):
            at = pl.multiple_of((z * bricks + inside) * edge, edge)
            keep = half(mask_ref[pl.ds(at, edge), own])
            outer = rt_ref[near, z, :, first if side else last]
            planes.append(pair(rt_ref[brick, z, :, own], outer, keep))
        planes.append(pair(rt_ref[z_high, 0, :, own], zero, zero))
        for brick_y, row in ((y_low, edge - 1), (y_high, 0)):
            gathered = zero
            for z in range(edge):
                tile = rt_ref[brick_y, z, :, own]
                if (z - row) % 8:
                    tile = pltpu.roll(tile, (z - row) % 8, 0)
                gathered = jnp.where(rows8 == z, tile, gathered)
            planes.append(pair(gathered, zero, zero))
        return [jnp.concatenate([p[c] for p in planes], axis=0) for c in range(2)]

    odd = lax.rem(lax.axis_index("space"), 2) == 1
    size = (edge + 4) * 8
    for k in range(slabs):
        down, up = window(0, k), window(1, k)
        for c in range(2):
            cols = slice(c * LANES, (c + 1) * LANES)
            at = slice(k * size, (k + 1) * size)
            pa_ref[at, cols] = jnp.where(odd, down[c], up[c]).astype(BF16)
            pb_ref[at, cols] = jnp.where(odd, up[c], down[c]).astype(BF16)


def banded(w_ref, layer, band_ref):
    blank = jnp.zeros(w_ref.shape[2:], BF16)
    depth = w_ref.shape[2]
    for tap in range(9):
        before, here, after = (w_ref[layer, 3 * tap + i] for i in range(3))
        for row, (left, right) in enumerate(
            ((before, blank), (here, before), (after, here), (blank, after))
        ):
            at = (tap * 4 + row) * depth
            band_ref[at : at + depth, :] = jnp.concatenate([left, right], axis=1)


def shifted(tile, rim, down):
    rows8 = iota(tile.shape, 0)
    if down:
        return pltpu.roll(jnp.where(rows8 == 7, rim, tile), 1, 0)
    return pltpu.roll(jnp.where(rows8 == 0, rim, tile), 7, 0)


def fill_padded(tables, rt_ref, high_ref, low_ref, pad_ref, bricks, edge):
    tiles = rt_ref.shape[-1] // LANES
    low = iota((8, LANES), 1) < LANES // 2
    zero = jnp.zeros((8, LANES), F32)

    def joined(parts, left, right):
        line = [left] + parts + [right]
        return [jnp.where(low, line[i], line[i + 1]) for i in range(tiles + 1)]

    def load(brick, z):
        return [rt_ref[brick, z, :, k * LANES : (k + 1) * LANES] for k in range(tiles)]

    index = [[tables.local(b, f) for f in range(2, 6)] for b in range(bricks)]
    outer = [(tables.rim(b, 0), tables.rim(b, 1)) for b in range(bricks)]
    for z in range(-1, edge + 1):
        for pair in range(0, bricks, 2):
            built = []
            for b in (pair, pair + 1):
                y_low, y_high, z_low, z_high = index[b]
                if z < 0 or z == edge:
                    own = load(z_low, edge - 1) if z < 0 else load(z_high, 0)
                    above = below = [zero] * tiles
                    left = right = zero
                else:
                    own, below, above = load(b, z), load(y_low, z), load(y_high, z)
                    left, right = high_ref[outer[b][0], z], low_ref[outer[b][1], z]
                built.append(
                    (
                        joined(
                            [shifted(t, r, True) for t, r in zip(own, below)],
                            shifted(left, zero, True),
                            shifted(right, zero, True),
                        ),
                        joined(own, left, right),
                        joined(
                            [shifted(t, r, False) for t, r in zip(own, above)],
                            shifted(left, zero, False),
                            shifted(right, zero, False),
                        ),
                    )
                )
            at = ((z + 1) * bricks + pair) * edge
            for dy in range(3):
                for k in range(tiles + 1):
                    block = jnp.concatenate([built[0][dy][k], built[1][dy][k]], axis=0)
                    pad_ref[dy, at : at + 2 * edge, k * LANES : (k + 1) * LANES] = block.astype(BF16)


def tap_rows(pad_ref, rows, step, first_lane):
    return jnp.concatenate(
        [
            pad_ref[dy, dz * step : dz * step + rows, first_lane : first_lane + 2 * LANES]
            for dz in range(3)
            for dy in range(3)
        ],
        axis=1,
    )


def spatial_kernel(
    send_ref,
    source_ref,
    ahead_ref,
    back_ref,
    rt_ref,
    mask_ref,
    ra_ref,
    rb_ref,
    w_ref,
    bias_ref,
    out_ref,
    fa_ref,
    fb_ref,
    rt2_ref,
    high_ref,
    low_ref,
    pad_ref,
    side_ref,
    band_ref,
):
    bricks, edge = rt_ref.shape[0] - 1, rt_ref.shape[1]
    slabs = send_ref.shape[1] // 2
    wide = rt_ref.shape[-1]
    tiles = wide // LANES
    rows = bricks * edge * edge
    tables = Tables(send_ref, source_ref, bricks, slabs)
    low = iota((8, LANES), 1) < LANES // 2
    zero = jnp.zeros((8, LANES), F32)
    odd = lax.rem(lax.axis_index("space"), 2) == 1
    size = (edge + 4) * 8

    arrived_a, arrived_b = ra_ref[...].astype(F32), rb_ref[...].astype(F32)
    from_below = jnp.where(odd, arrived_a, arrived_b)
    from_above = jnp.where(odd, arrived_b, arrived_a)

    def x_faces(field_ref):
        for b in range(bricks + 1):
            for z in range(edge):
                high_ref[b, z] = field_ref[b, z, :, wide - LANES : wide]
                low_ref[b, z] = field_ref[b, z, :, 0:LANES]

    x_faces(rt_ref)
    for k in range(slabs):
        for z in range(edge):
            at = k * size + (z + 1) * 8
            high_ref[bricks + 1 + k, z] = from_below[at : at + 8, LANES : 2 * LANES]
            low_ref[bricks + 1 + k, z] = from_above[at : at + 8, 0:LANES]
    fill_padded(tables, rt_ref, high_ref, low_ref, pad_ref, bricks, edge)

    for k in range(slabs):
        base = k * size

        def plane(source, index):
            at = base + index * 8
            return [source[at : at + 8, c * LANES : (c + 1) * LANES] for c in range(2)]

        below, above = [plane(from_below, i) for i in range(edge + 4)], [
            plane(from_above, i) for i in range(edge + 4)
        ]
        flag_below, flag_above = below[0][1], above[0][0]
        below[0][1] = jnp.where(low, below[0][1], zero)
        above[0][0] = jnp.where(low, zero, above[0][0])
        own_low, own_high = tables.sent(0, k), tables.sent(1, k)
        for z in range(edge):
            mine = low_ref[own_low, z] * flag_below
            below[z + 1][1] = below[z + 1][1] + jnp.where(low, zero, mine)
            mine = high_ref[own_high, z] * flag_above
            above[z + 1][0] = above[z + 1][0] + jnp.where(low, mine, zero)
        for c in range(2):
            for i in range(edge + 2):
                inner = 0 < i <= edge
                per_side = []
                for planes in (below, above):
                    tile = planes[i][c]
                    if inner:
                        first = jnp.broadcast_to(planes[edge + 2][c][i - 1 : i], (8, LANES))
                        after = jnp.broadcast_to(planes[edge + 3][c][i - 1 : i], (8, LANES))
                    else:
                        first = after = zero
                    per_side.append((shifted(tile, first, True), tile, shifted(tile, after, False)))
                at = (i * slabs + k) * 16
                for dy in range(3):
                    block = jnp.concatenate([per_side[0][dy], per_side[1][dy]], axis=0)
                    side_ref[dy, at : at + 16, c * LANES : (c + 1) * LANES] = block.astype(BF16)

    def bias_of(layer):
        row = bias_ref[layer : layer + 1, :]
        return jnp.concatenate([row, row], axis=1)

    banded(w_ref, 0, band_ref)
    bias = bias_of(0)
    step = bricks * edge
    for i in range(tiles):
        total = jnp.dot(
            tap_rows(pad_ref, rows, step, i * LANES), band_ref[...], preferred_element_type=F32
        )
        cols = slice(i * LANES, (i + 1) * LANES)
        value = half(jnp.maximum(total + bias, 0.0) * mask_ref[:, cols])
        for z in range(edge):
            for b in range(bricks):
                at = (z * bricks + b) * edge
                rt2_ref[b, z, :, cols] = value[at : at + edge]
    rt2_ref[bricks] = jnp.zeros_like(rt2_ref[bricks])
    step = 16 * slabs
    total = jnp.dot(
        tap_rows(side_ref, edge * step, step, 0), band_ref[...], preferred_element_type=F32
    )
    value = half(jnp.maximum(total + bias, 0.0))
    x_faces(rt2_ref)
    for k in range(slabs):
        for z in range(edge):
            at = (z * slabs + k) * 16
            from_row = k * size + (z + 1) * 8
            high_ref[bricks + 1 + k, z] = value[at : at + 8] * from_below[from_row : from_row + 8, 0:LANES]
            low_ref[bricks + 1 + k, z] = (
                value[at + 8 : at + 16] * from_above[from_row : from_row + 8, LANES : 2 * LANES]
            )
    fill_padded(tables, rt2_ref, high_ref, low_ref, pad_ref, bricks, edge)

    banded(w_ref, 1, band_ref)
    bias = bias_of(1)
    step = bricks * edge
    for i in range(tiles):
        total = jnp.dot(
            tap_rows(pad_ref, rows, step, i * LANES), band_ref[...], preferred_element_type=F32
        )
        cols = slice(i * LANES, (i + 1) * LANES)
        value = (jnp.maximum(total + bias, 0.0) * mask_ref[:, cols]).astype(BF16)
        for z in range(edge):
            for b in range(bricks):
                at = (z * bricks + b) * edge
                out_ref[b, z, :, cols] = value[at : at + edge]

    odd_frame = lax.rem(lax.axis_index("frame"), 2) == 1
    for slot in range(ahead_ref.shape[1]):
        ahead, back = ahead_ref[0, slot], back_ref[0, slot]
        fa_ref[slot] = out_ref[jnp.where(odd_frame, back, ahead)]
        fb_ref[slot] = out_ref[jnp.where(odd_frame, ahead, back)]


def temporal_kernel(
    prior_ref, later_ref, feat_ref, mask_ref, hid_ref, ga_ref, gb_ref, w_ref, out_ref
):
    _, bricks, edge, _, wide = feat_ref.shape
    depth = w_ref.shape[1]
    blank = jnp.zeros((depth, depth), BF16)
    bands = []
    for i in range(3):
        w = w_ref[i]
        bands.append(jnp.concatenate([w, blank], axis=1))
        bands.append(jnp.concatenate([blank, w], axis=1))
    band = jnp.concatenate(bands, axis=0)
    odd_frame = lax.rem(lax.axis_index("frame"), 2) == 1
    slots = ga_ref.shape[0]
    for b in range(bricks):
        prior, later = prior_ref[0, b], later_ref[0, b]
        at_prior, at_later = jnp.clip(prior, 0, slots - 1), jnp.clip(later, 0, slots - 1)

        def flat(block):
            return block.astype(F32).reshape(edge * edge, wide)

        before = flat(jnp.where(odd_frame, ga_ref[at_prior], gb_ref[at_prior]))
        after = flat(jnp.where(odd_frame, gb_ref[at_later], ga_ref[at_later]))
        before = jnp.where(prior >= 0, before, 0.0).astype(BF16)
        after = jnp.where(later >= 0, after, 0.0).astype(BF16)
        here = flat(hid_ref[b]).astype(BF16)
        for k in range(wide // LANES):
            cols = slice(k * LANES, (k + 1) * LANES)
            total = jnp.dot(
                jnp.concatenate([before[:, cols], here[:, cols], after[:, cols]], axis=1),
                band,
                preferred_element_type=F32,
            )
            for z in range(edge):
                at = (z * bricks + b) * edge
                keep = mask_ref[at : at + edge, cols]
                x = feat_ref[0, b, z, :, cols].astype(F32) * keep
                out_ref[0, b, z, :, cols] = (
                    keep * (x + total[z * edge : (z + 1) * edge])
                ).astype(BF16)


VMEM = pl.BlockSpec(memory_space=pltpu.VMEM)
SMEM = pl.BlockSpec(memory_space=pltpu.SMEM)


def cost(flops, moved):
    return pl.CostEstimate(flops=flops, bytes_accessed=moved, transcendentals=0)


def per_device(
    swaps,
    features,
    occupancy,
    w_spatial,
    b_spatial,
    w_temporal,
    face_send,
    face_source,
    send_ahead,
    from_prior,
    send_back,
    from_later,
):
    _, bricks, edge, _, wide = features.shape
    slabs = face_send.shape[1] // 2
    slots = send_ahead.shape[1]
    rows = bricks * edge * edge
    space_first, space_second, frame_first, frame_second = swaps
    parcel = jax.ShapeDtypeStruct((slabs * (edge + 4) * 8, 2 * LANES), BF16)
    rolled, mask, parcel_a, parcel_b = pl.pallas_call(
        pack_kernel,
        name="pack",
        out_shape=(
            jax.ShapeDtypeStruct((bricks + 1, edge, edge, wide), F32),
            jax.ShapeDtypeStruct((rows, wide), F32),
            parcel,
            parcel,
        ),
        in_specs=[SMEM, SMEM, VMEM, VMEM],
        out_specs=(VMEM, VMEM, VMEM, VMEM),
        compiler_params=pltpu.CompilerParams(vmem_limit_bytes=8 << 20),
        cost_estimate=cost(10**8, 10**6),
    )(face_send, face_source, features, occupancy)
    arrived_a = lax.ppermute(parcel_a, AXES, space_first)
    arrived_b = lax.ppermute(parcel_b, AXES, space_second)
    sent_block = jax.ShapeDtypeStruct((slots, edge, edge, wide), BF16)
    hidden, parcel_a, parcel_b = pl.pallas_call(
        spatial_kernel,
        name="spatial",
        out_shape=(
            jax.ShapeDtypeStruct((bricks, edge, edge, wide), BF16),
            sent_block,
            sent_block,
        ),
        in_specs=[SMEM] * 4 + [VMEM] * 6,
        out_specs=(VMEM, VMEM, VMEM),
        scratch_shapes=[
            pltpu.VMEM((bricks + 1, edge, edge, wide), F32),
            pltpu.VMEM((bricks + 1 + slabs, edge, edge, LANES), F32),
            pltpu.VMEM((bricks + 1 + slabs, edge, edge, LANES), F32),
            pltpu.VMEM((3, (edge + 2) * bricks * edge, wide + LANES), BF16),
            pltpu.VMEM((3, (edge + 2) * 16 * slabs, 2 * LANES), BF16),
            pltpu.VMEM((36 * w_spatial.shape[2], LANES), BF16),
        ],
        compiler_params=pltpu.CompilerParams(vmem_limit_bytes=24 << 20),
        cost_estimate=cost(10**9, 4 * 10**6),
    )(
        face_send,
        face_source,
        send_ahead,
        send_back,
        rolled,
        mask,
        arrived_a,
        arrived_b,
        w_spatial,
        b_spatial,
    )
    arrived_a = lax.ppermute(parcel_a, AXES, frame_first)
    arrived_b = lax.ppermute(parcel_b, AXES, frame_second)
    return pl.pallas_call(
        temporal_kernel,
        name="temporal",
        out_shape=jax.ShapeDtypeStruct(features.shape, BF16),
        in_specs=[SMEM] * 2 + [VMEM] * 6,
        out_specs=VMEM,
        compiler_params=pltpu.CompilerParams(vmem_limit_bytes=8 << 20),
        cost_estimate=cost(10**8, 2 * 10**6),
    )(from_prior, from_later, features, mask, hidden, arrived_a, arrived_b, w_temporal)


def solution(mesh):
    swaps = swap_pairs(mesh.shape["space"], mesh.shape["frame"])
    in_specs = (
        P("frame", "space", None, None, None),
        P("frame", "space", None),
        P(),
        P(),
        P(),
        P("frame", "space"),
        P("frame", "space", None),
        P("frame", "space"),
        P("frame", "space"),
        P("frame", "space"),
        P("frame", "space"),
    )
    out_specs = P("frame", "space", None, None, None)
    return jax.shard_map(
        functools.partial(per_device, swaps),
        mesh=mesh,
        in_specs=in_specs,
        out_specs=out_specs,
        check_vma=False,
    )
```

```python
import functools

import jax
import jax.numpy as jnp
from jax import lax
from jax.experimental import pallas as pl
from jax.experimental.pallas import tpu as pltpu
from jax.sharding import PartitionSpec as P

F32 = jnp.float32
BF16 = jnp.bfloat16
LANES = 128
AXES = ("space", "frame")


def swap_pairs(peers, frames):
    def at(s, t):
        return s * frames + t

    def second(i, n):
        return ((i + 1) ^ 1) - 1 if 0 < i < n - 1 else -1

    space_first, space_second, frame_first, frame_second = [], [], [], []
    for s in range(peers):
        for t in range(frames):
            space_first.append((at(s, t), at(s ^ 1, t)))
            other = second(s, peers)
            space_second.append((at(s, t), at(other, t) if other >= 0 else at(s, t ^ 1)))
            frame_first.append((at(s, t), at(s, t ^ 1)))
            other = second(t, frames)
            frame_second.append((at(s, t), at(s, other) if other >= 0 else at(s ^ 1, t)))
    return space_first, space_second, frame_first, frame_second


def iota(shape, dim):
    return lax.broadcasted_iota(jnp.int32, shape, dim)


def low_half():
    return iota((8, LANES), 1) < LANES // 2


def zero_tile():
    return jnp.zeros((8, LANES), F32)


def half(tile):
    return pltpu.roll(tile, LANES // 2, 1)


def tile_of(k):
    return slice(k * LANES, (k + 1) * LANES)


class Tables:
    def __init__(self, ref, bricks, slabs, slots):
        self.ref, self.bricks, self.slabs, self.slots = ref, bricks, slabs, slots
        self.at_send = 0
        self.at_source = 2 * slabs
        self.at_prior = self.at_source + 6 * bricks
        self.at_later = self.at_prior + bricks
        self.at_ahead = self.at_later + bricks
        self.at_back = self.at_ahead + slots

    def gather(self, send_ref, source_ref, ahead_ref, prior_ref, back_ref, later_ref):
        for i in range(2 * self.slabs):
            self.ref[0, self.at_send + i] = send_ref[0, i]
        for b in range(self.bricks):
            for f in range(6):
                self.ref[0, self.at_source + 6 * b + f] = source_ref[0, b, f]
            self.ref[0, self.at_prior + b] = prior_ref[0, b]
            self.ref[0, self.at_later + b] = later_ref[0, b]
        for i in range(self.slots):
            self.ref[0, self.at_ahead + i] = ahead_ref[0, i]
            self.ref[0, self.at_back + i] = back_ref[0, i]

    def has(self, side):
        return self.ref[0, self.at_send + side * self.slabs] >= 0

    def sent(self, side, k):
        entry = self.ref[0, self.at_send + side * self.slabs + k]
        return jnp.where(entry < 0, self.bricks, entry // 6)

    def raw(self, brick, face):
        inside = jnp.minimum(brick, self.bricks - 1)
        return jnp.where(brick < self.bricks, self.ref[0, self.at_source + 6 * inside + face], -1)

    def local(self, brick, face):
        entry = self.raw(brick, face)
        base = 2 * self.slabs
        return jnp.where(entry >= base, (entry - base) // 6, self.bricks)

    def remote(self, brick, face):
        entry = self.raw(brick, face)
        first = face * self.slabs
        return (entry >= first) & (entry < first + self.slabs)

    def rim(self, brick, face):
        arrived = self.bricks + 1 + self.raw(brick, face) - face * self.slabs
        return jnp.where(self.remote(brick, face), arrived, self.local(brick, face))

    def receiver(self, side, k):
        found = self.bricks
        for b in range(self.bricks):
            found = jnp.where(self.raw(b, side) == side * self.slabs + k, b, found)
        return found


def paired(side, tile, outer, spare):
    low = low_half()
    if side:
        return [jnp.where(low, spare, tile), jnp.where(low, tile, outer)]
    return [jnp.where(low, outer, tile), jnp.where(low, tile, spare)]


def pack_kernel(*refs):
    sources, (table_ref, rt_ref, mask_ref, pa_ref, pb_ref) = refs[:8], refs[8:13]
    held, sems = refs[13:21], refs[21]
    copies = [pltpu.make_async_copy(s, d, sems.at[i]) for i, (s, d) in enumerate(zip(sources, held))]
    for copy in copies:
        copy.start()
    occ_ref, feat_ref = held[6:]
    _, bricks, edge, _, wide = feat_ref.shape
    channels = wide // edge
    tables = Tables(table_ref, bricks, held[0].shape[1] // 2, held[2].shape[1])
    slabs = tables.slabs
    per_tile = LANES // (edge * edge)
    rows8, lanes8 = iota((8, LANES), 0), iota((8, LANES), 1)
    low = low_half()
    spread = (iota((LANES, wide), 0) % edge == iota((LANES, wide), 1) // channels).astype(F32)
    spread = spread.astype(BF16)
    for copy in copies[:-1]:
        copy.wait()
    tables.gather(*held[:6])
    occ = occ_ref[0].astype(F32)
    picked = []
    for z in range(edge):
        keep = (lanes8 // edge) == (z % per_tile) * edge + rows8
        for b in range(bricks):
            row = jnp.broadcast_to(occ[b : b + 1, tile_of(z // per_tile)], (8, LANES))
            picked.append(jnp.where(keep, row, 0.0))
    mask = jnp.dot(jnp.concatenate(picked, axis=0).astype(BF16), spread, preferred_element_type=F32)
    mask_ref[...] = mask
    tiles = wide // LANES
    copies[-1].wait()
    for z in range(edge):
        for b in range(bricks):
            at = (z * bricks + b) * edge
            block = feat_ref[0, b, z].astype(F32) * mask[at : at + edge]
            for k in range(tiles):
                rt_ref[b, z, :, tile_of(k)] = half(block[:, tile_of(k)])
    rt_ref[bricks] = jnp.zeros_like(rt_ref[bricks])

    zero = zero_tile()
    ends = (tile_of(0), tile_of(tiles - 1))

    def window(side, k):
        brick = tables.sent(side, k)
        inside = jnp.minimum(brick, bricks - 1)
        own, other = ends[side], ends[1 - side]
        flag = jnp.where(tables.remote(brick, side), 1.0, 0.0)
        near = tables.local(brick, side)
        planes = [paired(side, rt_ref[tables.local(brick, 4), edge - 1, :, own], flag + zero, zero)]
        for z in range(edge):
            at = pl.multiple_of((z * bricks + inside) * edge, edge)
            keep = half(mask_ref[pl.ds(at, edge), own])
            planes.append(paired(side, rt_ref[brick, z, :, own], rt_ref[near, z, :, other], keep))
        planes.append(paired(side, rt_ref[tables.local(brick, 5), 0, :, own], zero, zero))
        for face, row in ((2, edge - 1), (3, 0)):
            brick_y = tables.local(brick, face)
            gathered = zero
            for z in range(edge):
                tile = rt_ref[brick_y, z, :, own]
                if (z - row) % 8:
                    tile = pltpu.roll(tile, (z - row) % 8, 0)
                gathered = jnp.where(rows8 == z, tile, gathered)
            planes.append(paired(side, gathered, zero, zero))
        return [jnp.concatenate([p[c] for p in planes], axis=0) for c in range(2)]

    odd = lax.rem(lax.axis_index("space"), 2) == 1
    size = (edge + 4) * 8
    for k in range(slabs):
        down, up = window(0, k), window(1, k)
        for c in range(2):
            at = slice(k * size, (k + 1) * size)
            pa_ref[at, tile_of(c)] = jnp.where(odd, down[c], up[c]).astype(BF16)
            pb_ref[at, tile_of(c)] = jnp.where(odd, up[c], down[c]).astype(BF16)


def fill_band(w_ref, layer, band_ref):
    blank = jnp.zeros(w_ref.shape[2:], BF16)
    depth = w_ref.shape[2]
    for dy in range(3):
        for dz in range(3):
            tap = 3 * dz + dy
            before, here, after = (w_ref[layer, 3 * tap + i] for i in range(3))
            for row, (left, right) in enumerate(
                ((before, blank), (here, before), (after, here), (blank, after))
            ):
                block = jnp.concatenate([left, right], axis=1)
                for out in range(2):
                    at = (((dz + out) * 3 + dy) * 4 + row) * depth
                    band_ref[at : at + depth, tile_of(out)] = block
        for out, dz in ((0, 3), (1, 0)):
            at = (dz * 3 + dy) * 4 * depth
            band_ref[at : at + 4 * depth, tile_of(out)] = jnp.zeros((4 * depth, LANES), BF16)


def shifted(tile, rim, down):
    if tile is None and rim is None:
        return None
    zero = zero_tile()
    tile = zero if tile is None else tile
    rim = zero if rim is None else rim
    rows8 = iota(tile.shape, 0)
    if down:
        return pltpu.roll(jnp.where(rows8 == 7, rim, tile), 1, 0)
    return pltpu.roll(jnp.where(rows8 == 0, rim, tile), 7, 0)


def three_shifts(line, before, after):
    return (
        [shifted(t, r, True) for t, r in zip(line, before)],
        line,
        [shifted(t, r, False) for t, r in zip(line, after)],
    )


def merged(line, pairs):
    low, zero = low_half(), zero_tile()
    full = [zero if t is None else t for t in line]
    return [jnp.where(low, full[i], full[j]) for i, j in pairs]


def fill_padded(pad_ref, tables, edge, own, rim, pairs):
    bricks = tables.bricks
    index = [[tables.local(b, f) for f in range(2, 6)] for b in range(bricks)]
    for z in range(-1, edge + 1):
        for first in range(0, bricks, 2):
            built = []
            for b in (first, first + 1):
                y_low, y_high, z_low, z_high = index[b]
                if 0 <= z < edge:
                    line, before, after = own(b, z), rim(y_low, z), rim(y_high, z)
                else:
                    line = rim(z_low, edge - 1) if z < 0 else rim(z_high, 0)
                    before = after = [None] * len(line)
                built.append([merged(s, pairs) for s in three_shifts(line, before, after)])
            at = ((z + 1) * bricks + first) * edge
            for dy in range(3):
                for k in range(len(pairs)):
                    block = jnp.concatenate([built[0][dy][k], built[1][dy][k]], axis=0)
                    pad_ref[dy, at : at + 2 * edge, tile_of(k)] = block.astype(BF16)


def convolve(windows, rows, edge, band_ref):
    blocks = []
    for window in windows:
        parts = []
        for dz in range(4):
            for dy in range(3):
                parts.append(
                    jnp.concatenate(
                        [window(dy, (2 * zz + dz) * rows, rows) for zz in range(edge // 2)], axis=0
                    )
                )
        blocks.append(jnp.concatenate(parts, axis=1))
    total = jnp.dot(jnp.concatenate(blocks, axis=0), band_ref[...], preferred_element_type=F32)

    def result(window, z):
        at = (window * (edge // 2) + z // 2) * rows
        return total[at : at + rows, tile_of(z % 2)]

    return result


def inner_kernel(
    slabs,
    table_ref,
    rt_ref,
    mask_ref,
    w_hbm,
    bias_hbm,
    rt2_ref,
    pad2_ref,
    band1_ref,
    band2_ref,
    bias2_ref,
    mid_ref,
    fa_ref,
    fb_ref,
    w_ref,
    bias_ref,
    pad_ref,
    sems,
):
    copies = [
        pltpu.make_async_copy(w_hbm, w_ref, sems.at[0]),
        pltpu.make_async_copy(bias_hbm, bias_ref, sems.at[1]),
    ]
    for copy in copies:
        copy.start()
    bricks, edge, _, wide = rt_ref.shape
    bricks -= 1
    tiles = wide // LANES
    slots = fa_ref.shape[0]
    tables = Tables(table_ref, bricks, slabs, slots)
    rows = bricks * edge

    def load(field_ref, brick, z):
        return [field_ref[brick, z, :, tile_of(k)] for k in range(tiles)]

    near = [(tables.local(b, 0), tables.local(b, 1)) for b in range(bricks)]

    def own(b, z):
        left = rt_ref[near[b][0], z, :, tile_of(tiles - 1)]
        right = rt_ref[near[b][1], z, :, tile_of(0)]
        return [left] + load(rt_ref, b, z) + [right]

    def rim(brick, z):
        return [None] + load(rt_ref, brick, z) + [None]

    fill_padded(pad_ref, tables, edge, own, rim, [(k, k + 1) for k in range(tiles + 1)])
    for copy in copies:
        copy.wait()
    fill_band(w_ref, 0, band1_ref)
    for layer in range(2):
        row = bias_ref[layer : layer + 1, :]
        bias2_ref[layer : layer + 1, :] = jnp.concatenate([row, row], axis=1)

    def window_of(ref, first):
        def window(dy, at, count):
            return ref[dy, at : at + count, first * LANES : (first + 2) * LANES]

        return window

    result = convolve([window_of(pad_ref, i) for i in range(tiles)], rows, edge, band1_ref)
    bias = bias2_ref[0:1, :]
    for i in range(tiles):
        for z in range(edge):
            keep = mask_ref[z * rows : (z + 1) * rows, tile_of(i)]
            value = half(jnp.maximum(result(i, z) + bias, 0.0) * keep)
            for b in range(bricks):
                rt2_ref[b, z, :, tile_of(i)] = value[b * edge : (b + 1) * edge]
    rt2_ref[bricks] = jnp.zeros_like(rt2_ref[bricks])

    def field(b, z):
        return load(rt2_ref, b, z)

    fill_padded(pad2_ref, tables, edge, field, field, [(k, k + 1) for k in range(tiles - 1)])
    fill_band(w_ref, 1, band2_ref)
    result = convolve([window_of(pad2_ref, i) for i in range(tiles - 2)], rows, edge, band2_ref)
    bias = bias2_ref[1:2, :]
    for i in range(tiles - 2):
        for z in range(edge):
            keep = mask_ref[z * rows : (z + 1) * rows, tile_of(i + 1)]
            value = jnp.maximum(result(i, z) + bias, 0.0) * keep
            for b in range(bricks):
                mid_ref[b, z, :, tile_of(i)] = value[b * edge : (b + 1) * edge].astype(BF16)
    choose_parcels(tables, mid_ref, fa_ref, fb_ref)


def choose_parcels(tables, field_ref, fa_ref, fb_ref):
    odd = lax.rem(lax.axis_index("frame"), 2) == 1
    for slot in range(tables.slots):
        ahead = tables.ref[0, tables.at_ahead + slot]
        back = tables.ref[0, tables.at_back + slot]
        fa_ref[slot] = field_ref[jnp.where(odd, back, ahead)]
        fb_ref[slot] = field_ref[jnp.where(odd, ahead, back)]


def border_kernel(
    table_ref,
    rt_ref,
    mask_ref,
    rt2_ref,
    pad2_ref,
    band1_ref,
    band2_ref,
    bias2_ref,
    ra_ref,
    rb_ref,
    out_ref,
    fa_ref,
    fb_ref,
    edge_ref,
    side_ref,
    pad_ref,
):
    bricks, edge, _, wide = rt_ref.shape
    bricks -= 1
    tiles = wide // LANES
    size = (edge + 4) * 8
    slabs = ra_ref.shape[0] // size
    tables = Tables(table_ref, bricks, slabs, fa_ref.shape[0])
    rows = bricks * edge
    low, zero = low_half(), zero_tile()
    ends = (tile_of(0), tile_of(tiles - 1))
    odd = lax.rem(lax.axis_index("space"), 2) == 1
    arrived_a, arrived_b = ra_ref[...].astype(F32), rb_ref[...].astype(F32)
    arrived = (
        jnp.where(tables.has(0), jnp.where(odd, arrived_a, arrived_b), 0.0),
        jnp.where(tables.has(1), jnp.where(odd, arrived_b, arrived_a), 0.0),
    )

    def arrived_tile(side, k, i, c):
        at = k * size + i * 8
        return arrived[side][at : at + 8, tile_of(c)]

    def own_block(side, k):
        brick = tables.receiver(side, k)
        tile = ends[side]
        y_low, y_high = tables.local(brick, 2), tables.local(brick, 3)
        planes = [paired(side, rt_ref[tables.local(brick, 4), edge - 1, :, tile], zero, zero)]
        before, after = [[None, None]], [[None, None]]
        for z in range(edge):
            face = arrived_tile(side, k, z + 1, 1 - side)
            planes.append(paired(side, rt_ref[brick, z, :, tile], face, zero))
            before.append(paired(side, rt_ref[y_low, z, :, tile], zero, zero))
            after.append(paired(side, rt_ref[y_high, z, :, tile], zero, zero))
        planes.append(paired(side, rt_ref[tables.local(brick, 5), 0, :, tile], zero, zero))
        return planes, before + [[None, None]], after + [[None, None]]

    def far_block(side, k):
        planes = [[arrived_tile(side, k, i, c) for c in range(2)] for i in range(edge + 2)]
        c = 1 - side
        flag = planes[0][c]
        planes[0][c] = jnp.where(low, flag, zero) if c else jnp.where(low, zero, flag)
        mine = tables.sent(side, k)
        before, after = [[None, None]], [[None, None]]
        for z in range(edge):
            face = rt_ref[mine, z, :, ends[side]] * flag
            face = jnp.where(low, zero, face) if c else jnp.where(low, face, zero)
            planes[z + 1][c] = planes[z + 1][c] + face
            rims = []
            for i in (edge + 2, edge + 3):
                pair = [arrived_tile(side, k, i, d)[z : z + 1] for d in range(2)]
                rims.append([jnp.broadcast_to(r, (8, LANES)) for r in pair])
            before.append(rims[0])
            after.append(rims[1])
        return planes, before + [[None, None]], after + [[None, None]]

    blocks = []
    for k in range(slabs):
        blocks += [own_block(0, k), own_block(1, k), far_block(0, k), far_block(1, k)]
    count = len(blocks) * 8
    for i in range(edge + 2):
        for q in range(0, len(blocks), 2):
            shifts = [three_shifts(p[i], r[i], s[i]) for p, r, s in blocks[q : q + 2]]
            at = i * count + q * 8
            for dy in range(3):
                for c in range(2):
                    block = jnp.concatenate([shifts[0][dy][c], shifts[1][dy][c]], axis=0)
                    side_ref[dy, at : at + 16, tile_of(c)] = block.astype(BF16)

    for b in range(bricks + 1):
        for z in range(edge):
            for side in range(2):
                edge_ref[b, z, :, tile_of(side)] = rt2_ref[b, z, :, ends[side]]

    def side_window(dy, at, n):
        return side_ref[dy, at : at + n, :]

    result = convolve([side_window], count, edge, band1_ref)
    bias = bias2_ref[0:1, :]
    for z in range(edge):
        value = jnp.maximum(result(0, z) + bias, 0.0)
        for k in range(slabs):
            for side in range(2):
                at = (4 * k + side) * 8
                brick = tables.receiver(side, k)
                inside = jnp.minimum(brick, bricks - 1)
                from_row = pl.multiple_of((z * bricks + inside) * edge, edge)
                new = half(value[at : at + 8] * mask_ref[pl.ds(from_row, edge), ends[side]])
                old = edge_ref[brick, z, :, tile_of(side)]
                new = jnp.where(low, new, old) if side else jnp.where(low, old, new)
                edge_ref[brick, z, :, tile_of(side)] = jnp.where(brick < bricks, new, old)
                at += 16
                far = half(value[at : at + 8]) * arrived_tile(side, k, z + 1, side)
                edge_ref[bricks + 1 + k, z, :, tile_of(1 - side)] = far

    outer = [(tables.rim(b, 0), tables.rim(b, 1)) for b in range(bricks)]

    def own(b, z):
        left, right = edge_ref[outer[b][0], z, :, tile_of(1)], edge_ref[outer[b][1], z, :, tile_of(0)]
        return [left, edge_ref[b, z, :, tile_of(0)], edge_ref[b, z, :, tile_of(1)], right]

    def rim(brick, z):
        return [None, edge_ref[brick, z, :, tile_of(0)], edge_ref[brick, z, :, tile_of(1)], None]

    fill_padded(pad_ref, tables, edge, own, rim, [(0, 1), (2, 3)])

    def low_window(dy, at, n):
        return jnp.concatenate(
            [pad_ref[dy, at : at + n, tile_of(0)], pad2_ref[dy, at : at + n, tile_of(0)]], axis=1
        )

    def high_window(dy, at, n):
        return jnp.concatenate(
            [pad2_ref[dy, at : at + n, tile_of(tiles - 2)], pad_ref[dy, at : at + n, tile_of(1)]],
            axis=1,
        )

    result = convolve([low_window, high_window], rows, edge, band2_ref)
    bias = bias2_ref[1:2, :]
    for side in range(2):
        for z in range(edge):
            keep = mask_ref[z * rows : (z + 1) * rows, ends[side]]
            value = jnp.maximum(result(side, z) + bias, 0.0) * keep
            for b in range(bricks):
                out_ref[b, z, :, tile_of(side)] = value[b * edge : (b + 1) * edge].astype(BF16)
    choose_parcels(tables, out_ref, fa_ref, fb_ref)


def temporal_part(
    tables, tiles, rt_ref, mask_ref, hid_ref, ga_ref, gb_ref, band, out_hbm, held_ref, sems
):
    bricks, edge, _, part = hid_ref.shape
    odd = lax.rem(lax.axis_index("frame"), 2) == 1

    def flat(block):
        return block.astype(F32).reshape(edge * edge, part)

    copies = []
    for b in range(bricks):
        prior = tables.ref[0, tables.at_prior + b]
        later = tables.ref[0, tables.at_later + b]
        at_prior = jnp.clip(prior, 0, tables.slots - 1)
        at_later = jnp.clip(later, 0, tables.slots - 1)
        before = flat(jnp.where(odd, ga_ref[at_prior], gb_ref[at_prior]))
        after = flat(jnp.where(odd, gb_ref[at_later], ga_ref[at_later]))
        before = jnp.where(prior >= 0, before, 0.0).astype(BF16)
        after = jnp.where(later >= 0, after, 0.0).astype(BF16)
        here = flat(hid_ref[b]).astype(BF16)
        lhs = [
            jnp.concatenate([f[:, tile_of(k)] for f in (before, here, after)], axis=1)
            for k in range(len(tiles))
        ]
        total = jnp.dot(jnp.concatenate(lhs, axis=0), band, preferred_element_type=F32)
        for k, tile in enumerate(tiles):
            for z in range(edge):
                at = (z * bricks + b) * edge
                keep = mask_ref[at : at + edge, tile_of(tile)]
                row = k * edge * edge + z * edge
                sums = half(rt_ref[b, z, :, tile_of(tile)]) + total[row : row + edge]
                held_ref[b, z, :, tile_of(k)] = (keep * sums).astype(BF16)
        done = 0
        while done < len(tiles):
            run = 1
            while done + run < len(tiles) and tiles[done + run] == tiles[done] + run:
                run += 1
            first = tiles[done]
            copies.append(
                pltpu.make_async_copy(
                    held_ref.at[b, :, :, done * LANES : (done + run) * LANES],
                    out_hbm.at[0, b, :, :, first * LANES : (first + run) * LANES],
                    sems.at[len(copies)],
                )
            )
            copies[-1].start()
            done += run
    for copy in copies:
        copy.wait()


def middle_out_kernel(
    slabs,
    table_ref,
    rt_ref,
    mask_ref,
    hid_ref,
    ga_ref,
    gb_ref,
    w_hbm,
    order_ref,
    out_hbm,
    band_ref,
    w_ref,
    held_ref,
    sem,
    sems,
):
    copy = pltpu.make_async_copy(w_hbm, w_ref, sem)
    copy.start()
    copy.wait()
    depth = w_ref.shape[1]
    blank = jnp.zeros((depth, depth), BF16)
    for i in range(3):
        at = 2 * i * depth
        band_ref[at : at + depth, :] = jnp.concatenate([w_ref[i], blank], axis=1)
        band_ref[at + depth : at + 2 * depth, :] = jnp.concatenate([blank, w_ref[i]], axis=1)
    tables = Tables(table_ref, rt_ref.shape[0] - 1, slabs, ga_ref.shape[0])
    tiles = rt_ref.shape[-1] // LANES
    temporal_part(
        tables,
        list(range(1, tiles - 1)),
        rt_ref,
        mask_ref,
        hid_ref,
        ga_ref,
        gb_ref,
        band_ref[...],
        out_hbm,
        held_ref,
        sems,
    )


def edge_out_kernel(
    slabs,
    table_ref,
    rt_ref,
    mask_ref,
    hid_ref,
    ga_ref,
    gb_ref,
    band_ref,
    before_hbm,
    out_hbm,
    held_ref,
    sems,
):
    tables = Tables(table_ref, rt_ref.shape[0] - 1, slabs, ga_ref.shape[0])
    tiles = rt_ref.shape[-1] // LANES
    temporal_part(
        tables,
        [0, tiles - 1],
        rt_ref,
        mask_ref,
        hid_ref,
        ga_ref,
        gb_ref,
        band_ref[...],
        out_hbm,
        held_ref,
        sems,
    )


VMEM = pl.BlockSpec(memory_space=pltpu.VMEM)
SMEM = pl.BlockSpec(memory_space=pltpu.SMEM)
HBM = pl.BlockSpec(memory_space=pltpu.HBM)


def in_hbm(*arrays):
    return [pltpu.with_memory_space_constraint(a, pltpu.HBM) for a in arrays]


def cost(flops, moved):
    return pl.CostEstimate(flops=flops, bytes_accessed=moved, transcendentals=0)


def per_device(
    swaps,
    features,
    occupancy,
    w_spatial,
    b_spatial,
    w_temporal,
    face_send,
    face_source,
    send_ahead,
    from_prior,
    send_back,
    from_later,
):
    _, bricks, edge, _, wide = features.shape
    slabs = face_send.shape[1] // 2
    slots = send_ahead.shape[1]
    rows = bricks * edge * edge
    depth = w_spatial.shape[2]
    shape = jax.ShapeDtypeStruct
    space_first, space_second, frame_first, frame_second = swaps
    parcel = shape((slabs * (edge + 4) * 8, 2 * LANES), BF16)
    field = shape((bricks + 1, edge, edge, wide), F32)
    arguments = (
        face_send,
        face_source,
        send_ahead,
        from_prior,
        send_back,
        from_later,
        occupancy,
        features,
    )
    table, rolled, mask, parcel_a, parcel_b = pl.pallas_call(
        pack_kernel,
        name="pack",
        out_shape=(shape((1, LANES), jnp.int32), field, shape((rows, wide), F32), parcel, parcel),
        in_specs=[HBM] * 8,
        out_specs=(SMEM, VMEM, VMEM, VMEM, VMEM),
        scratch_shapes=[pltpu.SMEM(a.shape, a.dtype) for a in arguments[:6]]
        + [pltpu.VMEM(a.shape, a.dtype) for a in arguments[6:]]
        + [pltpu.SemaphoreType.DMA((8,))],
        compiler_params=pltpu.CompilerParams(vmem_limit_bytes=8 << 20),
        cost_estimate=cost(10**8, 10**6),
    )(*in_hbm(*arguments))
    space_a = lax.ppermute(parcel_a, AXES, space_first)
    space_b = lax.ppermute(parcel_b, AXES, space_second)

    half_wide = wide // 2
    band = shape((48 * depth, 2 * LANES), BF16)
    pad_rows = (edge + 2) * bricks * edge
    hidden = shape((bricks, edge, edge, half_wide), BF16)
    sent = shape((slots, edge, edge, half_wide), BF16)
    rolled2, pad2, band1, band2, bias2, middle, parcel_a, parcel_b = pl.pallas_call(
        functools.partial(inner_kernel, slabs),
        name="inner",
        out_shape=(
            field,
            shape((3, pad_rows, wide - LANES), BF16),
            band,
            band,
            shape((2, LANES), F32),
            hidden,
            sent,
            sent,
        ),
        in_specs=[SMEM, VMEM, VMEM, HBM, HBM],
        out_specs=(VMEM,) * 8,
        scratch_shapes=[
            pltpu.VMEM(w_spatial.shape, BF16),
            pltpu.VMEM(b_spatial.shape, F32),
            pltpu.VMEM((3, pad_rows, wide + LANES), BF16),
            pltpu.SemaphoreType.DMA((2,)),
        ],
        compiler_params=pltpu.CompilerParams(vmem_limit_bytes=24 << 20),
        cost_estimate=cost(10**9, 4 * 10**6),
    )(table, rolled, mask, *in_hbm(w_spatial, b_spatial))
    middle_a = lax.ppermute(parcel_a, AXES, frame_first)
    middle_b = lax.ppermute(parcel_b, AXES, frame_second)

    edges, parcel_a, parcel_b = pl.pallas_call(
        border_kernel,
        name="border",
        out_shape=(hidden, sent, sent),
        in_specs=[SMEM] + [VMEM] * 9,
        out_specs=(VMEM,) * 3,
        scratch_shapes=[
            pltpu.VMEM((bricks + 1 + slabs, edge, edge, 2 * LANES), F32),
            pltpu.VMEM((3, (edge + 2) * 32 * slabs, 2 * LANES), BF16),
            pltpu.VMEM((3, pad_rows, 2 * LANES), BF16),
        ],
        compiler_params=pltpu.CompilerParams(vmem_limit_bytes=16 << 20),
        cost_estimate=cost(5 * 10**8, 2 * 10**6),
    )(table, rolled, mask, rolled2, pad2, band1, band2, bias2, space_a, space_b)
    edge_a = lax.ppermute(parcel_a, AXES, frame_first)
    edge_b = lax.ppermute(parcel_b, AXES, frame_second)

    out_shape = shape(features.shape, BF16)
    out, band = pl.pallas_call(
        functools.partial(middle_out_kernel, slabs),
        name="middle_out",
        out_shape=(out_shape, shape((6 * depth, LANES), BF16)),
        in_specs=[SMEM] + [VMEM] * 5 + [HBM, pl.BlockSpec(memory_space=pl.ANY)],
        out_specs=(HBM, VMEM),
        scratch_shapes=[
            pltpu.VMEM(w_temporal.shape, BF16),
            pltpu.VMEM(hidden.shape, BF16),
            pltpu.SemaphoreType.DMA,
            pltpu.SemaphoreType.DMA((bricks,)),
        ],
        compiler_params=pltpu.CompilerParams(vmem_limit_bytes=8 << 20),
        cost_estimate=cost(10**8, 10**6),
    )(table, rolled, mask, middle, middle_a, middle_b, *in_hbm(w_temporal), edges)
    return pl.pallas_call(
        functools.partial(edge_out_kernel, slabs),
        name="edge_out",
        out_shape=out_shape,
        in_specs=[SMEM] + [VMEM] * 6 + [HBM],
        out_specs=HBM,
        scratch_shapes=[
            pltpu.VMEM(hidden.shape, BF16),
            pltpu.SemaphoreType.DMA((2 * bricks,)),
        ],
        input_output_aliases={7: 0},
        compiler_params=pltpu.CompilerParams(vmem_limit_bytes=8 << 20),
        cost_estimate=cost(10**8, 10**6),
    )(table, rolled, mask, edges, edge_a, edge_b, band, out)


def solution(mesh):
    swaps = swap_pairs(mesh.shape["space"], mesh.shape["frame"])
    in_specs = (
        P("frame", "space", None, None, None),
        P("frame", "space", None),
        P(),
        P(),
        P(),
        P("frame", "space"),
        P("frame", "space", None),
        P("frame", "space"),
        P("frame", "space"),
        P("frame", "space"),
        P("frame", "space"),
    )
    out_specs = P("frame", "space", None, None, None)
    return jax.shard_map(
        functools.partial(per_device, swaps),
        mesh=mesh,
        in_specs=in_specs,
        out_specs=out_specs,
        check_vma=False,
    )
```

```python
import functools

import jax
import jax.numpy as jnp
from jax import lax
from jax.experimental import pallas as pl
from jax.experimental.pallas import tpu as pltpu
from jax.sharding import PartitionSpec as P

F32 = jnp.float32
BF16 = jnp.bfloat16
LANES = 128
AXES = ("space", "frame")


def swap_pairs(peers, frames):
    def at(s, t):
        return s * frames + t

    def second(i, n):
        return ((i + 1) ^ 1) - 1 if 0 < i < n - 1 else -1

    space_first, space_second, frame_first, frame_second = [], [], [], []
    for s in range(peers):
        for t in range(frames):
            space_first.append((at(s, t), at(s ^ 1, t)))
            other = second(s, peers)
            space_second.append((at(s, t), at(other, t) if other >= 0 else at(s, t ^ 1)))
            frame_first.append((at(s, t), at(s, t ^ 1)))
            other = second(t, frames)
            frame_second.append((at(s, t), at(s, other) if other >= 0 else at(s ^ 1, t)))
    return space_first, space_second, frame_first, frame_second


def iota(shape, dim):
    return lax.broadcasted_iota(jnp.int32, shape, dim)


def low_half():
    return iota((8, LANES), 1) < LANES // 2


def zero_tile():
    return jnp.zeros((8, LANES), F32)


def half(tile):
    return pltpu.roll(tile, LANES // 2, 1)


def tile_of(k):
    return slice(k * LANES, (k + 1) * LANES)


class Tables:
    def __init__(self, ref, bricks, slabs, slots):
        self.ref, self.bricks, self.slabs, self.slots = ref, bricks, slabs, slots
        self.at_send = 0
        self.at_source = 2 * slabs
        self.at_prior = self.at_source + 6 * bricks
        self.at_later = self.at_prior + bricks
        self.at_ahead = self.at_later + bricks
        self.at_back = self.at_ahead + slots

    def gather(self, send_ref, source_ref, ahead_ref, prior_ref, back_ref, later_ref):
        for i in range(2 * self.slabs):
            self.ref[0, self.at_send + i] = send_ref[0, i]
        for b in range(self.bricks):
            for f in range(6):
                self.ref[0, self.at_source + 6 * b + f] = source_ref[0, b, f]
            self.ref[0, self.at_prior + b] = prior_ref[0, b]
            self.ref[0, self.at_later + b] = later_ref[0, b]
        for i in range(self.slots):
            self.ref[0, self.at_ahead + i] = ahead_ref[0, i]
            self.ref[0, self.at_back + i] = back_ref[0, i]

    def live(self):
        return self.ref[0, self.at_ahead] >= 0

    def has(self, side):
        return self.ref[0, self.at_send + side * self.slabs] >= 0

    def sent(self, side, k):
        entry = self.ref[0, self.at_send + side * self.slabs + k]
        return jnp.where(entry < 0, self.bricks, entry // 6)

    def raw(self, brick, face):
        inside = jnp.minimum(brick, self.bricks - 1)
        return jnp.where(brick < self.bricks, self.ref[0, self.at_source + 6 * inside + face], -1)

    def local(self, brick, face):
        entry = self.raw(brick, face)
        base = 2 * self.slabs
        return jnp.where(entry >= base, (entry - base) // 6, self.bricks)

    def remote(self, brick, face):
        entry = self.raw(brick, face)
        first = face * self.slabs
        return (entry >= first) & (entry < first + self.slabs)

    def rim(self, brick, face):
        arrived = self.bricks + 1 + self.raw(brick, face) - face * self.slabs
        return jnp.where(self.remote(brick, face), arrived, self.local(brick, face))

    def receiver(self, side, k):
        found = self.bricks
        for b in range(self.bricks):
            found = jnp.where(self.raw(b, side) == side * self.slabs + k, b, found)
        return found


def paired(side, tile, outer, spare):
    low = low_half()
    if side:
        return [jnp.where(low, spare, tile), jnp.where(low, tile, outer)]
    return [jnp.where(low, outer, tile), jnp.where(low, tile, spare)]


def pack_kernel(*refs):
    sources, (table_ref, rt_ref, mask_ref, pa_ref, pb_ref) = refs[:11], refs[11:16]
    held, sems = refs[19:27] + refs[16:19], refs[27]
    copies = [pltpu.make_async_copy(s, d, sems.at[i]) for i, (s, d) in enumerate(zip(sources, held))]
    for copy in copies:
        copy.start()
    copies, late_copies, held = copies[:8], copies[8:], held[:8]
    occ_ref, feat_ref = held[6:]
    _, bricks, edge, _, wide = feat_ref.shape
    channels = wide // edge
    tables = Tables(table_ref, bricks, held[0].shape[1] // 2, held[2].shape[1])
    slabs = tables.slabs
    per_tile = LANES // (edge * edge)
    rows8, lanes8 = iota((8, LANES), 0), iota((8, LANES), 1)
    low = low_half()
    spread = (iota((LANES, wide), 0) % edge == iota((LANES, wide), 1) // channels).astype(F32)
    spread = spread.astype(BF16)
    for copy in copies[:-1]:
        copy.wait()
    tables.gather(*held[:6])
    occ = occ_ref[0].astype(F32)
    picked = []
    for z in range(edge):
        keep = (lanes8 // edge) == (z % per_tile) * edge + rows8
        for b in range(bricks):
            row = jnp.broadcast_to(occ[b : b + 1, tile_of(z // per_tile)], (8, LANES))
            picked.append(jnp.where(keep, row, 0.0))
    mask = jnp.dot(jnp.concatenate(picked, axis=0).astype(BF16), spread, preferred_element_type=F32)
    mask_ref[...] = mask
    tiles = wide // LANES
    copies[-1].wait()
    for z in range(edge):
        for b in range(bricks):
            at = (z * bricks + b) * edge
            block = feat_ref[0, b, z].astype(F32) * mask[at : at + edge]
            for k in range(tiles):
                rt_ref[b, z, :, tile_of(k)] = half(block[:, tile_of(k)])
    rt_ref[bricks] = jnp.zeros_like(rt_ref[bricks])

    zero = zero_tile()
    ends = (tile_of(0), tile_of(tiles - 1))

    def window(side, k):
        brick = tables.sent(side, k)
        inside = jnp.minimum(brick, bricks - 1)
        own, other = ends[side], ends[1 - side]
        flag = jnp.where(tables.remote(brick, side), 1.0, 0.0)
        near = tables.local(brick, side)
        planes = [paired(side, rt_ref[tables.local(brick, 4), edge - 1, :, own], flag + zero, zero)]
        for z in range(edge):
            at = pl.multiple_of((z * bricks + inside) * edge, edge)
            keep = half(mask_ref[pl.ds(at, edge), own])
            planes.append(paired(side, rt_ref[brick, z, :, own], rt_ref[near, z, :, other], keep))
        planes.append(paired(side, rt_ref[tables.local(brick, 5), 0, :, own], zero, zero))
        for face, row in ((2, edge - 1), (3, 0)):
            brick_y = tables.local(brick, face)
            gathered = zero
            for z in range(edge):
                tile = rt_ref[brick_y, z, :, own]
                if (z - row) % 8:
                    tile = pltpu.roll(tile, (z - row) % 8, 0)
                gathered = jnp.where(rows8 == z, tile, gathered)
            planes.append(paired(side, gathered, zero, zero))
        return [jnp.concatenate([p[c] for p in planes], axis=0) for c in range(2)]

    odd = lax.rem(lax.axis_index("space"), 2) == 1
    size = (edge + 4) * 8
    for k in range(slabs):
        down, up = window(0, k), window(1, k)
        for c in range(2):
            at = slice(k * size, (k + 1) * size)
            pa_ref[at, tile_of(c)] = jnp.where(odd, down[c], up[c]).astype(BF16)
            pb_ref[at, tile_of(c)] = jnp.where(odd, up[c], down[c]).astype(BF16)
    for copy in late_copies:
        copy.wait()


def fill_band(w_ref, layer, band_ref):
    blank = jnp.zeros(w_ref.shape[2:], BF16)
    depth = w_ref.shape[2]
    for dy in range(3):
        for dz in range(3):
            tap = 3 * dz + dy
            before, here, after = (w_ref[layer, 3 * tap + i] for i in range(3))
            for row, (left, right) in enumerate(
                ((before, blank), (here, before), (after, here), (blank, after))
            ):
                block = jnp.concatenate([left, right], axis=1)
                for out in range(2):
                    at = (((dz + out) * 3 + dy) * 4 + row) * depth
                    band_ref[at : at + depth, tile_of(out)] = block
        for out, dz in ((0, 3), (1, 0)):
            at = (dz * 3 + dy) * 4 * depth
            band_ref[at : at + 4 * depth, tile_of(out)] = jnp.zeros((4 * depth, LANES), BF16)


def shifted(tile, rim, down):
    if tile is None and rim is None:
        return None
    zero = zero_tile()
    tile = zero if tile is None else tile
    rim = zero if rim is None else rim
    rows8 = iota(tile.shape, 0)
    if down:
        return pltpu.roll(jnp.where(rows8 == 7, rim, tile), 1, 0)
    return pltpu.roll(jnp.where(rows8 == 0, rim, tile), 7, 0)


def three_shifts(line, before, after):
    return (
        [shifted(t, r, True) for t, r in zip(line, before)],
        line,
        [shifted(t, r, False) for t, r in zip(line, after)],
    )


def merged(line, pairs):
    low, zero = low_half(), zero_tile()
    full = [zero if t is None else t for t in line]
    return [jnp.where(low, full[i], full[j]) for i, j in pairs]


def fill_padded(pad_ref, tables, edge, own, rim, pairs):
    bricks = tables.bricks
    index = [[tables.local(b, f) for f in range(2, 6)] for b in range(bricks)]
    for z in range(-1, edge + 1):
        for first in range(0, bricks, 2):
            built = []
            for b in (first, first + 1):
                y_low, y_high, z_low, z_high = index[b]
                if 0 <= z < edge:
                    line, before, after = own(b, z), rim(y_low, z), rim(y_high, z)
                else:
                    line = rim(z_low, edge - 1) if z < 0 else rim(z_high, 0)
                    before = after = [None] * len(line)
                built.append([merged(s, pairs) for s in three_shifts(line, before, after)])
            at = ((z + 1) * bricks + first) * edge
            for dy in range(3):
                for k in range(len(pairs)):
                    block = jnp.concatenate([built[0][dy][k], built[1][dy][k]], axis=0)
                    pad_ref[dy, at : at + 2 * edge, tile_of(k)] = block.astype(BF16)


def convolve(windows, rows, edge, band_ref):
    blocks = []
    for window in windows:
        parts = []
        for dz in range(4):
            for dy in range(3):
                parts.append(
                    jnp.concatenate(
                        [window(dy, (2 * zz + dz) * rows, rows) for zz in range(edge // 2)], axis=0
                    )
                )
        blocks.append(parts)
    total = 0.0
    for first in (0, 6):
        lhs = [jnp.concatenate(parts[first : first + 6], axis=1) for parts in blocks]
        band = band_ref[first * 2 * LANES : (first + 6) * 2 * LANES, :]
        total = total + jnp.dot(jnp.concatenate(lhs, axis=0), band, preferred_element_type=F32)

    def result(window, z):
        at = (window * (edge // 2) + z // 2) * rows
        return total[at : at + rows, tile_of(z % 2)]

    return result


def inner_kernel(
    slabs,
    table_ref,
    rt_ref,
    mask_ref,
    w_ref,
    bias_ref,
    rt2_ref,
    pad2_ref,
    band1_ref,
    band2_ref,
    bias2_ref,
    mid_ref,
    fa_ref,
    fb_ref,
    pad_ref,
):
    bricks, edge, _, wide = rt_ref.shape
    bricks -= 1
    tiles = wide // LANES
    slots = fa_ref.shape[0]
    tables = Tables(table_ref, bricks, slabs, slots)
    rows = bricks * edge

    def load(field_ref, brick, z):
        return [field_ref[brick, z, :, tile_of(k)] for k in range(tiles)]

    near = [(tables.local(b, 0), tables.local(b, 1)) for b in range(bricks)]

    def own(b, z):
        left = rt_ref[near[b][0], z, :, tile_of(tiles - 1)]
        right = rt_ref[near[b][1], z, :, tile_of(0)]
        return [left] + load(rt_ref, b, z) + [right]

    def rim(brick, z):
        return [None] + load(rt_ref, brick, z) + [None]

    fill_padded(pad_ref, tables, edge, own, rim, [(k, k + 1) for k in range(tiles + 1)])
    fill_band(w_ref, 0, band1_ref)
    for layer in range(2):
        row = bias_ref[layer : layer + 1, :]
        bias2_ref[layer : layer + 1, :] = jnp.concatenate([row, row], axis=1)

    def window_of(ref, first):
        def window(dy, at, count):
            return ref[dy, at : at + count, first * LANES : (first + 2) * LANES]

        return window

    fill_band(w_ref, 1, band2_ref)
    result = convolve([window_of(pad_ref, i) for i in range(tiles)], rows, edge, band1_ref)
    bias = bias2_ref[0:1, :]
    for i in range(tiles):
        for z in range(edge):
            keep = mask_ref[z * rows : (z + 1) * rows, tile_of(i)]
            value = half(jnp.maximum(result(i, z) + bias, 0.0) * keep)
            for b in range(bricks):
                rt2_ref[b, z, :, tile_of(i)] = value[b * edge : (b + 1) * edge]
    rt2_ref[bricks] = jnp.zeros_like(rt2_ref[bricks])

    @pl.when(tables.live())
    def _():
        def field(b, z):
            return load(rt2_ref, b, z)

        fill_padded(pad2_ref, tables, edge, field, field, [(k, k + 1) for k in range(tiles - 1)])
        result = convolve([window_of(pad2_ref, i) for i in range(tiles - 2)], rows, edge, band2_ref)
        bias = bias2_ref[1:2, :]
        for i in range(tiles - 2):
            for z in range(edge):
                keep = mask_ref[z * rows : (z + 1) * rows, tile_of(i + 1)]
                value = jnp.maximum(result(i, z) + bias, 0.0) * keep
                for b in range(bricks):
                    mid_ref[b, z, :, tile_of(i)] = value[b * edge : (b + 1) * edge].astype(BF16)
        choose_parcels(tables, mid_ref, fa_ref, fb_ref)


def choose_parcels(tables, field_ref, fa_ref, fb_ref):
    odd = lax.rem(lax.axis_index("frame"), 2) == 1
    for slot in range(tables.slots):
        ahead = tables.ref[0, tables.at_ahead + slot]
        back = tables.ref[0, tables.at_back + slot]
        fa_ref[slot] = field_ref[jnp.where(odd, back, ahead)]
        fb_ref[slot] = field_ref[jnp.where(odd, ahead, back)]


def border_kernel(
    table_ref,
    rt_ref,
    mask_ref,
    rt2_ref,
    pad2_ref,
    band1_ref,
    band2_ref,
    bias2_ref,
    ra_ref,
    rb_ref,
    out_ref,
    fa_ref,
    fb_ref,
    edge_ref,
    side_ref,
    pad_ref,
):
    bricks, edge, _, wide = rt_ref.shape
    bricks -= 1
    tiles = wide // LANES
    size = (edge + 4) * 8
    slabs = ra_ref.shape[0] // size
    tables = Tables(table_ref, bricks, slabs, fa_ref.shape[0])
    rows = bricks * edge
    low, zero = low_half(), zero_tile()
    ends = (tile_of(0), tile_of(tiles - 1))
    odd = lax.rem(lax.axis_index("space"), 2) == 1
    arrived_a, arrived_b = ra_ref[...].astype(F32), rb_ref[...].astype(F32)
    arrived = (
        jnp.where(tables.has(0), jnp.where(odd, arrived_a, arrived_b), 0.0),
        jnp.where(tables.has(1), jnp.where(odd, arrived_b, arrived_a), 0.0),
    )

    def arrived_tile(side, k, i, c):
        at = k * size + i * 8
        return arrived[side][at : at + 8, tile_of(c)]

    def own_block(side, k):
        brick = tables.receiver(side, k)
        tile = ends[side]
        y_low, y_high = tables.local(brick, 2), tables.local(brick, 3)
        planes = [paired(side, rt_ref[tables.local(brick, 4), edge - 1, :, tile], zero, zero)]
        before, after = [[None, None]], [[None, None]]
        for z in range(edge):
            face = arrived_tile(side, k, z + 1, 1 - side)
            planes.append(paired(side, rt_ref[brick, z, :, tile], face, zero))
            before.append(paired(side, rt_ref[y_low, z, :, tile], zero, zero))
            after.append(paired(side, rt_ref[y_high, z, :, tile], zero, zero))
        planes.append(paired(side, rt_ref[tables.local(brick, 5), 0, :, tile], zero, zero))
        return planes, before + [[None, None]], after + [[None, None]]

    def far_block(side, k):
        planes = [[arrived_tile(side, k, i, c) for c in range(2)] for i in range(edge + 2)]
        c = 1 - side
        flag = planes[0][c]
        planes[0][c] = jnp.where(low, flag, zero) if c else jnp.where(low, zero, flag)
        mine = tables.sent(side, k)
        before, after = [[None, None]], [[None, None]]
        for z in range(edge):
            face = rt_ref[mine, z, :, ends[side]] * flag
            face = jnp.where(low, zero, face) if c else jnp.where(low, face, zero)
            planes[z + 1][c] = planes[z + 1][c] + face
            rims = []
            for i in (edge + 2, edge + 3):
                pair = [arrived_tile(side, k, i, d)[z : z + 1] for d in range(2)]
                rims.append([jnp.broadcast_to(r, (8, LANES)) for r in pair])
            before.append(rims[0])
            after.append(rims[1])
        return planes, before + [[None, None]], after + [[None, None]]

    blocks = []
    for k in range(slabs):
        blocks += [own_block(0, k), own_block(1, k), far_block(0, k), far_block(1, k)]
    count = len(blocks) * 8
    for i in range(edge + 2):
        for q in range(0, len(blocks), 2):
            shifts = [three_shifts(p[i], r[i], s[i]) for p, r, s in blocks[q : q + 2]]
            at = i * count + q * 8
            for dy in range(3):
                for c in range(2):
                    block = jnp.concatenate([shifts[0][dy][c], shifts[1][dy][c]], axis=0)
                    side_ref[dy, at : at + 16, tile_of(c)] = block.astype(BF16)

    for b in range(bricks + 1):
        for z in range(edge):
            for side in range(2):
                edge_ref[b, z, :, tile_of(side)] = rt2_ref[b, z, :, ends[side]]

    def side_window(dy, at, n):
        return side_ref[dy, at : at + n, :]

    result = convolve([side_window], count, edge, band1_ref)
    bias = bias2_ref[0:1, :]
    for z in range(edge):
        value = jnp.maximum(result(0, z) + bias, 0.0)
        for k in range(slabs):
            for side in range(2):
                at = (4 * k + side) * 8
                brick = tables.receiver(side, k)
                inside = jnp.minimum(brick, bricks - 1)
                from_row = pl.multiple_of((z * bricks + inside) * edge, edge)
                new = half(value[at : at + 8] * mask_ref[pl.ds(from_row, edge), ends[side]])
                old = edge_ref[brick, z, :, tile_of(side)]
                new = jnp.where(low, new, old) if side else jnp.where(low, old, new)
                edge_ref[brick, z, :, tile_of(side)] = jnp.where(brick < bricks, new, old)
                at += 16
                far = half(value[at : at + 8]) * arrived_tile(side, k, z + 1, side)
                edge_ref[bricks + 1 + k, z, :, tile_of(1 - side)] = far

    outer = [(tables.rim(b, 0), tables.rim(b, 1)) for b in range(bricks)]

    @pl.when(tables.live())
    def _():
        def own(b, z):
            left, right = edge_ref[outer[b][0], z, :, tile_of(1)], edge_ref[outer[b][1], z, :, tile_of(0)]
            return [left, edge_ref[b, z, :, tile_of(0)], edge_ref[b, z, :, tile_of(1)], right]

        def rim(brick, z):
            return [None, edge_ref[brick, z, :, tile_of(0)], edge_ref[brick, z, :, tile_of(1)], None]

        fill_padded(pad_ref, tables, edge, own, rim, [(0, 1), (2, 3)])

        def low_window(dy, at, n):
            return jnp.concatenate(
                [pad_ref[dy, at : at + n, tile_of(0)], pad2_ref[dy, at : at + n, tile_of(0)]], axis=1
            )

        def high_window(dy, at, n):
            return jnp.concatenate(
                [pad2_ref[dy, at : at + n, tile_of(tiles - 2)], pad_ref[dy, at : at + n, tile_of(1)]],
                axis=1,
            )

        result = convolve([low_window, high_window], rows, edge, band2_ref)
        bias = bias2_ref[1:2, :]
        for side in range(2):
            for z in range(edge):
                keep = mask_ref[z * rows : (z + 1) * rows, ends[side]]
                value = jnp.maximum(result(side, z) + bias, 0.0) * keep
                for b in range(bricks):
                    out_ref[b, z, :, tile_of(side)] = value[b * edge : (b + 1) * edge].astype(BF16)
        choose_parcels(tables, out_ref, fa_ref, fb_ref)


def temporal_part(tables, tiles, rt_ref, mask_ref, hid_ref, ga_ref, gb_ref, band, b, put):
    bricks, edge, _, part = hid_ref.shape
    odd = lax.rem(lax.axis_index("frame"), 2) == 1

    def flat(block):
        return block.astype(F32).reshape(edge * edge, part)

    prior = tables.ref[0, tables.at_prior + b]
    later = tables.ref[0, tables.at_later + b]
    at_prior = jnp.clip(prior, 0, tables.slots - 1)
    at_later = jnp.clip(later, 0, tables.slots - 1)
    before = flat(jnp.where(odd, ga_ref[at_prior], gb_ref[at_prior]))
    after = flat(jnp.where(odd, gb_ref[at_later], ga_ref[at_later]))
    before = jnp.where(prior >= 0, before, 0.0).astype(BF16)
    after = jnp.where(later >= 0, after, 0.0).astype(BF16)
    here = flat(hid_ref[b]).astype(BF16)
    lhs = [
        jnp.concatenate([f[:, tile_of(k)] for f in (before, here, after)], axis=1)
        for k in range(len(tiles))
    ]
    total = jnp.dot(jnp.concatenate(lhs, axis=0), band, preferred_element_type=F32)
    for k, tile in enumerate(tiles):
        for z in range(edge):
            at = (z * bricks + b) * edge
            keep = mask_ref[at : at + edge, tile_of(tile)]
            row = k * edge * edge + z * edge
            sums = half(rt_ref[b, z, :, tile_of(tile)]) + total[row : row + edge]
            put(b, z, k, (keep * sums).astype(BF16))


def middle_out_kernel(
    slabs,
    table_ref,
    rt_ref,
    mask_ref,
    hid_ref,
    ga_ref,
    gb_ref,
    w_ref,
    order_ref,
    out_ref,
    band_ref,
):
    depth = w_ref.shape[1]
    blank = jnp.zeros((depth, depth), BF16)
    for i in range(3):
        at = 2 * i * depth
        band_ref[at : at + depth, :] = jnp.concatenate([w_ref[i], blank], axis=1)
        band_ref[at + depth : at + 2 * depth, :] = jnp.concatenate([blank, w_ref[i]], axis=1)
    tables = Tables(table_ref, rt_ref.shape[0] - 1, slabs, ga_ref.shape[0])
    tiles = rt_ref.shape[-1] // LANES

    def put(b, z, k, value):
        out_ref[b, z, :, tile_of(k)] = value

    band = band_ref[...]
    for b in range(tables.bricks):
        temporal_part(
            tables,
            list(range(1, tiles - 1)),
            rt_ref,
            mask_ref,
            hid_ref,
            ga_ref,
            gb_ref,
            band,
            b,
            put,
        )


def edge_out_kernel(
    slabs,
    table_ref,
    rt_ref,
    mask_ref,
    hid_ref,
    ga_ref,
    gb_ref,
    band_ref,
    middle_ref,
    out_hbm,
    held_ref,
    sems,
):
    tables = Tables(table_ref, rt_ref.shape[0] - 1, slabs, ga_ref.shape[0])
    tiles = rt_ref.shape[-1] // LANES
    wide = tiles * LANES
    copies = [
        pltpu.make_async_copy(
            middle_ref, out_hbm.at[0, :, :, :, LANES : wide - LANES], sems.at[2 * tables.bricks]
        )
    ]
    copies[0].start()

    def put(b, z, k, value):
        held_ref[k, b, z] = value

    band = band_ref[...]
    for b in range(tables.bricks):
        temporal_part(
            tables, [0, tiles - 1], rt_ref, mask_ref, hid_ref, ga_ref, gb_ref, band, b, put
        )
        for k, tile in enumerate((0, tiles - 1)):
            copies.append(
                pltpu.make_async_copy(
                    held_ref.at[k, b], out_hbm.at[0, b, :, :, tile_of(tile)], sems.at[2 * b + k]
                )
            )
            copies[-1].start()
    for copy in copies:
        copy.wait()


VMEM = pl.BlockSpec(memory_space=pltpu.VMEM)
SMEM = pl.BlockSpec(memory_space=pltpu.SMEM)
HBM = pl.BlockSpec(memory_space=pltpu.HBM)


def in_hbm(*arrays):
    return [pltpu.with_memory_space_constraint(a, pltpu.HBM) for a in arrays]


def cost(flops, moved):
    return pl.CostEstimate(flops=flops, bytes_accessed=moved, transcendentals=0)


def per_device(
    swaps,
    features,
    occupancy,
    w_spatial,
    b_spatial,
    w_temporal,
    face_send,
    face_source,
    send_ahead,
    from_prior,
    send_back,
    from_later,
):
    _, bricks, edge, _, wide = features.shape
    slabs = face_send.shape[1] // 2
    slots = send_ahead.shape[1]
    rows = bricks * edge * edge
    depth = w_spatial.shape[2]
    shape = jax.ShapeDtypeStruct
    space_first, space_second, frame_first, frame_second = swaps
    parcel = shape((slabs * (edge + 4) * 8, 2 * LANES), BF16)
    field = shape((bricks + 1, edge, edge, wide), F32)
    arguments = (
        face_send,
        face_source,
        send_ahead,
        from_prior,
        send_back,
        from_later,
        occupancy,
        features,
        w_spatial,
        b_spatial,
        w_temporal,
    )
    table, rolled, mask, parcel_a, parcel_b, w_held, b_held, wt_held = pl.pallas_call(
        pack_kernel,
        name="pack",
        out_shape=(shape((1, LANES), jnp.int32), field, shape((rows, wide), F32), parcel, parcel)
        + tuple(shape(a.shape, a.dtype) for a in arguments[8:]),
        in_specs=[HBM] * 11,
        out_specs=(SMEM,) + (VMEM,) * 7,
        scratch_shapes=[pltpu.SMEM(a.shape, a.dtype) for a in arguments[:6]]
        + [pltpu.VMEM(a.shape, a.dtype) for a in arguments[6:8]]
        + [pltpu.SemaphoreType.DMA((11,))],
        compiler_params=pltpu.CompilerParams(vmem_limit_bytes=8 << 20),
        cost_estimate=cost(10**8, 10**6),
    )(*in_hbm(*arguments))
    space_a = lax.ppermute(parcel_a, AXES, space_first)
    space_b = lax.ppermute(parcel_b, AXES, space_second)

    half_wide = wide // 2
    band = shape((48 * depth, 2 * LANES), BF16)
    pad_rows = (edge + 2) * bricks * edge
    hidden = shape((bricks, edge, edge, half_wide), BF16)
    sent = shape((slots, edge, edge, half_wide), BF16)
    rolled2, pad2, band1, band2, bias2, middle, parcel_a, parcel_b = pl.pallas_call(
        functools.partial(inner_kernel, slabs),
        name="inner",
        out_shape=(
            field,
            shape((3, pad_rows, wide - LANES), BF16),
            band,
            band,
            shape((2, LANES), F32),
            hidden,
            sent,
            sent,
        ),
        in_specs=[SMEM] + [VMEM] * 4,
        out_specs=(VMEM,) * 8,
        scratch_shapes=[pltpu.VMEM((3, pad_rows, wide + LANES), BF16)],
        compiler_params=pltpu.CompilerParams(vmem_limit_bytes=24 << 20),
        cost_estimate=cost(10**9, 4 * 10**6),
    )(table, rolled, mask, w_held, b_held)
    middle_a = lax.ppermute(parcel_a, AXES, frame_first)
    middle_b = lax.ppermute(parcel_b, AXES, frame_second)

    edges, parcel_a, parcel_b = pl.pallas_call(
        border_kernel,
        name="border",
        out_shape=(hidden, sent, sent),
        in_specs=[SMEM] + [VMEM] * 9,
        out_specs=(VMEM,) * 3,
        scratch_shapes=[
            pltpu.VMEM((bricks + 1 + slabs, edge, edge, 2 * LANES), F32),
            pltpu.VMEM((3, (edge + 2) * 32 * slabs, 2 * LANES), BF16),
            pltpu.VMEM((3, pad_rows, 2 * LANES), BF16),
        ],
        compiler_params=pltpu.CompilerParams(vmem_limit_bytes=16 << 20),
        cost_estimate=cost(5 * 10**8, 2 * 10**6),
    )(table, rolled, mask, rolled2, pad2, band1, band2, bias2, space_a, space_b)
    edge_a = lax.ppermute(parcel_a, AXES, frame_first)
    edge_b = lax.ppermute(parcel_b, AXES, frame_second)

    middle_out, band = pl.pallas_call(
        functools.partial(middle_out_kernel, slabs),
        name="middle_out",
        out_shape=(hidden, shape((6 * depth, LANES), BF16)),
        in_specs=[SMEM] + [VMEM] * 6 + [pl.BlockSpec(memory_space=pl.ANY)],
        out_specs=(VMEM, VMEM),
        compiler_params=pltpu.CompilerParams(vmem_limit_bytes=8 << 20),
        cost_estimate=cost(10**8, 10**6),
    )(table, rolled, mask, middle, middle_a, middle_b, wt_held, edges)
    return pl.pallas_call(
        functools.partial(edge_out_kernel, slabs),
        name="edge_out",
        out_shape=shape(features.shape, BF16),
        in_specs=[SMEM] + [VMEM] * 7,
        out_specs=HBM,
        scratch_shapes=[
            pltpu.VMEM((2, bricks, edge, edge, LANES), BF16),
            pltpu.SemaphoreType.DMA((2 * bricks + 1,)),
        ],
        compiler_params=pltpu.CompilerParams(vmem_limit_bytes=8 << 20),
        cost_estimate=cost(10**8, 10**6),
    )(table, rolled, mask, edges, edge_a, edge_b, band, middle_out)


def solution(mesh):
    swaps = swap_pairs(mesh.shape["space"], mesh.shape["frame"])
    in_specs = (
        P("frame", "space", None, None, None),
        P("frame", "space", None),
        P(),
        P(),
        P(),
        P("frame", "space"),
        P("frame", "space", None),
        P("frame", "space"),
        P("frame", "space"),
        P("frame", "space"),
        P("frame", "space"),
    )
    out_specs = P("frame", "space", None, None, None)
    return jax.shard_map(
        functools.partial(per_device, swaps),
        mesh=mesh,
        in_specs=in_specs,
        out_specs=out_specs,
        check_vma=False,
    )
```

```python
import functools

import jax
import jax.numpy as jnp
from jax import lax
from jax.experimental import pallas as pl
from jax.experimental.pallas import tpu as pltpu
from jax.sharding import PartitionSpec as P

F32 = jnp.float32
BF16 = jnp.bfloat16
LANES = 128
AXES = ("space", "frame")


def swap_pairs(peers, frames):
    def at(s, t):
        return s * frames + t

    def second(i, n):
        return ((i + 1) ^ 1) - 1 if 0 < i < n - 1 else -1

    space_first, space_second, frame_first, frame_second = [], [], [], []
    for s in range(peers):
        for t in range(frames):
            space_first.append((at(s, t), at(s ^ 1, t)))
            other = second(s, peers)
            space_second.append((at(s, t), at(other, t) if other >= 0 else at(s, t ^ 1)))
            frame_first.append((at(s, t), at(s, t ^ 1)))
            other = second(t, frames)
            frame_second.append((at(s, t), at(s, other) if other >= 0 else at(s ^ 1, t)))
    return space_first, space_second, frame_first, frame_second


def iota(shape, dim):
    return lax.broadcasted_iota(jnp.int32, shape, dim)


def low_half():
    return iota((8, LANES), 1) < LANES // 2


def zero_tile():
    return jnp.zeros((8, LANES), F32)


def half(tile):
    return pltpu.roll(tile, LANES // 2, 1)


def tile_of(k):
    return slice(k * LANES, (k + 1) * LANES)


class Tables:
    def __init__(self, refs):
        self.send_ref, source_ref, self.ahead_ref, self.prior_ref, self.back_ref, self.later_ref = refs
        self.bricks = source_ref.shape[1]
        self.slabs = self.send_ref.shape[1] // 2
        self.slots = self.ahead_ref.shape[1]
        self.source = [[source_ref[0, b, f] for f in range(6)] for b in range(self.bricks)]

    def live(self):
        return self.ahead_ref[0, 0] >= 0

    def has(self, side):
        return self.send_ref[0, side * self.slabs] >= 0

    def brick_of(self, entry):
        return (entry * 10923) >> 16

    def sent(self, side, k):
        entry = self.send_ref[0, side * self.slabs + k]
        return jnp.where(entry < 0, self.bricks, self.brick_of(entry))

    def raw(self, brick, face):
        if isinstance(brick, int):
            return self.source[brick][face]
        entry = -1
        for b in range(self.bricks):
            entry = jnp.where(brick == b, self.source[b][face], entry)
        return entry

    def local(self, brick, face):
        entry = self.raw(brick, face) - 2 * self.slabs
        return jnp.where(entry >= 0, self.brick_of(entry), self.bricks)

    def remote(self, brick, face):
        entry = self.raw(brick, face)
        first = face * self.slabs
        return (entry >= first) & (entry < first + self.slabs)

    def rim(self, brick, face):
        arrived = self.bricks + 1 + self.raw(brick, face) - face * self.slabs
        return jnp.where(self.remote(brick, face), arrived, self.local(brick, face))

    def receiver(self, side, k):
        found = self.bricks
        for b in range(self.bricks):
            found = jnp.where(self.raw(b, side) == side * self.slabs + k, b, found)
        return found


def paired(side, tile, outer, spare):
    low = low_half()
    if side:
        return [jnp.where(low, spare, tile), jnp.where(low, tile, outer)]
    return [jnp.where(low, outer, tile), jnp.where(low, tile, spare)]


def pack_kernel(*refs):
    sources, table_refs, (rt_ref, mask_ref, pa_ref, pb_ref) = refs[:11], refs[11:17], refs[17:21]
    held, sems = table_refs + refs[24:26] + refs[21:24], refs[26]
    copies = [pltpu.make_async_copy(s, d, sems.at[i]) for i, (s, d) in enumerate(zip(sources, held))]
    for copy in copies:
        copy.start()
    copies, late_copies, held = copies[:8], copies[8:], held[:8]
    occ_ref, feat_ref = held[6:]
    _, bricks, edge, _, wide = feat_ref.shape
    channels = wide // edge
    per_tile = LANES // (edge * edge)
    rows8, lanes8 = iota((8, LANES), 0), iota((8, LANES), 1)
    low = low_half()
    spread = (iota((LANES, wide), 0) % edge == iota((LANES, wide), 1) // channels).astype(F32)
    spread = spread.astype(BF16)
    for copy in copies[:-1]:
        copy.wait()
    tables = Tables(table_refs)
    slabs = tables.slabs
    occ = occ_ref[0].astype(F32)
    picked = []
    for z in range(edge):
        keep = (lanes8 // edge) == (z % per_tile) * edge + rows8
        for b in range(bricks):
            row = jnp.broadcast_to(occ[b : b + 1, tile_of(z // per_tile)], (8, LANES))
            picked.append(jnp.where(keep, row, 0.0))
    mask = jnp.dot(jnp.concatenate(picked, axis=0).astype(BF16), spread, preferred_element_type=F32)
    mask_ref[...] = mask
    tiles = wide // LANES
    copies[-1].wait()
    for z in range(edge):
        for b in range(bricks):
            at = (z * bricks + b) * edge
            block = feat_ref[0, b, z].astype(F32) * mask[at : at + edge]
            for k in range(tiles):
                rt_ref[b, z, :, tile_of(k)] = half(block[:, tile_of(k)])
    rt_ref[bricks] = jnp.zeros_like(rt_ref[bricks])

    zero = zero_tile()
    ends = (tile_of(0), tile_of(tiles - 1))

    def window(side, k):
        brick = tables.sent(side, k)
        inside = jnp.minimum(brick, bricks - 1)
        own, other = ends[side], ends[1 - side]
        flag = jnp.where(tables.remote(brick, side), 1.0, 0.0)
        near = tables.local(brick, side)
        planes = [paired(side, rt_ref[tables.local(brick, 4), edge - 1, :, own], flag + zero, zero)]
        for z in range(edge):
            at = pl.multiple_of((z * bricks + inside) * edge, edge)
            keep = half(mask_ref[pl.ds(at, edge), own])
            planes.append(paired(side, rt_ref[brick, z, :, own], rt_ref[near, z, :, other], keep))
        planes.append(paired(side, rt_ref[tables.local(brick, 5), 0, :, own], zero, zero))
        for face, row in ((2, edge - 1), (3, 0)):
            brick_y = tables.local(brick, face)
            gathered = zero
            for z in range(edge):
                tile = rt_ref[brick_y, z, :, own]
                if (z - row) % 8:
                    tile = pltpu.roll(tile, (z - row) % 8, 0)
                gathered = jnp.where(rows8 == z, tile, gathered)
            planes.append(paired(side, gathered, zero, zero))
        return [jnp.concatenate([p[c] for p in planes], axis=0) for c in range(2)]

    odd = lax.rem(lax.axis_index("space"), 2) == 1
    size = (edge + 4) * 8
    for k in range(slabs):
        down, up = window(0, k), window(1, k)
        for c in range(2):
            at = slice(k * size, (k + 1) * size)
            pa_ref[at, tile_of(c)] = jnp.where(odd, down[c], up[c]).astype(BF16)
            pb_ref[at, tile_of(c)] = jnp.where(odd, up[c], down[c]).astype(BF16)
    for copy in late_copies:
        copy.wait()


def fill_band(w_ref, layer, band_ref):
    blank = jnp.zeros(w_ref.shape[2:], BF16)
    depth = w_ref.shape[2]
    for dy in range(3):
        for dz in range(3):
            tap = 3 * dz + dy
            before, here, after = (w_ref[layer, 3 * tap + i] for i in range(3))
            for row, (left, right) in enumerate(
                ((before, blank), (here, before), (after, here), (blank, after))
            ):
                block = jnp.concatenate([left, right], axis=1)
                for out in range(2):
                    at = (((dz + out) * 3 + dy) * 4 + row) * depth
                    band_ref[at : at + depth, tile_of(out)] = block
        for out, dz in ((0, 3), (1, 0)):
            at = (dz * 3 + dy) * 4 * depth
            band_ref[at : at + 4 * depth, tile_of(out)] = jnp.zeros((4 * depth, LANES), BF16)


def shifted(tile, rim, down):
    if tile is None and rim is None:
        return None
    zero = zero_tile()
    tile = zero if tile is None else tile
    rim = zero if rim is None else rim
    rows8 = iota(tile.shape, 0)
    if down:
        return pltpu.roll(jnp.where(rows8 == 7, rim, tile), 1, 0)
    return pltpu.roll(jnp.where(rows8 == 0, rim, tile), 7, 0)


def three_shifts(line, before, after):
    return (
        [shifted(t, r, True) for t, r in zip(line, before)],
        line,
        [shifted(t, r, False) for t, r in zip(line, after)],
    )


def merged(line, pairs):
    low, zero = low_half(), zero_tile()
    full = [zero if t is None else t for t in line]
    return [jnp.where(low, full[i], full[j]) for i, j in pairs]


def fill_padded(pad_ref, tables, edge, own, rim, pairs):
    bricks = tables.bricks
    index = [[tables.local(b, f) for f in range(2, 6)] for b in range(bricks)]
    for z in range(-1, edge + 1):
        for first in range(0, bricks, 2):
            built = []
            for b in (first, first + 1):
                y_low, y_high, z_low, z_high = index[b]
                if 0 <= z < edge:
                    line, before, after = own(b, z), rim(y_low, z), rim(y_high, z)
                else:
                    line = rim(z_low, edge - 1) if z < 0 else rim(z_high, 0)
                    before = after = [None] * len(line)
                built.append([merged(s, pairs) for s in three_shifts(line, before, after)])
            at = ((z + 1) * bricks + first) * edge
            for dy in range(3):
                for k in range(len(pairs)):
                    block = jnp.concatenate([built[0][dy][k], built[1][dy][k]], axis=0)
                    pad_ref[dy, at : at + 2 * edge, tile_of(k)] = block.astype(BF16)


def convolve(windows, rows, edge, band_ref):
    blocks = []
    for window in windows:
        parts = []
        for dz in range(4):
            for dy in range(3):
                parts.append(
                    jnp.concatenate(
                        [window(dy, (2 * zz + dz) * rows, rows) for zz in range(edge // 2)], axis=0
                    )
                )
        blocks.append(parts)
    total = 0.0
    for first in (0, 6):
        lhs = [jnp.concatenate(parts[first : first + 6], axis=1) for parts in blocks]
        band = band_ref[first * 2 * LANES : (first + 6) * 2 * LANES, :]
        total = total + jnp.dot(jnp.concatenate(lhs, axis=0), band, preferred_element_type=F32)

    def result(window, z):
        at = (window * (edge // 2) + z // 2) * rows
        return total[at : at + rows, tile_of(z % 2)]

    return result


def inner_kernel(
    *refs,
):
    tables, refs = Tables(refs[:6]), refs[6:]
    inner_body(tables, *refs)


def inner_body(
    tables,
    rt_ref,
    mask_ref,
    w_ref,
    bias_ref,
    rt2_ref,
    pad2_ref,
    band1_ref,
    band2_ref,
    bias2_ref,
    mid_ref,
    fa_ref,
    fb_ref,
    pad_ref,
):
    bricks, edge, _, wide = rt_ref.shape
    bricks -= 1
    tiles = wide // LANES
    rows = bricks * edge

    def load(field_ref, brick, z):
        return [field_ref[brick, z, :, tile_of(k)] for k in range(tiles)]

    near = [(tables.local(b, 0), tables.local(b, 1)) for b in range(bricks)]

    def own(b, z):
        left = rt_ref[near[b][0], z, :, tile_of(tiles - 1)]
        right = rt_ref[near[b][1], z, :, tile_of(0)]
        return [left] + load(rt_ref, b, z) + [right]

    def rim(brick, z):
        return [None] + load(rt_ref, brick, z) + [None]

    fill_padded(pad_ref, tables, edge, own, rim, [(k, k + 1) for k in range(tiles + 1)])
    fill_band(w_ref, 0, band1_ref)
    for layer in range(2):
        row = bias_ref[layer : layer + 1, :]
        bias2_ref[layer : layer + 1, :] = jnp.concatenate([row, row], axis=1)

    def window_of(ref, first):
        def window(dy, at, count):
            return ref[dy, at : at + count, first * LANES : (first + 2) * LANES]

        return window

    fill_band(w_ref, 1, band2_ref)
    result = convolve([window_of(pad_ref, i) for i in range(tiles)], rows, edge, band1_ref)
    bias = bias2_ref[0:1, :]
    for i in range(tiles):
        for z in range(edge):
            keep = mask_ref[z * rows : (z + 1) * rows, tile_of(i)]
            value = half(jnp.maximum(result(i, z) + bias, 0.0) * keep)
            for b in range(bricks):
                rt2_ref[b, z, :, tile_of(i)] = value[b * edge : (b + 1) * edge]
    rt2_ref[bricks] = jnp.zeros_like(rt2_ref[bricks])

    @pl.when(tables.live())
    def _():
        def field(b, z):
            return load(rt2_ref, b, z)

        fill_padded(pad2_ref, tables, edge, field, field, [(k, k + 1) for k in range(tiles - 1)])
        result = convolve([window_of(pad2_ref, i) for i in range(tiles - 2)], rows, edge, band2_ref)
        bias = bias2_ref[1:2, :]
        for i in range(tiles - 2):
            for z in range(edge):
                keep = mask_ref[z * rows : (z + 1) * rows, tile_of(i + 1)]
                value = jnp.maximum(result(i, z) + bias, 0.0) * keep
                for b in range(bricks):
                    mid_ref[b, z, :, tile_of(i)] = value[b * edge : (b + 1) * edge].astype(BF16)
        choose_parcels(tables, mid_ref, fa_ref, fb_ref)


def choose_parcels(tables, field_ref, fa_ref, fb_ref):
    odd = lax.rem(lax.axis_index("frame"), 2) == 1
    for slot in range(tables.slots):
        ahead, back = tables.ahead_ref[0, slot], tables.back_ref[0, slot]
        fa_ref[slot] = field_ref[jnp.where(odd, back, ahead)]
        fb_ref[slot] = field_ref[jnp.where(odd, ahead, back)]


def border_kernel(*refs):
    tables, refs = Tables(refs[:6]), refs[6:]
    border_body(tables, *refs)


def border_body(
    tables,
    rt_ref,
    mask_ref,
    rt2_ref,
    pad2_ref,
    band1_ref,
    band2_ref,
    bias2_ref,
    ra_ref,
    rb_ref,
    out_ref,
    fa_ref,
    fb_ref,
    edge_ref,
    side_ref,
    pad_ref,
):
    bricks, edge, _, wide = rt_ref.shape
    bricks -= 1
    tiles = wide // LANES
    size = (edge + 4) * 8
    slabs = tables.slabs
    rows = bricks * edge
    low, zero = low_half(), zero_tile()
    ends = (tile_of(0), tile_of(tiles - 1))
    odd = lax.rem(lax.axis_index("space"), 2) == 1
    arrived_a, arrived_b = ra_ref[...].astype(F32), rb_ref[...].astype(F32)
    arrived = (
        jnp.where(tables.has(0), jnp.where(odd, arrived_a, arrived_b), 0.0),
        jnp.where(tables.has(1), jnp.where(odd, arrived_b, arrived_a), 0.0),
    )

    def arrived_tile(side, k, i, c):
        at = k * size + i * 8
        return arrived[side][at : at + 8, tile_of(c)]

    def own_block(side, k):
        brick = tables.receiver(side, k)
        tile = ends[side]
        y_low, y_high = tables.local(brick, 2), tables.local(brick, 3)
        planes = [paired(side, rt_ref[tables.local(brick, 4), edge - 1, :, tile], zero, zero)]
        before, after = [[None, None]], [[None, None]]
        for z in range(edge):
            face = arrived_tile(side, k, z + 1, 1 - side)
            planes.append(paired(side, rt_ref[brick, z, :, tile], face, zero))
            before.append(paired(side, rt_ref[y_low, z, :, tile], zero, zero))
            after.append(paired(side, rt_ref[y_high, z, :, tile], zero, zero))
        planes.append(paired(side, rt_ref[tables.local(brick, 5), 0, :, tile], zero, zero))
        return planes, before + [[None, None]], after + [[None, None]]

    def far_block(side, k):
        planes = [[arrived_tile(side, k, i, c) for c in range(2)] for i in range(edge + 2)]
        c = 1 - side
        flag = planes[0][c]
        planes[0][c] = jnp.where(low, flag, zero) if c else jnp.where(low, zero, flag)
        mine = tables.sent(side, k)
        before, after = [[None, None]], [[None, None]]
        for z in range(edge):
            face = rt_ref[mine, z, :, ends[side]] * flag
            face = jnp.where(low, zero, face) if c else jnp.where(low, face, zero)
            planes[z + 1][c] = planes[z + 1][c] + face
            rims = []
            for i in (edge + 2, edge + 3):
                pair = [arrived_tile(side, k, i, d)[z : z + 1] for d in range(2)]
                rims.append([jnp.broadcast_to(r, (8, LANES)) for r in pair])
            before.append(rims[0])
            after.append(rims[1])
        return planes, before + [[None, None]], after + [[None, None]]

    blocks = []
    for k in range(slabs):
        blocks += [own_block(0, k), own_block(1, k), far_block(0, k), far_block(1, k)]
    count = len(blocks) * 8
    for i in range(edge + 2):
        for q in range(0, len(blocks), 2):
            shifts = [three_shifts(p[i], r[i], s[i]) for p, r, s in blocks[q : q + 2]]
            at = i * count + q * 8
            for dy in range(3):
                for c in range(2):
                    block = jnp.concatenate([shifts[0][dy][c], shifts[1][dy][c]], axis=0)
                    side_ref[dy, at : at + 16, tile_of(c)] = block.astype(BF16)

    for b in range(bricks + 1):
        for z in range(edge):
            for side in range(2):
                edge_ref[b, z, :, tile_of(side)] = rt2_ref[b, z, :, ends[side]]

    def side_window(dy, at, n):
        return side_ref[dy, at : at + n, :]

    result = convolve([side_window], count, edge, band1_ref)
    bias = bias2_ref[0:1, :]
    for z in range(edge):
        value = jnp.maximum(result(0, z) + bias, 0.0)
        for k in range(slabs):
            for side in range(2):
                at = (4 * k + side) * 8
                brick = tables.receiver(side, k)
                inside = jnp.minimum(brick, bricks - 1)
                from_row = pl.multiple_of((z * bricks + inside) * edge, edge)
                new = half(value[at : at + 8] * mask_ref[pl.ds(from_row, edge), ends[side]])
                old = edge_ref[brick, z, :, tile_of(side)]
                new = jnp.where(low, new, old) if side else jnp.where(low, old, new)
                edge_ref[brick, z, :, tile_of(side)] = jnp.where(brick < bricks, new, old)
                at += 16
                far = half(value[at : at + 8]) * arrived_tile(side, k, z + 1, side)
                edge_ref[bricks + 1 + k, z, :, tile_of(1 - side)] = far

    outer = [(tables.rim(b, 0), tables.rim(b, 1)) for b in range(bricks)]

    @pl.when(tables.live())
    def _():
        def own(b, z):
            left, right = edge_ref[outer[b][0], z, :, tile_of(1)], edge_ref[outer[b][1], z, :, tile_of(0)]
            return [left, edge_ref[b, z, :, tile_of(0)], edge_ref[b, z, :, tile_of(1)], right]

        def rim(brick, z):
            return [None, edge_ref[brick, z, :, tile_of(0)], edge_ref[brick, z, :, tile_of(1)], None]

        fill_padded(pad_ref, tables, edge, own, rim, [(0, 1), (2, 3)])

        def low_window(dy, at, n):
            return jnp.concatenate(
                [pad_ref[dy, at : at + n, tile_of(0)], pad2_ref[dy, at : at + n, tile_of(0)]], axis=1
            )

        def high_window(dy, at, n):
            return jnp.concatenate(
                [pad2_ref[dy, at : at + n, tile_of(tiles - 2)], pad_ref[dy, at : at + n, tile_of(1)]],
                axis=1,
            )

        result = convolve([low_window, high_window], rows, edge, band2_ref)
        bias = bias2_ref[1:2, :]
        for side in range(2):
            for z in range(edge):
                keep = mask_ref[z * rows : (z + 1) * rows, ends[side]]
                value = jnp.maximum(result(side, z) + bias, 0.0) * keep
                for b in range(bricks):
                    out_ref[b, z, :, tile_of(side)] = value[b * edge : (b + 1) * edge].astype(BF16)
        choose_parcels(tables, out_ref, fa_ref, fb_ref)


def temporal_part(tables, tiles, rt_ref, mask_ref, hid_ref, ga_ref, gb_ref, band, b, put):
    bricks, edge, _, part = hid_ref.shape
    odd = lax.rem(lax.axis_index("frame"), 2) == 1

    def flat(block):
        return block.astype(F32).reshape(edge * edge, part)

    prior, later = tables.prior_ref[0, b], tables.later_ref[0, b]
    at_prior = jnp.clip(prior, 0, tables.slots - 1)
    at_later = jnp.clip(later, 0, tables.slots - 1)
    before = flat(jnp.where(odd, ga_ref[at_prior], gb_ref[at_prior]))
    after = flat(jnp.where(odd, gb_ref[at_later], ga_ref[at_later]))
    before = jnp.where(prior >= 0, before, 0.0).astype(BF16)
    after = jnp.where(later >= 0, after, 0.0).astype(BF16)
    here = flat(hid_ref[b]).astype(BF16)
    lhs = [
        jnp.concatenate([f[:, tile_of(k)] for f in (before, here, after)], axis=1)
        for k in range(len(tiles))
    ]
    total = jnp.dot(jnp.concatenate(lhs, axis=0), band, preferred_element_type=F32)
    for k, tile in enumerate(tiles):
        for z in range(edge):
            at = (z * bricks + b) * edge
            keep = mask_ref[at : at + edge, tile_of(tile)]
            row = k * edge * edge + z * edge
            sums = half(rt_ref[b, z, :, tile_of(tile)]) + total[row : row + edge]
            put(b, z, k, (keep * sums).astype(BF16))


def middle_out_kernel(*refs):
    tables, refs = Tables(refs[:6]), refs[6:]
    middle_out_body(tables, *refs)


def middle_out_body(
    tables,
    rt_ref,
    mask_ref,
    hid_ref,
    ga_ref,
    gb_ref,
    w_ref,
    order_ref,
    out_ref,
    band_ref,
):
    depth = w_ref.shape[1]
    blank = jnp.zeros((depth, depth), BF16)
    for i in range(3):
        at = 2 * i * depth
        band_ref[at : at + depth, :] = jnp.concatenate([w_ref[i], blank], axis=1)
        band_ref[at + depth : at + 2 * depth, :] = jnp.concatenate([blank, w_ref[i]], axis=1)
    tiles = rt_ref.shape[-1] // LANES

    def put(b, z, k, value):
        out_ref[b, z, :, tile_of(k)] = value

    band = band_ref[...]
    for b in range(tables.bricks):
        temporal_part(
            tables,
            list(range(1, tiles - 1)),
            rt_ref,
            mask_ref,
            hid_ref,
            ga_ref,
            gb_ref,
            band,
            b,
            put,
        )


def edge_out_kernel(*refs):
    tables, refs = Tables(refs[:6]), refs[6:]
    edge_out_body(tables, *refs)


def edge_out_body(
    tables,
    rt_ref,
    mask_ref,
    hid_ref,
    ga_ref,
    gb_ref,
    band_ref,
    middle_ref,
    out_hbm,
    held_ref,
    sems,
):
    tiles = rt_ref.shape[-1] // LANES
    wide = tiles * LANES
    copies = [
        pltpu.make_async_copy(
            middle_ref, out_hbm.at[0, :, :, :, LANES : wide - LANES], sems.at[2 * tables.bricks]
        )
    ]
    copies[0].start()

    def put(b, z, k, value):
        held_ref[k, b, z] = value

    band = band_ref[...]
    for b in range(tables.bricks):
        temporal_part(
            tables, [0, tiles - 1], rt_ref, mask_ref, hid_ref, ga_ref, gb_ref, band, b, put
        )
        for k, tile in enumerate((0, tiles - 1)):
            copies.append(
                pltpu.make_async_copy(
                    held_ref.at[k, b], out_hbm.at[0, b, :, :, tile_of(tile)], sems.at[2 * b + k]
                )
            )
            copies[-1].start()
    for copy in copies:
        copy.wait()


VMEM = pl.BlockSpec(memory_space=pltpu.VMEM)
HBM = pl.BlockSpec(memory_space=pltpu.HBM)


def in_hbm(*arrays):
    return [pltpu.with_memory_space_constraint(a, pltpu.HBM) for a in arrays]


def cost(flops, moved):
    return pl.CostEstimate(flops=flops, bytes_accessed=moved, transcendentals=0)


def per_device(
    swaps,
    features,
    occupancy,
    w_spatial,
    b_spatial,
    w_temporal,
    face_send,
    face_source,
    send_ahead,
    from_prior,
    send_back,
    from_later,
):
    _, bricks, edge, _, wide = features.shape
    slabs = face_send.shape[1] // 2
    slots = send_ahead.shape[1]
    rows = bricks * edge * edge
    depth = w_spatial.shape[2]
    shape = jax.ShapeDtypeStruct
    space_first, space_second, frame_first, frame_second = swaps
    parcel = shape((slabs * (edge + 4) * 8, 2 * LANES), BF16)
    field = shape((bricks + 1, edge, edge, wide), F32)
    arguments = (
        face_send,
        face_source,
        send_ahead,
        from_prior,
        send_back,
        from_later,
        occupancy,
        features,
        w_spatial,
        b_spatial,
        w_temporal,
    )
    *table, rolled, mask, parcel_a, parcel_b, w_held, b_held, wt_held = pl.pallas_call(
        pack_kernel,
        name="pack",
        out_shape=tuple(shape(a.shape, a.dtype) for a in arguments[:6])
        + (field, shape((rows, wide), F32), parcel, parcel)
        + tuple(shape(a.shape, a.dtype) for a in arguments[8:]),
        in_specs=[HBM] * 11,
        out_specs=(VMEM,) * 13,
        scratch_shapes=[pltpu.VMEM(a.shape, a.dtype) for a in arguments[6:8]]
        + [pltpu.SemaphoreType.DMA((11,))],
        compiler_params=pltpu.CompilerParams(vmem_limit_bytes=8 << 20),
        cost_estimate=cost(10**8, 10**6),
    )(*in_hbm(*arguments))
    space_a = lax.ppermute(parcel_a, AXES, space_first)
    space_b = lax.ppermute(parcel_b, AXES, space_second)

    half_wide = wide // 2
    band = shape((48 * depth, 2 * LANES), BF16)
    pad_rows = (edge + 2) * bricks * edge
    hidden = shape((bricks, edge, edge, half_wide), BF16)
    sent = shape((slots, edge, edge, half_wide), BF16)
    rolled2, pad2, band1, band2, bias2, middle, parcel_a, parcel_b = pl.pallas_call(
        inner_kernel,
        name="inner",
        out_shape=(
            field,
            shape((3, pad_rows, wide - LANES), BF16),
            band,
            band,
            shape((2, LANES), F32),
            hidden,
            sent,
            sent,
        ),
        in_specs=[VMEM] * 10,
        out_specs=(VMEM,) * 8,
        scratch_shapes=[pltpu.VMEM((3, pad_rows, wide + LANES), BF16)],
        compiler_params=pltpu.CompilerParams(vmem_limit_bytes=24 << 20),
        cost_estimate=cost(10**9, 4 * 10**6),
    )(*table, rolled, mask, w_held, b_held)
    middle_a = lax.ppermute(parcel_a, AXES, frame_first)
    middle_b = lax.ppermute(parcel_b, AXES, frame_second)

    edges, parcel_a, parcel_b = pl.pallas_call(
        border_kernel,
        name="border",
        out_shape=(hidden, sent, sent),
        in_specs=[VMEM] * 15,
        out_specs=(VMEM,) * 3,
        scratch_shapes=[
            pltpu.VMEM((bricks + 1 + slabs, edge, edge, 2 * LANES), F32),
            pltpu.VMEM((3, (edge + 2) * 32 * slabs, 2 * LANES), BF16),
            pltpu.VMEM((3, pad_rows, 2 * LANES), BF16),
        ],
        compiler_params=pltpu.CompilerParams(vmem_limit_bytes=16 << 20),
        cost_estimate=cost(5 * 10**8, 2 * 10**6),
    )(*table, rolled, mask, rolled2, pad2, band1, band2, bias2, space_a, space_b)
    edge_a = lax.ppermute(parcel_a, AXES, frame_first)
    edge_b = lax.ppermute(parcel_b, AXES, frame_second)

    middle_out, band = pl.pallas_call(
        middle_out_kernel,
        name="middle_out",
        out_shape=(hidden, shape((6 * depth, LANES), BF16)),
        in_specs=[VMEM] * 12 + [pl.BlockSpec(memory_space=pl.ANY)],
        out_specs=(VMEM, VMEM),
        compiler_params=pltpu.CompilerParams(vmem_limit_bytes=8 << 20),
        cost_estimate=cost(10**8, 10**6),
    )(*table, rolled, mask, middle, middle_a, middle_b, wt_held, edges)
    return pl.pallas_call(
        edge_out_kernel,
        name="edge_out",
        out_shape=shape(features.shape, BF16),
        in_specs=[VMEM] * 13,
        out_specs=HBM,
        scratch_shapes=[
            pltpu.VMEM((2, bricks, edge, edge, LANES), BF16),
            pltpu.SemaphoreType.DMA((2 * bricks + 1,)),
        ],
        compiler_params=pltpu.CompilerParams(vmem_limit_bytes=8 << 20),
        cost_estimate=cost(10**8, 10**6),
    )(*table, rolled, mask, edges, edge_a, edge_b, band, middle_out)


def solution(mesh):
    swaps = swap_pairs(mesh.shape["space"], mesh.shape["frame"])
    in_specs = (
        P("frame", "space", None, None, None),
        P("frame", "space", None),
        P(),
        P(),
        P(),
        P("frame", "space"),
        P("frame", "space", None),
        P("frame", "space"),
        P("frame", "space"),
        P("frame", "space"),
        P("frame", "space"),
    )
    out_specs = P("frame", "space", None, None, None)
    return jax.shard_map(
        functools.partial(per_device, swaps),
        mesh=mesh,
        in_specs=in_specs,
        out_specs=out_specs,
        check_vma=False,
    )
```

```python
import functools

import jax
import jax.numpy as jnp
from jax import lax
from jax.experimental import pallas as pl
from jax.experimental.pallas import tpu as pltpu
from jax.sharding import PartitionSpec as P

F32 = jnp.float32
BF16 = jnp.bfloat16
LANES = 128
AXES = ("space", "frame")


def swap_pairs(peers, frames):
    def at(s, t):
        return s * frames + t

    def second(i, n):
        return ((i + 1) ^ 1) - 1 if 0 < i < n - 1 else -1

    space_first, space_second, frame_first, frame_second = [], [], [], []
    for s in range(peers):
        for t in range(frames):
            space_first.append((at(s, t), at(s ^ 1, t)))
            other = second(s, peers)
            space_second.append((at(s, t), at(other, t) if other >= 0 else at(s, t ^ 1)))
            frame_first.append((at(s, t), at(s, t ^ 1)))
            other = second(t, frames)
            frame_second.append((at(s, t), at(s, other) if other >= 0 else at(s ^ 1, t)))
    return space_first, space_second, frame_first, frame_second


def iota(shape, dim):
    return lax.broadcasted_iota(jnp.int32, shape, dim)


def low_half():
    return iota((8, LANES), 1) < LANES // 2


def zero_tile():
    return jnp.zeros((8, LANES), F32)


def half(tile):
    return pltpu.roll(tile, LANES // 2, 1)


def tile_of(k):
    return slice(k * LANES, (k + 1) * LANES)


class Tables:
    def __init__(self, refs):
        self.send_ref, source_ref, self.ahead_ref, self.prior_ref, self.back_ref, self.later_ref = refs
        self.bricks = source_ref.shape[1]
        self.slabs = self.send_ref.shape[1] // 2
        self.slots = self.ahead_ref.shape[1]
        self.source = [[source_ref[0, b, f] for f in range(6)] for b in range(self.bricks)]

    def live(self):
        return self.ahead_ref[0, 0] >= 0

    def has(self, side):
        return self.send_ref[0, side * self.slabs] >= 0

    def brick_of(self, entry):
        return (entry * 10923) >> 16

    def sent(self, side, k):
        entry = self.send_ref[0, side * self.slabs + k]
        return jnp.where(entry < 0, self.bricks, self.brick_of(entry))

    def raw(self, brick, face):
        if isinstance(brick, int):
            return self.source[brick][face]
        entry = -1
        for b in range(self.bricks):
            entry = jnp.where(brick == b, self.source[b][face], entry)
        return entry

    def local(self, brick, face):
        entry = self.raw(brick, face) - 2 * self.slabs
        return jnp.where(entry >= 0, self.brick_of(entry), self.bricks)

    def remote(self, brick, face):
        entry = self.raw(brick, face)
        first = face * self.slabs
        return (entry >= first) & (entry < first + self.slabs)

    def rim(self, brick, face):
        arrived = self.bricks + 1 + self.raw(brick, face) - face * self.slabs
        return jnp.where(self.remote(brick, face), arrived, self.local(brick, face))

    def receiver(self, side, k):
        found = self.bricks
        for b in range(self.bricks):
            found = jnp.where(self.raw(b, side) == side * self.slabs + k, b, found)
        return found


def paired(side, tile, outer, spare):
    low = low_half()
    if side:
        return [jnp.where(low, spare, tile), jnp.where(low, tile, outer)]
    return [jnp.where(low, outer, tile), jnp.where(low, tile, spare)]


def pack_kernel(*refs):
    sources, table_refs, (rt_ref, mask_ref, pa_ref, pb_ref) = refs[:11], refs[11:17], refs[17:21]
    held, sems = table_refs + refs[24:26] + refs[21:24], refs[26]
    copies = [pltpu.make_async_copy(s, d, sems.at[i]) for i, (s, d) in enumerate(zip(sources, held))]
    for copy in copies:
        copy.start()
    copies, late_copies, held = copies[:8], copies[8:], held[:8]
    occ_ref, feat_ref = held[6:]
    _, bricks, edge, _, wide = feat_ref.shape
    channels = wide // edge
    per_tile = LANES // (edge * edge)
    rows8, lanes8 = iota((8, LANES), 0), iota((8, LANES), 1)
    low = low_half()
    spread = (iota((LANES, wide), 0) % edge == iota((LANES, wide), 1) // channels).astype(F32)
    spread = spread.astype(BF16)
    for copy in copies[:-1]:
        copy.wait()
    tables = Tables(table_refs)
    slabs = tables.slabs
    occ = occ_ref[0].astype(F32)
    picked = []
    for z in range(edge):
        keep = (lanes8 // edge) == (z % per_tile) * edge + rows8
        for b in range(bricks):
            row = jnp.broadcast_to(occ[b : b + 1, tile_of(z // per_tile)], (8, LANES))
            picked.append(jnp.where(keep, row, 0.0))
    mask = jnp.dot(jnp.concatenate(picked, axis=0).astype(BF16), spread, preferred_element_type=F32)
    mask_ref[...] = mask
    tiles = wide // LANES
    copies[-1].wait()
    for z in range(edge):
        for b in range(bricks):
            at = (z * bricks + b) * edge
            block = feat_ref[0, b, z].astype(F32) * mask[at : at + edge]
            for k in range(tiles):
                rt_ref[b, z, :, tile_of(k)] = half(block[:, tile_of(k)])
    rt_ref[bricks] = jnp.zeros_like(rt_ref[bricks])

    zero = zero_tile()
    ends = (tile_of(0), tile_of(tiles - 1))

    def window(side, k):
        brick = tables.sent(side, k)
        inside = jnp.minimum(brick, bricks - 1)
        own, other = ends[side], ends[1 - side]
        flag = jnp.where(tables.remote(brick, side), 1.0, 0.0)
        near = tables.local(brick, side)
        planes = [paired(side, rt_ref[tables.local(brick, 4), edge - 1, :, own], flag + zero, zero)]
        for z in range(edge):
            at = pl.multiple_of((z * bricks + inside) * edge, edge)
            keep = half(mask_ref[pl.ds(at, edge), own])
            planes.append(paired(side, rt_ref[brick, z, :, own], rt_ref[near, z, :, other], keep))
        planes.append(paired(side, rt_ref[tables.local(brick, 5), 0, :, own], zero, zero))
        for face, row in ((2, edge - 1), (3, 0)):
            brick_y = tables.local(brick, face)
            gathered = zero
            for z in range(edge):
                tile = rt_ref[brick_y, z, :, own]
                if (z - row) % 8:
                    tile = pltpu.roll(tile, (z - row) % 8, 0)
                gathered = jnp.where(rows8 == z, tile, gathered)
            planes.append(paired(side, gathered, zero, zero))
        return [jnp.concatenate([p[c] for p in planes], axis=0) for c in range(2)]

    odd = lax.rem(lax.axis_index("space"), 2) == 1
    size = (edge + 4) * 8
    for k in range(slabs):
        down, up = window(0, k), window(1, k)
        for c in range(2):
            at = slice(k * size, (k + 1) * size)
            pa_ref[at, tile_of(c)] = jnp.where(odd, down[c], up[c]).astype(BF16)
            pb_ref[at, tile_of(c)] = jnp.where(odd, up[c], down[c]).astype(BF16)
    for copy in late_copies:
        copy.wait()


def tap_place(dz, dy):
    return (dz // 2) * 6 + (1, 0, 2)[dy] * 2 + dz % 2


def fill_band(w_ref, layer, band_ref):
    blank = jnp.zeros(w_ref.shape[2:], BF16)
    depth = w_ref.shape[2]
    for dy in (1, 0, 2):
        for dz in range(3):
            tap = 3 * dz + dy
            before, here, after = (w_ref[layer, 3 * tap + i] for i in range(3))
            for row, (left, right) in enumerate(
                ((before, blank), (here, before), (after, here), (blank, after))
            ):
                block = jnp.concatenate([left, right], axis=1)
                for out in range(2):
                    at = (tap_place(dz + out, dy) * 4 + row) * depth
                    band_ref[at : at + depth, tile_of(out)] = block
        for out, dz in ((0, 3), (1, 0)):
            at = tap_place(dz, dy) * 4 * depth
            band_ref[at : at + 4 * depth, tile_of(out)] = jnp.zeros((4 * depth, LANES), BF16)


def shifted(tile, rim, down):
    if tile is None and rim is None:
        return None
    zero = zero_tile()
    tile = zero if tile is None else tile
    rim = zero if rim is None else rim
    rows8 = iota(tile.shape, 0)
    if down:
        return pltpu.roll(jnp.where(rows8 == 7, rim, tile), 1, 0)
    return pltpu.roll(jnp.where(rows8 == 0, rim, tile), 7, 0)


def three_shifts(line, before, after):
    return (
        [shifted(t, r, True) for t, r in zip(line, before)],
        line,
        [shifted(t, r, False) for t, r in zip(line, after)],
    )


def merged(line, pairs):
    low, zero = low_half(), zero_tile()
    full = [zero if t is None else t for t in line]
    return [jnp.where(low, full[i], full[j]) for i, j in pairs]


def fill_padded(pad_ref, tables, edge, own, rim, pairs):
    bricks = tables.bricks
    index = [[tables.local(b, f) for f in range(2, 6)] for b in range(bricks)]

    def lines(b, z):
        y_low, y_high, z_low, z_high = index[b]
        if 0 <= z < edge:
            return own(b, z), rim(y_low, z), rim(y_high, z)
        line = rim(z_low, edge - 1) if z < 0 else rim(z_high, 0)
        return line, [None] * len(line), [None] * len(line)

    def store(dy, z, first, built):
        at = ((z + 1) * bricks + first) * edge
        for k in range(len(pairs)):
            block = jnp.concatenate([built[0][k], built[1][k]], axis=0)
            pad_ref[dy, at : at + 2 * edge, tile_of(k)] = block.astype(BF16)

    places = [(z, first) for z in range(-1, edge + 1) for first in range(0, bricks, 2)]
    for z, first in places:
        store(1, z, first, [merged(lines(b, z)[0], pairs) for b in (first, first + 1)])
    for dy in (0, 2):
        for z, first in places:
            built = []
            for b in (first, first + 1):
                sides = lines(b, z)
                moved = [shifted(t, r, dy == 0) for t, r in zip(sides[0], sides[1 + dy // 2])]
                built.append(merged(moved, pairs))
            store(dy, z, first, built)


def convolve(windows, rows, edge, band_ref):
    blocks = []
    for window in windows:
        parts = []
        for first in (0, 2):
            for dy in (1, 0, 2):
                for dz in (first, first + 1):
                    starts = [(2 * zz + dz) * rows for zz in range(edge // 2)]
                    parts.append(jnp.concatenate([window(dy, at, rows) for at in starts], axis=0))
        blocks.append(parts)
    total = 0.0
    for first in (0, 6):
        lhs = [jnp.concatenate(parts[first : first + 6], axis=1) for parts in blocks]
        band = band_ref[first * 2 * LANES : (first + 6) * 2 * LANES, :]
        total = total + jnp.dot(jnp.concatenate(lhs, axis=0), band, preferred_element_type=F32)

    def result(window, z):
        at = (window * (edge // 2) + z // 2) * rows
        return total[at : at + rows, tile_of(z % 2)]

    return result


def inner_kernel(
    *refs,
):
    tables, refs = Tables(refs[:6]), refs[6:]
    inner_body(tables, *refs)


def inner_body(
    tables,
    rt_ref,
    mask_ref,
    w_ref,
    bias_ref,
    rt2_ref,
    pad2_ref,
    band1_ref,
    band2_ref,
    bias2_ref,
    mid_ref,
    fa_ref,
    fb_ref,
    pad_ref,
):
    bricks, edge, _, wide = rt_ref.shape
    bricks -= 1
    tiles = wide // LANES
    rows = bricks * edge

    def load(field_ref, brick, z):
        return [field_ref[brick, z, :, tile_of(k)] for k in range(tiles)]

    near = [(tables.local(b, 0), tables.local(b, 1)) for b in range(bricks)]

    def own(b, z):
        left = rt_ref[near[b][0], z, :, tile_of(tiles - 1)]
        right = rt_ref[near[b][1], z, :, tile_of(0)]
        return [left] + load(rt_ref, b, z) + [right]

    def rim(brick, z):
        return [None] + load(rt_ref, brick, z) + [None]

    fill_padded(pad_ref, tables, edge, own, rim, [(k, k + 1) for k in range(tiles + 1)])
    fill_band(w_ref, 0, band1_ref)
    for layer in range(2):
        row = bias_ref[layer : layer + 1, :]
        bias2_ref[layer : layer + 1, :] = jnp.concatenate([row, row], axis=1)

    def window_of(ref, first):
        def window(dy, at, count):
            return ref[dy, at : at + count, first * LANES : (first + 2) * LANES]

        return window

    fill_band(w_ref, 1, band2_ref)
    result = convolve([window_of(pad_ref, i) for i in range(tiles)], rows, edge, band1_ref)
    bias = bias2_ref[0:1, :]
    for i in range(tiles):
        for z in range(edge):
            keep = mask_ref[z * rows : (z + 1) * rows, tile_of(i)]
            value = half(jnp.maximum(result(i, z) + bias, 0.0) * keep)
            for b in range(bricks):
                rt2_ref[b, z, :, tile_of(i)] = value[b * edge : (b + 1) * edge]
    rt2_ref[bricks] = jnp.zeros_like(rt2_ref[bricks])

    @pl.when(tables.live())
    def _():
        def field(b, z):
            return load(rt2_ref, b, z)

        fill_padded(pad2_ref, tables, edge, field, field, [(k, k + 1) for k in range(tiles - 1)])
        result = convolve([window_of(pad2_ref, i) for i in range(tiles - 2)], rows, edge, band2_ref)
        bias = bias2_ref[1:2, :]
        for i in range(tiles - 2):
            for z in range(edge):
                keep = mask_ref[z * rows : (z + 1) * rows, tile_of(i + 1)]
                value = jnp.maximum(result(i, z) + bias, 0.0) * keep
                for b in range(bricks):
                    mid_ref[b, z, :, tile_of(i)] = value[b * edge : (b + 1) * edge].astype(BF16)
        choose_parcels(tables, mid_ref, fa_ref, fb_ref)


def choose_parcels(tables, field_ref, fa_ref, fb_ref):
    odd = lax.rem(lax.axis_index("frame"), 2) == 1
    for slot in range(tables.slots):
        ahead, back = tables.ahead_ref[0, slot], tables.back_ref[0, slot]
        fa_ref[slot] = field_ref[jnp.where(odd, back, ahead)]
        fb_ref[slot] = field_ref[jnp.where(odd, ahead, back)]


def border_kernel(*refs):
    tables, refs = Tables(refs[:6]), refs[6:]
    border_body(tables, *refs)


def border_body(
    tables,
    rt_ref,
    mask_ref,
    rt2_ref,
    pad2_ref,
    band1_ref,
    band2_ref,
    bias2_ref,
    ra_ref,
    rb_ref,
    out_ref,
    fa_ref,
    fb_ref,
    edge_ref,
    side_ref,
    pad_ref,
):
    bricks, edge, _, wide = rt_ref.shape
    bricks -= 1
    tiles = wide // LANES
    size = (edge + 4) * 8
    slabs = tables.slabs
    rows = bricks * edge
    low, zero = low_half(), zero_tile()
    ends = (tile_of(0), tile_of(tiles - 1))
    odd = lax.rem(lax.axis_index("space"), 2) == 1
    arrived_a, arrived_b = ra_ref[...].astype(F32), rb_ref[...].astype(F32)
    arrived = (
        jnp.where(tables.has(0), jnp.where(odd, arrived_a, arrived_b), 0.0),
        jnp.where(tables.has(1), jnp.where(odd, arrived_b, arrived_a), 0.0),
    )

    def arrived_tile(side, k, i, c):
        at = k * size + i * 8
        return arrived[side][at : at + 8, tile_of(c)]

    def own_block(side, k):
        brick = tables.receiver(side, k)
        tile = ends[side]
        y_low, y_high = tables.local(brick, 2), tables.local(brick, 3)
        planes = [paired(side, rt_ref[tables.local(brick, 4), edge - 1, :, tile], zero, zero)]
        before, after = [[None, None]], [[None, None]]
        for z in range(edge):
            face = arrived_tile(side, k, z + 1, 1 - side)
            planes.append(paired(side, rt_ref[brick, z, :, tile], face, zero))
            before.append(paired(side, rt_ref[y_low, z, :, tile], zero, zero))
            after.append(paired(side, rt_ref[y_high, z, :, tile], zero, zero))
        planes.append(paired(side, rt_ref[tables.local(brick, 5), 0, :, tile], zero, zero))
        return planes, before + [[None, None]], after + [[None, None]]

    def far_block(side, k):
        planes = [[arrived_tile(side, k, i, c) for c in range(2)] for i in range(edge + 2)]
        c = 1 - side
        flag = planes[0][c]
        planes[0][c] = jnp.where(low, flag, zero) if c else jnp.where(low, zero, flag)
        mine = tables.sent(side, k)
        before, after = [[None, None]], [[None, None]]
        for z in range(edge):
            face = rt_ref[mine, z, :, ends[side]] * flag
            face = jnp.where(low, zero, face) if c else jnp.where(low, face, zero)
            planes[z + 1][c] = planes[z + 1][c] + face
            rims = []
            for i in (edge + 2, edge + 3):
                pair = [arrived_tile(side, k, i, d)[z : z + 1] for d in range(2)]
                rims.append([jnp.broadcast_to(r, (8, LANES)) for r in pair])
            before.append(rims[0])
            after.append(rims[1])
        return planes, before + [[None, None]], after + [[None, None]]

    blocks = []
    for k in range(slabs):
        blocks += [own_block(0, k), own_block(1, k), far_block(0, k), far_block(1, k)]
    count = len(blocks) * 8
    for i in range(edge + 2):
        for q in range(0, len(blocks), 2):
            shifts = [three_shifts(p[i], r[i], s[i]) for p, r, s in blocks[q : q + 2]]
            at = i * count + q * 8
            for dy in range(3):
                for c in range(2):
                    block = jnp.concatenate([shifts[0][dy][c], shifts[1][dy][c]], axis=0)
                    side_ref[dy, at : at + 16, tile_of(c)] = block.astype(BF16)

    for b in range(bricks + 1):
        for z in range(edge):
            for side in range(2):
                edge_ref[b, z, :, tile_of(side)] = rt2_ref[b, z, :, ends[side]]

    def side_window(dy, at, n):
        return side_ref[dy, at : at + n, :]

    result = convolve([side_window], count, edge, band1_ref)
    bias = bias2_ref[0:1, :]
    for z in range(edge):
        value = jnp.maximum(result(0, z) + bias, 0.0)
        for k in range(slabs):
            for side in range(2):
                at = (4 * k + side) * 8
                brick = tables.receiver(side, k)
                inside = jnp.minimum(brick, bricks - 1)
                from_row = pl.multiple_of((z * bricks + inside) * edge, edge)
                new = half(value[at : at + 8] * mask_ref[pl.ds(from_row, edge), ends[side]])
                old = edge_ref[brick, z, :, tile_of(side)]
                new = jnp.where(low, new, old) if side else jnp.where(low, old, new)
                edge_ref[brick, z, :, tile_of(side)] = jnp.where(brick < bricks, new, old)
                at += 16
                far = half(value[at : at + 8]) * arrived_tile(side, k, z + 1, side)
                edge_ref[bricks + 1 + k, z, :, tile_of(1 - side)] = far

    outer = [(tables.rim(b, 0), tables.rim(b, 1)) for b in range(bricks)]

    @pl.when(tables.live())
    def _():
        def own(b, z):
            left, right = edge_ref[outer[b][0], z, :, tile_of(1)], edge_ref[outer[b][1], z, :, tile_of(0)]
            return [left, edge_ref[b, z, :, tile_of(0)], edge_ref[b, z, :, tile_of(1)], right]

        def rim(brick, z):
            return [None, edge_ref[brick, z, :, tile_of(0)], edge_ref[brick, z, :, tile_of(1)], None]

        fill_padded(pad_ref, tables, edge, own, rim, [(0, 1), (2, 3)])

        def low_window(dy, at, n):
            return jnp.concatenate(
                [pad_ref[dy, at : at + n, tile_of(0)], pad2_ref[dy, at : at + n, tile_of(0)]], axis=1
            )

        def high_window(dy, at, n):
            return jnp.concatenate(
                [pad2_ref[dy, at : at + n, tile_of(tiles - 2)], pad_ref[dy, at : at + n, tile_of(1)]],
                axis=1,
            )

        result = convolve([low_window, high_window], rows, edge, band2_ref)
        bias = bias2_ref[1:2, :]
        for side in range(2):
            for z in range(edge):
                keep = mask_ref[z * rows : (z + 1) * rows, ends[side]]
                value = jnp.maximum(result(side, z) + bias, 0.0) * keep
                for b in range(bricks):
                    out_ref[b, z, :, tile_of(side)] = value[b * edge : (b + 1) * edge].astype(BF16)
        choose_parcels(tables, out_ref, fa_ref, fb_ref)


def temporal_part(tables, tiles, rt_ref, mask_ref, hid_ref, ga_ref, gb_ref, band, b, put):
    bricks, edge, _, part = hid_ref.shape
    odd = lax.rem(lax.axis_index("frame"), 2) == 1

    def flat(block):
        return block.astype(F32).reshape(edge * edge, part)

    prior, later = tables.prior_ref[0, b], tables.later_ref[0, b]
    at_prior = jnp.clip(prior, 0, tables.slots - 1)
    at_later = jnp.clip(later, 0, tables.slots - 1)
    before = flat(jnp.where(odd, ga_ref[at_prior], gb_ref[at_prior]))
    after = flat(jnp.where(odd, gb_ref[at_later], ga_ref[at_later]))
    before = jnp.where(prior >= 0, before, 0.0).astype(BF16)
    after = jnp.where(later >= 0, after, 0.0).astype(BF16)
    here = flat(hid_ref[b]).astype(BF16)
    lhs = [
        jnp.concatenate([f[:, tile_of(k)] for f in (before, here, after)], axis=1)
        for k in range(len(tiles))
    ]
    total = jnp.dot(jnp.concatenate(lhs, axis=0), band, preferred_element_type=F32)
    for k, tile in enumerate(tiles):
        for z in range(edge):
            at = (z * bricks + b) * edge
            keep = mask_ref[at : at + edge, tile_of(tile)]
            row = k * edge * edge + z * edge
            sums = half(rt_ref[b, z, :, tile_of(tile)]) + total[row : row + edge]
            put(b, z, k, (keep * sums).astype(BF16))


def middle_out_kernel(*refs):
    tables, refs = Tables(refs[:6]), refs[6:]
    middle_out_body(tables, *refs)


def middle_out_body(
    tables,
    rt_ref,
    mask_ref,
    hid_ref,
    ga_ref,
    gb_ref,
    w_ref,
    order_ref,
    out_ref,
    band_ref,
):
    depth = w_ref.shape[1]
    blank = jnp.zeros((depth, depth), BF16)
    for i in range(3):
        at = 2 * i * depth
        band_ref[at : at + depth, :] = jnp.concatenate([w_ref[i], blank], axis=1)
        band_ref[at + depth : at + 2 * depth, :] = jnp.concatenate([blank, w_ref[i]], axis=1)
    tiles = rt_ref.shape[-1] // LANES

    def put(b, z, k, value):
        out_ref[b, z, :, tile_of(k)] = value

    band = band_ref[...]
    for b in range(tables.bricks):
        temporal_part(
            tables,
            list(range(1, tiles - 1)),
            rt_ref,
            mask_ref,
            hid_ref,
            ga_ref,
            gb_ref,
            band,
            b,
            put,
        )


def edge_out_kernel(*refs):
    tables, refs = Tables(refs[:6]), refs[6:]
    edge_out_body(tables, *refs)


def edge_out_body(
    tables,
    rt_ref,
    mask_ref,
    hid_ref,
    ga_ref,
    gb_ref,
    band_ref,
    middle_ref,
    out_hbm,
    held_ref,
    sems,
):
    tiles = rt_ref.shape[-1] // LANES
    wide = tiles * LANES
    copies = [
        pltpu.make_async_copy(
            middle_ref, out_hbm.at[0, :, :, :, LANES : wide - LANES], sems.at[2 * tables.bricks]
        )
    ]
    copies[0].start()

    def put(b, z, k, value):
        held_ref[k, b, z] = value

    band = band_ref[...]
    for b in range(tables.bricks):
        temporal_part(
            tables, [0, tiles - 1], rt_ref, mask_ref, hid_ref, ga_ref, gb_ref, band, b, put
        )
        for k, tile in enumerate((0, tiles - 1)):
            copies.append(
                pltpu.make_async_copy(
                    held_ref.at[k, b], out_hbm.at[0, b, :, :, tile_of(tile)], sems.at[2 * b + k]
                )
            )
            copies[-1].start()
    for copy in copies:
        copy.wait()


VMEM = pl.BlockSpec(memory_space=pltpu.VMEM)
HBM = pl.BlockSpec(memory_space=pltpu.HBM)


def in_hbm(*arrays):
    return [pltpu.with_memory_space_constraint(a, pltpu.HBM) for a in arrays]


def cost(flops, moved):
    return pl.CostEstimate(flops=flops, bytes_accessed=moved, transcendentals=0)


def per_device(
    swaps,
    features,
    occupancy,
    w_spatial,
    b_spatial,
    w_temporal,
    face_send,
    face_source,
    send_ahead,
    from_prior,
    send_back,
    from_later,
):
    _, bricks, edge, _, wide = features.shape
    slabs = face_send.shape[1] // 2
    slots = send_ahead.shape[1]
    rows = bricks * edge * edge
    depth = w_spatial.shape[2]
    shape = jax.ShapeDtypeStruct
    space_first, space_second, frame_first, frame_second = swaps
    parcel = shape((slabs * (edge + 4) * 8, 2 * LANES), BF16)
    field = shape((bricks + 1, edge, edge, wide), F32)
    arguments = (
        face_send,
        face_source,
        send_ahead,
        from_prior,
        send_back,
        from_later,
        occupancy,
        features,
        w_spatial,
        b_spatial,
        w_temporal,
    )
    *table, rolled, mask, parcel_a, parcel_b, w_held, b_held, wt_held = pl.pallas_call(
        pack_kernel,
        name="pack",
        out_shape=tuple(shape(a.shape, a.dtype) for a in arguments[:6])
        + (field, shape((rows, wide), F32), parcel, parcel)
        + tuple(shape(a.shape, a.dtype) for a in arguments[8:]),
        in_specs=[HBM] * 11,
        out_specs=(VMEM,) * 13,
        scratch_shapes=[pltpu.VMEM(a.shape, a.dtype) for a in arguments[6:8]]
        + [pltpu.SemaphoreType.DMA((11,))],
        compiler_params=pltpu.CompilerParams(vmem_limit_bytes=8 << 20),
        cost_estimate=cost(10**8, 10**6),
    )(*in_hbm(*arguments))
    space_a = lax.ppermute(parcel_a, AXES, space_first)
    space_b = lax.ppermute(parcel_b, AXES, space_second)

    half_wide = wide // 2
    band = shape((48 * depth, 2 * LANES), BF16)
    pad_rows = (edge + 2) * bricks * edge
    hidden = shape((bricks, edge, edge, half_wide), BF16)
    sent = shape((slots, edge, edge, half_wide), BF16)
    rolled2, pad2, band1, band2, bias2, middle, parcel_a, parcel_b = pl.pallas_call(
        inner_kernel,
        name="inner",
        out_shape=(
            field,
            shape((3, pad_rows, wide - LANES), BF16),
            band,
            band,
            shape((2, LANES), F32),
            hidden,
            sent,
            sent,
        ),
        in_specs=[VMEM] * 10,
        out_specs=(VMEM,) * 8,
        scratch_shapes=[pltpu.VMEM((3, pad_rows, wide + LANES), BF16)],
        compiler_params=pltpu.CompilerParams(vmem_limit_bytes=24 << 20),
        cost_estimate=cost(10**9, 4 * 10**6),
    )(*table, rolled, mask, w_held, b_held)
    middle_a = lax.ppermute(parcel_a, AXES, frame_first)
    middle_b = lax.ppermute(parcel_b, AXES, frame_second)

    edges, parcel_a, parcel_b = pl.pallas_call(
        border_kernel,
        name="border",
        out_shape=(hidden, sent, sent),
        in_specs=[VMEM] * 15,
        out_specs=(VMEM,) * 3,
        scratch_shapes=[
            pltpu.VMEM((bricks + 1 + slabs, edge, edge, 2 * LANES), F32),
            pltpu.VMEM((3, (edge + 2) * 32 * slabs, 2 * LANES), BF16),
            pltpu.VMEM((3, pad_rows, 2 * LANES), BF16),
        ],
        compiler_params=pltpu.CompilerParams(vmem_limit_bytes=16 << 20),
        cost_estimate=cost(5 * 10**8, 2 * 10**6),
    )(*table, rolled, mask, rolled2, pad2, band1, band2, bias2, space_a, space_b)
    edge_a = lax.ppermute(parcel_a, AXES, frame_first)
    edge_b = lax.ppermute(parcel_b, AXES, frame_second)

    middle_out, band = pl.pallas_call(
        middle_out_kernel,
        name="middle_out",
        out_shape=(hidden, shape((6 * depth, LANES), BF16)),
        in_specs=[VMEM] * 12 + [pl.BlockSpec(memory_space=pl.ANY)],
        out_specs=(VMEM, VMEM),
        compiler_params=pltpu.CompilerParams(vmem_limit_bytes=8 << 20),
        cost_estimate=cost(10**8, 10**6),
    )(*table, rolled, mask, middle, middle_a, middle_b, wt_held, edges)
    return pl.pallas_call(
        edge_out_kernel,
        name="edge_out",
        out_shape=shape(features.shape, BF16),
        in_specs=[VMEM] * 13,
        out_specs=HBM,
        scratch_shapes=[
            pltpu.VMEM((2, bricks, edge, edge, LANES), BF16),
            pltpu.SemaphoreType.DMA((2 * bricks + 1,)),
        ],
        compiler_params=pltpu.CompilerParams(vmem_limit_bytes=8 << 20),
        cost_estimate=cost(10**8, 10**6),
    )(*table, rolled, mask, edges, edge_a, edge_b, band, middle_out)


def solution(mesh):
    swaps = swap_pairs(mesh.shape["space"], mesh.shape["frame"])
    in_specs = (
        P("frame", "space", None, None, None),
        P("frame", "space", None),
        P(),
        P(),
        P(),
        P("frame", "space"),
        P("frame", "space", None),
        P("frame", "space"),
        P("frame", "space"),
        P("frame", "space"),
        P("frame", "space"),
    )
    out_specs = P("frame", "space", None, None, None)
    return jax.shard_map(
        functools.partial(per_device, swaps),
        mesh=mesh,
        in_specs=in_specs,
        out_specs=out_specs,
        check_vma=False,
    )
```

```python
import functools

import jax
import jax.numpy as jnp
from jax import lax
from jax.experimental import pallas as pl
from jax.experimental.pallas import tpu as pltpu
from jax.sharding import PartitionSpec as P


F32 = jnp.float32
BF16 = jnp.bfloat16
LANES = 128
AXES = ("space", "frame")


def swap(parcel, pairs):
    return lax.ppermute(parcel, AXES, pairs)


def swap_pairs(peers, frames):
    def at(s, t):
        return s * frames + t

    def second(i, n):
        return ((i + 1) ^ 1) - 1 if 0 < i < n - 1 else -1

    idle = {at(s, t): at(s, t ^ 1) for s in (0, peers - 1) for t in range(frames)}
    space_first, space_second, frame_first, frame_second = [], [], [], []
    thirds = [[], [], []]
    for s in range(peers):
        for t in range(frames):
            space_first.append((at(s, t), at(s ^ 1, t)))
            other = second(s, peers)
            space_second.append((at(s, t), at(other, t) if other >= 0 else idle[at(s, t)]))
            frame_first.append((at(s, t), at(s, t ^ 1)))
            other = second(t, frames)
            frame_second.append((at(s, t), at(s, other) if other >= 0 else at(s ^ 1, t)))
            for turn in range(3):
                if t % 3 == turn and t + 1 < frames:
                    target = at(s, t + 1)
                elif (t + 2) % 3 == turn and t > 0:
                    target = at(s, t - 1)
                else:
                    target = at(s ^ 1, t)
                thirds[turn].append((at(s, t), target))
    return space_first, space_second, frame_first, frame_second, thirds


def iota(shape, dim):
    return lax.broadcasted_iota(jnp.int32, shape, dim)


def low_half():
    return iota((8, LANES), 1) < LANES // 2


def zero_tile():
    return jnp.zeros((8, LANES), F32)


def half(tile):
    return pltpu.roll(tile, LANES // 2, 1)


def tile_of(k):
    return slice(k * LANES, (k + 1) * LANES)


class Tables:
    def __init__(self, refs):
        self.send_ref, source_ref, self.ahead_ref, self.prior_ref, self.back_ref, self.later_ref = refs
        self.bricks = source_ref.shape[1]
        self.slabs = self.send_ref.shape[1] // 2
        self.slots = self.ahead_ref.shape[1]
        self.source = [[source_ref[0, b, f] for f in range(6)] for b in range(self.bricks)]

    def live(self):
        return self.ahead_ref[0, 0] >= 0

    def has(self, side):
        return self.send_ref[0, side * self.slabs] >= 0

    def brick_of(self, entry):
        return (entry * 10923) >> 16

    def sent(self, side, k):
        entry = self.send_ref[0, side * self.slabs + k]
        return jnp.where(entry < 0, self.bricks, self.brick_of(entry))

    def raw(self, brick, face):
        if isinstance(brick, int):
            return self.source[brick][face]
        entry = -1
        for b in range(self.bricks):
            entry = jnp.where(brick == b, self.source[b][face], entry)
        return entry

    def local(self, brick, face):
        entry = self.raw(brick, face) - 2 * self.slabs
        return jnp.where(entry >= 0, self.brick_of(entry), self.bricks)

    def remote(self, brick, face):
        entry = self.raw(brick, face)
        first = face * self.slabs
        return (entry >= first) & (entry < first + self.slabs)

    def rim(self, brick, face):
        arrived = self.bricks + 1 + self.raw(brick, face) - face * self.slabs
        return jnp.where(self.remote(brick, face), arrived, self.local(brick, face))

    def receiver(self, side, k):
        found = self.bricks
        for b in range(self.bricks):
            found = jnp.where(self.raw(b, side) == side * self.slabs + k, b, found)
        return found


def paired(side, tile, outer, spare):
    low = low_half()
    if side:
        return [jnp.where(low, spare, tile), jnp.where(low, tile, outer)]
    return [jnp.where(low, outer, tile), jnp.where(low, tile, spare)]


def pack_kernel(*refs):
    sources, table_refs, (rt_ref, mask_ref, pa_ref, pb_ref) = refs[:11], refs[11:17], refs[17:21]
    held, sems = table_refs + refs[24:26] + refs[21:24], refs[26]
    copies = [pltpu.make_async_copy(s, d, sems.at[i]) for i, (s, d) in enumerate(zip(sources, held))]
    for copy in copies:
        copy.start()
    copies, late_copies, held = copies[:8], copies[8:], held[:8]
    occ_ref, feat_ref = held[6:]
    _, bricks, edge, _, wide = feat_ref.shape
    channels = wide // edge
    per_tile = LANES // (edge * edge)
    rows8, lanes8 = iota((8, LANES), 0), iota((8, LANES), 1)
    low = low_half()
    spread = (iota((LANES, wide), 0) % edge == iota((LANES, wide), 1) // channels).astype(F32)
    spread = spread.astype(BF16)
    for copy in copies[:-1]:
        copy.wait()
    tables = Tables(table_refs)
    slabs = tables.slabs
    occ = occ_ref[0].astype(F32)
    picked = []
    for z in range(edge):
        keep = (lanes8 // edge) == (z % per_tile) * edge + rows8
        for b in range(bricks):
            row = jnp.broadcast_to(occ[b : b + 1, tile_of(z // per_tile)], (8, LANES))
            picked.append(jnp.where(keep, row, 0.0))
    mask = jnp.dot(jnp.concatenate(picked, axis=0).astype(BF16), spread, preferred_element_type=F32)
    mask_ref[...] = mask
    tiles = wide // LANES
    copies[-1].wait()
    for z in range(edge):
        for b in range(bricks):
            at = (z * bricks + b) * edge
            block = feat_ref[0, b, z].astype(F32) * mask[at : at + edge]
            for k in range(tiles):
                rt_ref[b, z, :, tile_of(k)] = half(block[:, tile_of(k)])
    rt_ref[bricks] = jnp.zeros_like(rt_ref[bricks])

    zero = zero_tile()
    ends = (tile_of(0), tile_of(tiles - 1))

    def window(side, k):
        brick = tables.sent(side, k)
        inside = jnp.minimum(brick, bricks - 1)
        own, other = ends[side], ends[1 - side]
        flag = jnp.where(tables.remote(brick, side), 1.0, 0.0)
        near = tables.local(brick, side)
        planes = [paired(side, rt_ref[tables.local(brick, 4), edge - 1, :, own], flag + zero, zero)]
        for z in range(edge):
            at = pl.multiple_of((z * bricks + inside) * edge, edge)
            keep = half(mask_ref[pl.ds(at, edge), own])
            planes.append(paired(side, rt_ref[brick, z, :, own], rt_ref[near, z, :, other], keep))
        planes.append(paired(side, rt_ref[tables.local(brick, 5), 0, :, own], zero, zero))
        for face, row in ((2, edge - 1), (3, 0)):
            brick_y = tables.local(brick, face)
            gathered = zero
            for z in range(edge):
                tile = rt_ref[brick_y, z, :, own]
                if (z - row) % 8:
                    tile = pltpu.roll(tile, (z - row) % 8, 0)
                gathered = jnp.where(rows8 == z, tile, gathered)
            planes.append(paired(side, gathered, zero, zero))
        return [jnp.concatenate([p[c] for p in planes], axis=0) for c in range(2)]

    odd = lax.rem(lax.axis_index("space"), 2) == 1
    size = (edge + 4) * 8
    for k in range(slabs):
        down, up = window(0, k), window(1, k)
        for c in range(2):
            at = slice(k * size, (k + 1) * size)
            pa_ref[at, tile_of(c)] = jnp.where(odd, down[c], up[c]).astype(BF16)
            pb_ref[at, tile_of(c)] = jnp.where(odd, up[c], down[c]).astype(BF16)
    for copy in late_copies:
        copy.wait()


def tap_place(dz, dy):
    return (dz // 2) * 6 + (1, 0, 2)[dy] * 2 + dz % 2


def fill_band(w_ref, layer, band_ref):
    blank = jnp.zeros(w_ref.shape[2:], BF16)
    depth = w_ref.shape[2]
    for dy in (1, 0, 2):
        for dz in range(3):
            tap = 3 * dz + dy
            before, here, after = (w_ref[layer, 3 * tap + i] for i in range(3))
            for row, (left, right) in enumerate(
                ((before, blank), (here, before), (after, here), (blank, after))
            ):
                block = jnp.concatenate([left, right], axis=1)
                for out in range(2):
                    at = (tap_place(dz + out, dy) * 4 + row) * depth
                    band_ref[at : at + depth, tile_of(out)] = block
        for out, dz in ((0, 3), (1, 0)):
            at = tap_place(dz, dy) * 4 * depth
            band_ref[at : at + 4 * depth, tile_of(out)] = jnp.zeros((4 * depth, LANES), BF16)


def shifted(tile, rim, down):
    if tile is None and rim is None:
        return None
    zero = zero_tile()
    tile = zero if tile is None else tile
    rim = zero if rim is None else rim
    rows8 = iota(tile.shape, 0)
    if down:
        return pltpu.roll(jnp.where(rows8 == 7, rim, tile), 1, 0)
    return pltpu.roll(jnp.where(rows8 == 0, rim, tile), 7, 0)


def three_shifts(line, before, after):
    return (
        [shifted(t, r, True) for t, r in zip(line, before)],
        line,
        [shifted(t, r, False) for t, r in zip(line, after)],
    )


def merged(line, pairs):
    low, zero = low_half(), zero_tile()
    full = [zero if t is None else t for t in line]
    return [jnp.where(low, full[i], full[j]) for i, j in pairs]


def fill_padded(pad_ref, tables, edge, own, rim, pairs):
    bricks = tables.bricks
    index = [[tables.local(b, f) for f in range(2, 6)] for b in range(bricks)]

    def lines(b, z):
        y_low, y_high, z_low, z_high = index[b]
        if 0 <= z < edge:
            return own(b, z), rim(y_low, z), rim(y_high, z)
        line = rim(z_low, edge - 1) if z < 0 else rim(z_high, 0)
        return line, [None] * len(line), [None] * len(line)

    def store(dy, z, first, built):
        at = ((z + 1) * bricks + first) * edge
        for k in range(len(pairs)):
            block = jnp.concatenate([built[0][k], built[1][k]], axis=0)
            pad_ref[dy, at : at + 2 * edge, tile_of(k)] = block.astype(BF16)

    places = [(z, first) for z in range(-1, edge + 1) for first in range(0, bricks, 2)]
    for z, first in places:
        store(1, z, first, [merged(lines(b, z)[0], pairs) for b in (first, first + 1)])
    for dy in (0, 2):
        for z, first in places:
            built = []
            for b in (first, first + 1):
                sides = lines(b, z)
                moved = [shifted(t, r, dy == 0) for t, r in zip(sides[0], sides[1 + dy // 2])]
                built.append(merged(moved, pairs))
            store(dy, z, first, built)


def convolve(windows, rows, edge, band_ref):
    blocks = []
    for window in windows:
        parts = []
        for first in (0, 2):
            for dy in (1, 0, 2):
                for dz in (first, first + 1):
                    starts = [(2 * zz + dz) * rows for zz in range(edge // 2)]
                    parts.append(jnp.concatenate([window(dy, at, rows) for at in starts], axis=0))
        blocks.append(parts)
    total = 0.0
    for first in (0, 6):
        lhs = [jnp.concatenate(parts[first : first + 6], axis=1) for parts in blocks]
        band = band_ref[first * 2 * LANES : (first + 6) * 2 * LANES, :]
        total = total + jnp.dot(jnp.concatenate(lhs, axis=0), band, preferred_element_type=F32)

    def result(window, z):
        at = (window * (edge // 2) + z // 2) * rows
        return total[at : at + rows, tile_of(z % 2)]

    return result


def inner_kernel(
    *refs,
):
    tables, refs = Tables(refs[:6]), refs[6:]
    inner_body(tables, *refs)


def inner_body(
    tables,
    rt_ref,
    mask_ref,
    w_ref,
    bias_ref,
    rt2_ref,
    pad2_ref,
    band1_ref,
    band2_ref,
    bias2_ref,
    mid_ref,
    fa_ref,
    fb_ref,
    fc_ref,
    pad_ref,
):
    bricks, edge, _, wide = rt_ref.shape
    bricks -= 1
    tiles = wide // LANES
    rows = bricks * edge

    def load(field_ref, brick, z):
        return [field_ref[brick, z, :, tile_of(k)] for k in range(tiles)]

    near = [(tables.local(b, 0), tables.local(b, 1)) for b in range(bricks)]

    def own(b, z):
        left = rt_ref[near[b][0], z, :, tile_of(tiles - 1)]
        right = rt_ref[near[b][1], z, :, tile_of(0)]
        return [left] + load(rt_ref, b, z) + [right]

    def rim(brick, z):
        return [None] + load(rt_ref, brick, z) + [None]

    fill_padded(pad_ref, tables, edge, own, rim, [(k, k + 1) for k in range(tiles + 1)])
    fill_band(w_ref, 0, band1_ref)
    for layer in range(2):
        row = bias_ref[layer : layer + 1, :]
        bias2_ref[layer : layer + 1, :] = jnp.concatenate([row, row], axis=1)

    def window_of(ref, first):
        def window(dy, at, count):
            return ref[dy, at : at + count, first * LANES : (first + 2) * LANES]

        return window

    fill_band(w_ref, 1, band2_ref)
    result = convolve([window_of(pad_ref, i) for i in range(tiles)], rows, edge, band1_ref)
    bias = bias2_ref[0:1, :]
    for i in range(tiles):
        for z in range(edge):
            keep = mask_ref[z * rows : (z + 1) * rows, tile_of(i)]
            value = half(jnp.maximum(result(i, z) + bias, 0.0) * keep)
            for b in range(bricks):
                rt2_ref[b, z, :, tile_of(i)] = value[b * edge : (b + 1) * edge]
    rt2_ref[bricks] = jnp.zeros_like(rt2_ref[bricks])

    @pl.when(tables.live())
    def _():
        def field(b, z):
            return load(rt2_ref, b, z)

        fill_padded(pad2_ref, tables, edge, field, field, [(k, k + 1) for k in range(tiles - 1)])
        result = convolve([window_of(pad2_ref, i) for i in range(tiles - 2)], rows, edge, band2_ref)
        bias = bias2_ref[1:2, :]
        for i in range(tiles - 2):
            for z in range(edge):
                keep = mask_ref[z * rows : (z + 1) * rows, tile_of(i + 1)]
                value = jnp.maximum(result(i, z) + bias, 0.0) * keep
                for b in range(bricks):
                    mid_ref[b, z, :, tile_of(i)] = value[b * edge : (b + 1) * edge].astype(BF16)
        frame = lax.rem(lax.axis_index("frame"), 3)
        for slot in range(tables.slots):
            ahead, back = tables.ahead_ref[0, slot], tables.back_ref[0, slot]
            for turn, parcel_ref in enumerate((fa_ref, fb_ref, fc_ref)):
                parcel_ref[slot] = mid_ref[jnp.where(frame == turn, ahead, back)]


def choose_parcels(tables, field_ref, fa_ref, fb_ref):
    odd = lax.rem(lax.axis_index("frame"), 2) == 1
    for slot in range(tables.slots):
        ahead, back = tables.ahead_ref[0, slot], tables.back_ref[0, slot]
        fa_ref[slot] = field_ref[jnp.where(odd, back, ahead)]
        fb_ref[slot] = field_ref[jnp.where(odd, ahead, back)]


def border_kernel(*refs):
    tables, refs = Tables(refs[:6]), refs[6:]
    border_body(tables, *refs)


def border_body(
    tables,
    rt_ref,
    mask_ref,
    rt2_ref,
    pad2_ref,
    band1_ref,
    band2_ref,
    bias2_ref,
    ra_ref,
    rb_ref,
    out_ref,
    fa_ref,
    fb_ref,
    edge_ref,
    side_ref,
    pad_ref,
):
    bricks, edge, _, wide = rt_ref.shape
    bricks -= 1
    tiles = wide // LANES
    size = (edge + 4) * 8
    slabs = tables.slabs
    rows = bricks * edge
    low, zero = low_half(), zero_tile()
    ends = (tile_of(0), tile_of(tiles - 1))
    odd = lax.rem(lax.axis_index("space"), 2) == 1
    arrived_a, arrived_b = ra_ref[...].astype(F32), rb_ref[...].astype(F32)
    arrived = (
        jnp.where(tables.has(0), jnp.where(odd, arrived_a, arrived_b), 0.0),
        jnp.where(tables.has(1), jnp.where(odd, arrived_b, arrived_a), 0.0),
    )

    def arrived_tile(side, k, i, c):
        at = k * size + i * 8
        return arrived[side][at : at + 8, tile_of(c)]

    def own_block(side, k):
        brick = tables.receiver(side, k)
        tile = ends[side]
        y_low, y_high = tables.local(brick, 2), tables.local(brick, 3)
        planes = [paired(side, rt_ref[tables.local(brick, 4), edge - 1, :, tile], zero, zero)]
        before, after = [[None, None]], [[None, None]]
        for z in range(edge):
            face = arrived_tile(side, k, z + 1, 1 - side)
            planes.append(paired(side, rt_ref[brick, z, :, tile], face, zero))
            before.append(paired(side, rt_ref[y_low, z, :, tile], zero, zero))
            after.append(paired(side, rt_ref[y_high, z, :, tile], zero, zero))
        planes.append(paired(side, rt_ref[tables.local(brick, 5), 0, :, tile], zero, zero))
        return planes, before + [[None, None]], after + [[None, None]]

    def far_block(side, k):
        planes = [[arrived_tile(side, k, i, c) for c in range(2)] for i in range(edge + 2)]
        c = 1 - side
        flag = planes[0][c]
        planes[0][c] = jnp.where(low, flag, zero) if c else jnp.where(low, zero, flag)
        mine = tables.sent(side, k)
        before, after = [[None, None]], [[None, None]]
        for z in range(edge):
            face = rt_ref[mine, z, :, ends[side]] * flag
            face = jnp.where(low, zero, face) if c else jnp.where(low, face, zero)
            planes[z + 1][c] = planes[z + 1][c] + face
            rims = []
            for i in (edge + 2, edge + 3):
                pair = [arrived_tile(side, k, i, d)[z : z + 1] for d in range(2)]
                rims.append([jnp.broadcast_to(r, (8, LANES)) for r in pair])
            before.append(rims[0])
            after.append(rims[1])
        return planes, before + [[None, None]], after + [[None, None]]

    blocks = []
    for k in range(slabs):
        blocks += [own_block(0, k), own_block(1, k), far_block(0, k), far_block(1, k)]
    count = len(blocks) * 8
    for i in range(edge + 2):
        for q in range(0, len(blocks), 2):
            shifts = [three_shifts(p[i], r[i], s[i]) for p, r, s in blocks[q : q + 2]]
            at = i * count + q * 8
            for dy in range(3):
                for c in range(2):
                    block = jnp.concatenate([shifts[0][dy][c], shifts[1][dy][c]], axis=0)
                    side_ref[dy, at : at + 16, tile_of(c)] = block.astype(BF16)

    for b in range(bricks + 1):
        for z in range(edge):
            for side in range(2):
                edge_ref[b, z, :, tile_of(side)] = rt2_ref[b, z, :, ends[side]]

    def side_window(dy, at, n):
        return side_ref[dy, at : at + n, :]

    result = convolve([side_window], count, edge, band1_ref)
    bias = bias2_ref[0:1, :]
    for z in range(edge):
        value = jnp.maximum(result(0, z) + bias, 0.0)
        for k in range(slabs):
            for side in range(2):
                at = (4 * k + side) * 8
                brick = tables.receiver(side, k)
                inside = jnp.minimum(brick, bricks - 1)
                from_row = pl.multiple_of((z * bricks + inside) * edge, edge)
                new = half(value[at : at + 8] * mask_ref[pl.ds(from_row, edge), ends[side]])
                old = edge_ref[brick, z, :, tile_of(side)]
                new = jnp.where(low, new, old) if side else jnp.where(low, old, new)
                edge_ref[brick, z, :, tile_of(side)] = jnp.where(brick < bricks, new, old)
                at += 16
                far = half(value[at : at + 8]) * arrived_tile(side, k, z + 1, side)
                edge_ref[bricks + 1 + k, z, :, tile_of(1 - side)] = far

    outer = [(tables.rim(b, 0), tables.rim(b, 1)) for b in range(bricks)]

    @pl.when(tables.live())
    def _():
        def own(b, z):
            left, right = edge_ref[outer[b][0], z, :, tile_of(1)], edge_ref[outer[b][1], z, :, tile_of(0)]
            return [left, edge_ref[b, z, :, tile_of(0)], edge_ref[b, z, :, tile_of(1)], right]

        def rim(brick, z):
            return [None, edge_ref[brick, z, :, tile_of(0)], edge_ref[brick, z, :, tile_of(1)], None]

        fill_padded(pad_ref, tables, edge, own, rim, [(0, 1), (2, 3)])

        def low_window(dy, at, n):
            return jnp.concatenate(
                [pad_ref[dy, at : at + n, tile_of(0)], pad2_ref[dy, at : at + n, tile_of(0)]], axis=1
            )

        def high_window(dy, at, n):
            return jnp.concatenate(
                [pad2_ref[dy, at : at + n, tile_of(tiles - 2)], pad_ref[dy, at : at + n, tile_of(1)]],
                axis=1,
            )

        result = convolve([low_window, high_window], rows, edge, band2_ref)
        bias = bias2_ref[1:2, :]
        for side in range(2):
            for z in range(edge):
                keep = mask_ref[z * rows : (z + 1) * rows, ends[side]]
                value = jnp.maximum(result(side, z) + bias, 0.0) * keep
                for b in range(bricks):
                    out_ref[b, z, :, tile_of(side)] = value[b * edge : (b + 1) * edge].astype(BF16)
        choose_parcels(tables, out_ref, fa_ref, fb_ref)


def pick_second(frame_refs):
    ga_ref, gb_ref = frame_refs
    odd = lax.rem(lax.axis_index("frame"), 2) == 1
    return (
        lambda slot: jnp.where(odd, ga_ref[slot], gb_ref[slot]),
        lambda slot: jnp.where(odd, gb_ref[slot], ga_ref[slot]),
    )


def pick_third(frame_refs):
    frame = lax.rem(lax.axis_index("frame"), 3)

    def choose(slot, turn):
        first, second, third = (ref[slot] for ref in frame_refs)
        return jnp.where(turn == 0, first, jnp.where(turn == 1, second, third))

    return (lambda slot: choose(slot, lax.rem(frame + 2, 3)), lambda slot: choose(slot, frame))


def temporal_part(tables, tiles, rt_ref, mask_ref, hid_ref, picks, band, b, put):
    bricks, edge, _, part = hid_ref.shape
    from_prior, from_later = picks

    def flat(block):
        return block.astype(F32).reshape(edge * edge, part)

    prior, later = tables.prior_ref[0, b], tables.later_ref[0, b]
    at_prior = jnp.clip(prior, 0, tables.slots - 1)
    at_later = jnp.clip(later, 0, tables.slots - 1)
    before = flat(from_prior(at_prior))
    after = flat(from_later(at_later))
    before = jnp.where(prior >= 0, before, 0.0).astype(BF16)
    after = jnp.where(later >= 0, after, 0.0).astype(BF16)
    here = flat(hid_ref[b]).astype(BF16)
    lhs = [
        jnp.concatenate([f[:, tile_of(k)] for f in (before, here, after)], axis=1)
        for k in range(len(tiles))
    ]
    total = jnp.dot(jnp.concatenate(lhs, axis=0), band, preferred_element_type=F32)
    for k, tile in enumerate(tiles):
        for z in range(edge):
            at = (z * bricks + b) * edge
            keep = mask_ref[at : at + edge, tile_of(tile)]
            row = k * edge * edge + z * edge
            sums = half(rt_ref[b, z, :, tile_of(tile)]) + total[row : row + edge]
            put(b, z, k, (keep * sums).astype(BF16))


def middle_out_kernel(*refs):
    tables, refs = Tables(refs[:6]), refs[6:]
    middle_out_body(tables, *refs)


def middle_out_body(
    tables,
    rt_ref,
    mask_ref,
    hid_ref,
    ga_ref,
    gb_ref,
    gc_ref,
    w_ref,
    order_ref,
    out_ref,
    band_ref,
):
    depth = w_ref.shape[1]
    blank = jnp.zeros((depth, depth), BF16)
    for i in range(3):
        at = 2 * i * depth
        band_ref[at : at + depth, :] = jnp.concatenate([w_ref[i], blank], axis=1)
        band_ref[at + depth : at + 2 * depth, :] = jnp.concatenate([blank, w_ref[i]], axis=1)
    tiles = rt_ref.shape[-1] // LANES

    def put(b, z, k, value):
        out_ref[b, z, :, tile_of(k)] = value

    band = band_ref[...]
    for b in range(tables.bricks):
        temporal_part(
            tables,
            list(range(1, tiles - 1)),
            rt_ref,
            mask_ref,
            hid_ref,
            pick_third((ga_ref, gb_ref, gc_ref)),
            band,
            b,
            put,
        )


def edge_out_kernel(*refs):
    tables, refs = Tables(refs[:6]), refs[6:]
    edge_out_body(tables, *refs)


def edge_out_body(
    tables,
    rt_ref,
    mask_ref,
    hid_ref,
    ga_ref,
    gb_ref,
    band_ref,
    middle_ref,
    out_hbm,
    held_ref,
    sems,
):
    tiles = rt_ref.shape[-1] // LANES
    wide = tiles * LANES
    copies = [
        pltpu.make_async_copy(
            middle_ref, out_hbm.at[0, :, :, :, LANES : wide - LANES], sems.at[2 * tables.bricks]
        )
    ]
    copies[0].start()

    def put(b, z, k, value):
        held_ref[k, b, z] = value

    band = band_ref[...]
    for b in range(tables.bricks):
        temporal_part(
            tables,
            [0, tiles - 1],
            rt_ref,
            mask_ref,
            hid_ref,
            pick_second((ga_ref, gb_ref)),
            band,
            b,
            put,
        )
        for k, tile in enumerate((0, tiles - 1)):
            copies.append(
                pltpu.make_async_copy(
                    held_ref.at[k, b], out_hbm.at[0, b, :, :, tile_of(tile)], sems.at[2 * b + k]
                )
            )
            copies[-1].start()
    for copy in copies:
        copy.wait()


VMEM = pl.BlockSpec(memory_space=pltpu.VMEM)
HBM = pl.BlockSpec(memory_space=pltpu.HBM)


def in_hbm(*arrays):
    return [pltpu.with_memory_space_constraint(a, pltpu.HBM) for a in arrays]


def cost(flops, moved):
    return pl.CostEstimate(flops=flops, bytes_accessed=moved, transcendentals=0)


def per_device(
    swaps,
    features,
    occupancy,
    w_spatial,
    b_spatial,
    w_temporal,
    face_send,
    face_source,
    send_ahead,
    from_prior,
    send_back,
    from_later,
):
    _, bricks, edge, _, wide = features.shape
    slabs = face_send.shape[1] // 2
    slots = send_ahead.shape[1]
    rows = bricks * edge * edge
    depth = w_spatial.shape[2]
    shape = jax.ShapeDtypeStruct
    space_first, space_second, frame_first, frame_second, thirds = swaps
    parcel = shape((slabs * (edge + 4) * 8, 2 * LANES), BF16)
    field = shape((bricks + 1, edge, edge, wide), F32)
    arguments = (
        face_send,
        face_source,
        send_ahead,
        from_prior,
        send_back,
        from_later,
        occupancy,
        features,
        w_spatial,
        b_spatial,
        w_temporal,
    )
    *table, rolled, mask, parcel_a, parcel_b, w_held, b_held, wt_held = pl.pallas_call(
        pack_kernel,
        name="pack",
        out_shape=tuple(shape(a.shape, a.dtype) for a in arguments[:6])
        + (field, shape((rows, wide), F32), parcel, parcel)
        + tuple(shape(a.shape, a.dtype) for a in arguments[8:]),
        in_specs=[HBM] * 11,
        out_specs=(VMEM,) * 13,
        scratch_shapes=[pltpu.VMEM(a.shape, a.dtype) for a in arguments[6:8]]
        + [pltpu.SemaphoreType.DMA((11,))],
        compiler_params=pltpu.CompilerParams(vmem_limit_bytes=8 << 20),
        cost_estimate=cost(10**8, 10**6),
    )(*in_hbm(*arguments))
    space_a = lax.ppermute(parcel_a, AXES, space_first)
    space_b = lax.ppermute(parcel_b, AXES, space_second)

    half_wide = wide // 2
    band = shape((48 * depth, 2 * LANES), BF16)
    pad_rows = (edge + 2) * bricks * edge
    hidden = shape((bricks, edge, edge, half_wide), BF16)
    sent = shape((slots, edge, edge, half_wide), BF16)
    rolled2, pad2, band1, band2, bias2, middle, *parcels = pl.pallas_call(
        inner_kernel,
        name="inner",
        out_shape=(
            field,
            shape((3, pad_rows, wide - LANES), BF16),
            band,
            band,
            shape((2, LANES), F32),
            hidden,
            sent,
            sent,
            sent,
        ),
        in_specs=[VMEM] * 10,
        out_specs=(VMEM,) * 9,
        scratch_shapes=[pltpu.VMEM((3, pad_rows, wide + LANES), BF16)],
        compiler_params=pltpu.CompilerParams(vmem_limit_bytes=24 << 20),
        cost_estimate=cost(10**9, 4 * 10**6),
    )(*table, rolled, mask, w_held, b_held)
    middles = [swap(parcel, turn) for parcel, turn in zip(parcels, thirds)]

    edges, parcel_a, parcel_b = pl.pallas_call(
        border_kernel,
        name="border",
        out_shape=(hidden, sent, sent),
        in_specs=[VMEM] * 15,
        out_specs=(VMEM,) * 3,
        scratch_shapes=[
            pltpu.VMEM((bricks + 1 + slabs, edge, edge, 2 * LANES), F32),
            pltpu.VMEM((3, (edge + 2) * 32 * slabs, 2 * LANES), BF16),
            pltpu.VMEM((3, pad_rows, 2 * LANES), BF16),
        ],
        compiler_params=pltpu.CompilerParams(vmem_limit_bytes=16 << 20),
        cost_estimate=cost(5 * 10**8, 2 * 10**6),
    )(*table, rolled, mask, rolled2, pad2, band1, band2, bias2, space_a, space_b)
    edge_a = swap(parcel_a, frame_first)
    edge_b = swap(parcel_b, frame_second)

    middle_out, band = pl.pallas_call(
        middle_out_kernel,
        name="middle_out",
        out_shape=(hidden, shape((6 * depth, LANES), BF16)),
        in_specs=[VMEM] * 13 + [pl.BlockSpec(memory_space=pl.ANY)],
        out_specs=(VMEM, VMEM),
        compiler_params=pltpu.CompilerParams(vmem_limit_bytes=8 << 20),
        cost_estimate=cost(10**8, 10**6),
    )(*table, rolled, mask, middle, *middles, wt_held, edges)
    return pl.pallas_call(
        edge_out_kernel,
        name="edge_out",
        out_shape=shape(features.shape, BF16),
        in_specs=[VMEM] * 13,
        out_specs=HBM,
        scratch_shapes=[
            pltpu.VMEM((2, bricks, edge, edge, LANES), BF16),
            pltpu.SemaphoreType.DMA((2 * bricks + 1,)),
        ],
        compiler_params=pltpu.CompilerParams(vmem_limit_bytes=8 << 20),
        cost_estimate=cost(10**8, 10**6),
    )(*table, rolled, mask, edges, edge_a, edge_b, band, middle_out)


def solution(mesh):
    swaps = swap_pairs(mesh.shape["space"], mesh.shape["frame"])
    in_specs = (
        P("frame", "space", None, None, None),
        P("frame", "space", None),
        P(),
        P(),
        P(),
        P("frame", "space"),
        P("frame", "space", None),
        P("frame", "space"),
        P("frame", "space"),
        P("frame", "space"),
        P("frame", "space"),
    )
    out_specs = P("frame", "space", None, None, None)
    return jax.shard_map(
        functools.partial(per_device, swaps),
        mesh=mesh,
        in_specs=in_specs,
        out_specs=out_specs,
        check_vma=False,
    )
```

```python
import functools

import jax
import jax.numpy as jnp
from jax import lax
from jax.experimental import pallas as pl
from jax.experimental.pallas import tpu as pltpu
from jax.sharding import PartitionSpec as P


F32 = jnp.float32
BF16 = jnp.bfloat16
LANES = 128
AXES = ("space", "frame")


def swap(parcel, pairs):
    return lax.ppermute(parcel, AXES, pairs)


def swap_pairs(peers, frames):
    def at(s, t):
        return s * frames + t

    def second(i, n):
        return ((i + 1) ^ 1) - 1 if 0 < i < n - 1 else -1

    idle = {at(s, t): at(s, t ^ 1) for s in (0, peers - 1) for t in range(frames)}
    space_first, space_second, frame_first, frame_second = [], [], [], []
    thirds = [[], [], []]
    for s in range(peers):
        for t in range(frames):
            space_first.append((at(s, t), at(s ^ 1, t)))
            other = second(s, peers)
            space_second.append((at(s, t), at(other, t) if other >= 0 else idle[at(s, t)]))
            frame_first.append((at(s, t), at(s, t ^ 1)))
            other = second(t, frames)
            frame_second.append((at(s, t), at(s, other) if other >= 0 else at(s ^ 1, t)))
            for turn in range(3):
                if t % 3 == turn and t + 1 < frames:
                    target = at(s, t + 1)
                elif (t + 2) % 3 == turn and t > 0:
                    target = at(s, t - 1)
                else:
                    target = at(s ^ 1, t)
                thirds[turn].append((at(s, t), target))
    return space_first, space_second, frame_first, frame_second, thirds


def iota(shape, dim):
    return lax.broadcasted_iota(jnp.int32, shape, dim)


def low_half():
    return iota((8, LANES), 1) < LANES // 2


def zero_tile():
    return jnp.zeros((8, LANES), F32)


def half(tile):
    return pltpu.roll(tile, LANES // 2, 1)


def tile_of(k):
    return slice(k * LANES, (k + 1) * LANES)


class Tables:
    def __init__(self, refs):
        self.send_ref, source_ref, self.ahead_ref, self.prior_ref, self.back_ref, self.later_ref = refs
        self.bricks = source_ref.shape[1]
        self.slabs = self.send_ref.shape[1] // 2
        self.slots = self.ahead_ref.shape[1]
        self.source = [[source_ref[0, b, f] for f in range(6)] for b in range(self.bricks)]

    def live(self):
        return self.ahead_ref[0, 0] >= 0

    def has(self, side):
        return self.send_ref[0, side * self.slabs] >= 0

    def brick_of(self, entry):
        return (entry * 10923) >> 16

    def sent(self, side, k):
        entry = self.send_ref[0, side * self.slabs + k]
        return jnp.where(entry < 0, self.bricks, self.brick_of(entry))

    def raw(self, brick, face):
        if isinstance(brick, int):
            return self.source[brick][face]
        entry = -1
        for b in range(self.bricks):
            entry = jnp.where(brick == b, self.source[b][face], entry)
        return entry

    def local(self, brick, face):
        entry = self.raw(brick, face) - 2 * self.slabs
        return jnp.where(entry >= 0, self.brick_of(entry), self.bricks)

    def remote(self, brick, face):
        entry = self.raw(brick, face)
        first = face * self.slabs
        return (entry >= first) & (entry < first + self.slabs)

    def rim(self, brick, face):
        arrived = self.bricks + 1 + self.raw(brick, face) - face * self.slabs
        return jnp.where(self.remote(brick, face), arrived, self.local(brick, face))

    def receiver(self, side, k):
        found = self.bricks
        for b in range(self.bricks):
            found = jnp.where(self.raw(b, side) == side * self.slabs + k, b, found)
        return found


def paired(side, tile, outer, spare):
    low = low_half()
    if side:
        return [jnp.where(low, spare, tile), jnp.where(low, tile, outer)]
    return [jnp.where(low, outer, tile), jnp.where(low, tile, spare)]


def pack_kernel(*refs):
    sources, table_refs, (rt_ref, mask_ref, pa_ref, pb_ref) = refs[:11], refs[11:17], refs[17:21]
    held, sems = table_refs + refs[24:26] + refs[21:24], refs[26]
    copies = [pltpu.make_async_copy(s, d, sems.at[i]) for i, (s, d) in enumerate(zip(sources, held))]
    for copy in copies:
        copy.start()
    copies, late_copies, held = copies[:8], copies[8:], held[:8]
    occ_ref, feat_ref = held[6:]
    _, bricks, edge, _, wide = feat_ref.shape
    channels = wide // edge
    per_tile = LANES // (edge * edge)
    rows8, lanes8 = iota((8, LANES), 0), iota((8, LANES), 1)
    low = low_half()
    spread = (iota((LANES, wide), 0) % edge == iota((LANES, wide), 1) // channels).astype(F32)
    spread = spread.astype(BF16)
    for copy in copies[:-1]:
        copy.wait()
    tables = Tables(table_refs)
    slabs = tables.slabs
    occ = occ_ref[0].astype(F32)
    picked = []
    for z in range(edge):
        keep = (lanes8 // edge) == (z % per_tile) * edge + rows8
        for b in range(bricks):
            row = jnp.broadcast_to(occ[b : b + 1, tile_of(z // per_tile)], (8, LANES))
            picked.append(jnp.where(keep, row, 0.0))
    mask = jnp.dot(jnp.concatenate(picked, axis=0).astype(BF16), spread, preferred_element_type=F32)
    mask_ref[...] = mask
    tiles = wide // LANES
    copies[-1].wait()
    for z in range(edge):
        for b in range(bricks):
            at = (z * bricks + b) * edge
            block = feat_ref[0, b, z].astype(F32) * mask[at : at + edge]
            for k in range(tiles):
                rt_ref[b, z, :, tile_of(k)] = half(block[:, tile_of(k)])
    rt_ref[bricks] = jnp.zeros_like(rt_ref[bricks])

    zero = zero_tile()
    ends = (tile_of(0), tile_of(tiles - 1))

    def window(side, k):
        brick = tables.sent(side, k)
        inside = jnp.minimum(brick, bricks - 1)
        own, other = ends[side], ends[1 - side]
        flag = jnp.where(tables.remote(brick, side), 1.0, 0.0)
        near = tables.local(brick, side)
        planes = [paired(side, rt_ref[tables.local(brick, 4), edge - 1, :, own], flag + zero, zero)]
        for z in range(edge):
            at = pl.multiple_of((z * bricks + inside) * edge, edge)
            keep = half(mask_ref[pl.ds(at, edge), own])
            planes.append(paired(side, rt_ref[brick, z, :, own], rt_ref[near, z, :, other], keep))
        planes.append(paired(side, rt_ref[tables.local(brick, 5), 0, :, own], zero, zero))
        for face, row in ((2, edge - 1), (3, 0)):
            brick_y = tables.local(brick, face)
            gathered = zero
            for z in range(edge):
                tile = rt_ref[brick_y, z, :, own]
                if (z - row) % 8:
                    tile = pltpu.roll(tile, (z - row) % 8, 0)
                gathered = jnp.where(rows8 == z, tile, gathered)
            planes.append(paired(side, gathered, zero, zero))
        return [jnp.concatenate([p[c] for p in planes], axis=0) for c in range(2)]

    odd = lax.rem(lax.axis_index("space"), 2) == 1
    size = (edge + 4) * 8
    for k in range(slabs):
        down, up = window(0, k), window(1, k)
        for c in range(2):
            at = slice(k * size, (k + 1) * size)
            pa_ref[at, tile_of(c)] = jnp.where(odd, down[c], up[c]).astype(BF16)
            pb_ref[at, tile_of(c)] = jnp.where(odd, up[c], down[c]).astype(BF16)
    for copy in late_copies:
        copy.wait()


def tap_place(dz, dy):
    return (dz // 2) * 6 + (1, 0, 2)[dy] * 2 + dz % 2


def fill_band(w_ref, layer, band_ref):
    blank = jnp.zeros(w_ref.shape[2:], BF16)
    depth = w_ref.shape[2]
    for dy in (1, 0, 2):
        for dz in range(3):
            tap = 3 * dz + dy
            before, here, after = (w_ref[layer, 3 * tap + i] for i in range(3))
            for row, (left, right) in enumerate(
                ((before, blank), (here, before), (after, here), (blank, after))
            ):
                block = jnp.concatenate([left, right], axis=1)
                for out in range(2):
                    at = (tap_place(dz + out, dy) * 4 + row) * depth
                    band_ref[at : at + depth, tile_of(out)] = block
        for out, dz in ((0, 3), (1, 0)):
            at = tap_place(dz, dy) * 4 * depth
            band_ref[at : at + 4 * depth, tile_of(out)] = jnp.zeros((4 * depth, LANES), BF16)


def shifted(tile, rim, down):
    if tile is None and rim is None:
        return None
    zero = zero_tile()
    tile = zero if tile is None else tile
    rim = zero if rim is None else rim
    rows8 = iota(tile.shape, 0)
    if down:
        return pltpu.roll(jnp.where(rows8 == 7, rim, tile), 1, 0)
    return pltpu.roll(jnp.where(rows8 == 0, rim, tile), 7, 0)


def three_shifts(line, before, after):
    return (
        [shifted(t, r, True) for t, r in zip(line, before)],
        line,
        [shifted(t, r, False) for t, r in zip(line, after)],
    )


def merged(line, pairs):
    low, zero = low_half(), zero_tile()
    full = [zero if t is None else t for t in line]
    return [jnp.where(low, full[i], full[j]) for i, j in pairs]


def fill_padded(pad_ref, tables, edge, own, rim, pairs):
    bricks = tables.bricks
    index = [[tables.local(b, f) for f in range(2, 6)] for b in range(bricks)]

    def lines(b, z):
        y_low, y_high, z_low, z_high = index[b]
        if 0 <= z < edge:
            return own(b, z), rim(y_low, z), rim(y_high, z)
        line = rim(z_low, edge - 1) if z < 0 else rim(z_high, 0)
        return line, [None] * len(line), [None] * len(line)

    def store(dy, z, first, built):
        at = ((z + 1) * bricks + first) * edge
        for k in range(len(pairs)):
            block = jnp.concatenate([built[0][k], built[1][k]], axis=0)
            pad_ref[dy, at : at + 2 * edge, tile_of(k)] = block.astype(BF16)

    places = [(z, first) for z in range(-1, edge + 1) for first in range(0, bricks, 2)]
    for z, first in places:
        store(1, z, first, [merged(lines(b, z)[0], pairs) for b in (first, first + 1)])
    for dy in (0, 2):
        for z, first in places:
            built = []
            for b in (first, first + 1):
                sides = lines(b, z)
                moved = [shifted(t, r, dy == 0) for t, r in zip(sides[0], sides[1 + dy // 2])]
                built.append(merged(moved, pairs))
            store(dy, z, first, built)


def convolve(windows, rows, edge, band_ref):
    blocks = []
    for window in windows:
        parts = []
        for first in (0, 2):
            for dy in (1, 0, 2):
                for dz in (first, first + 1):
                    starts = [(2 * zz + dz) * rows for zz in range(edge // 2)]
                    parts.append(jnp.concatenate([window(dy, at, rows) for at in starts], axis=0))
        blocks.append(parts)
    total = 0.0
    for first in (0, 6):
        lhs = [jnp.concatenate(parts[first : first + 6], axis=1) for parts in blocks]
        band = band_ref[first * 2 * LANES : (first + 6) * 2 * LANES, :]
        total = total + jnp.dot(jnp.concatenate(lhs, axis=0), band, preferred_element_type=F32)

    def result(window, z):
        at = (window * (edge // 2) + z // 2) * rows
        return total[at : at + rows, tile_of(z % 2)]

    return result


def inner_kernel(
    *refs,
):
    tables, refs = Tables(refs[:6]), refs[6:]
    inner_body(tables, *refs)


def inner_body(
    tables,
    rt_ref,
    mask_ref,
    w_ref,
    bias_ref,
    rt2_ref,
    pad2_ref,
    band1_ref,
    band2_ref,
    bias2_ref,
    mid_ref,
    fa_ref,
    fb_ref,
    fc_ref,
    pad_ref,
):
    bricks, edge, _, wide = rt_ref.shape
    bricks -= 1
    tiles = wide // LANES
    rows = bricks * edge

    def load(field_ref, brick, z):
        return [field_ref[brick, z, :, tile_of(k)] for k in range(tiles)]

    near = [(tables.local(b, 0), tables.local(b, 1)) for b in range(bricks)]

    def own(b, z):
        left = rt_ref[near[b][0], z, :, tile_of(tiles - 1)]
        right = rt_ref[near[b][1], z, :, tile_of(0)]
        return [left] + load(rt_ref, b, z) + [right]

    def rim(brick, z):
        return [None] + load(rt_ref, brick, z) + [None]

    fill_padded(pad_ref, tables, edge, own, rim, [(k, k + 1) for k in range(tiles + 1)])
    fill_band(w_ref, 0, band1_ref)
    for layer in range(2):
        row = bias_ref[layer : layer + 1, :]
        bias2_ref[layer : layer + 1, :] = jnp.concatenate([row, row], axis=1)

    def window_of(ref, first):
        def window(dy, at, count):
            return ref[dy, at : at + count, first * LANES : (first + 2) * LANES]

        return window

    fill_band(w_ref, 1, band2_ref)
    result = convolve([window_of(pad_ref, i) for i in range(tiles)], rows, edge, band1_ref)
    bias = bias2_ref[0:1, :]
    for i in range(tiles):
        for z in range(edge):
            keep = mask_ref[z * rows : (z + 1) * rows, tile_of(i)]
            value = half(jnp.maximum(result(i, z) + bias, 0.0) * keep)
            for b in range(bricks):
                rt2_ref[b, z, :, tile_of(i)] = value[b * edge : (b + 1) * edge]
    rt2_ref[bricks] = jnp.zeros_like(rt2_ref[bricks])

    @pl.when(tables.live())
    def _():
        def field(b, z):
            return load(rt2_ref, b, z)

        fill_padded(pad2_ref, tables, edge, field, field, [(k, k + 1) for k in range(tiles - 1)])
        result = convolve([window_of(pad2_ref, i) for i in range(tiles - 2)], rows, edge, band2_ref)
        bias = bias2_ref[1:2, :]
        for i in range(tiles - 2):
            for z in range(edge):
                keep = mask_ref[z * rows : (z + 1) * rows, tile_of(i + 1)]
                value = jnp.maximum(result(i, z) + bias, 0.0) * keep
                for b in range(bricks):
                    mid_ref[b, z, :, tile_of(i)] = value[b * edge : (b + 1) * edge].astype(BF16)
        frame = lax.rem(lax.axis_index("frame"), 3)
        for slot in range(tables.slots):
            ahead, back = tables.ahead_ref[0, slot], tables.back_ref[0, slot]
            for turn, parcel_ref in enumerate((fa_ref, fb_ref, fc_ref)):
                parcel_ref[slot] = mid_ref[jnp.where(frame == turn, ahead, back)]


def choose_parcels(tables, field_ref, fa_ref, fb_ref):
    odd = lax.rem(lax.axis_index("frame"), 2) == 1
    for slot in range(tables.slots):
        ahead, back = tables.ahead_ref[0, slot], tables.back_ref[0, slot]
        fa_ref[slot] = field_ref[jnp.where(odd, back, ahead)]
        fb_ref[slot] = field_ref[jnp.where(odd, ahead, back)]


def border_kernel(*refs):
    tables, refs = Tables(refs[:6]), refs[6:]
    border_body(tables, *refs)


def border_body(
    tables,
    rt_ref,
    mask_ref,
    rt2_ref,
    pad2_ref,
    band1_ref,
    band2_ref,
    bias2_ref,
    ra_ref,
    rb_ref,
    out_ref,
    fa_ref,
    fb_ref,
    edge_ref,
    side_ref,
    pad_ref,
):
    bricks, edge, _, wide = rt_ref.shape
    bricks -= 1
    tiles = wide // LANES
    size = (edge + 4) * 8
    slabs = tables.slabs
    rows = bricks * edge
    low, zero = low_half(), zero_tile()
    ends = (tile_of(0), tile_of(tiles - 1))
    odd = lax.rem(lax.axis_index("space"), 2) == 1
    arrived_a, arrived_b = ra_ref[...].astype(F32), rb_ref[...].astype(F32)
    arrived = (
        jnp.where(tables.has(0), jnp.where(odd, arrived_a, arrived_b), 0.0),
        jnp.where(tables.has(1), jnp.where(odd, arrived_b, arrived_a), 0.0),
    )

    def arrived_tile(side, k, i, c):
        at = k * size + i * 8
        return arrived[side][at : at + 8, tile_of(c)]

    def own_block(side, k):
        brick = tables.receiver(side, k)
        tile = ends[side]
        y_low, y_high = tables.local(brick, 2), tables.local(brick, 3)
        planes = [paired(side, rt_ref[tables.local(brick, 4), edge - 1, :, tile], zero, zero)]
        before, after = [[None, None]], [[None, None]]
        for z in range(edge):
            face = arrived_tile(side, k, z + 1, 1 - side)
            planes.append(paired(side, rt_ref[brick, z, :, tile], face, zero))
            before.append(paired(side, rt_ref[y_low, z, :, tile], zero, zero))
            after.append(paired(side, rt_ref[y_high, z, :, tile], zero, zero))
        planes.append(paired(side, rt_ref[tables.local(brick, 5), 0, :, tile], zero, zero))
        return planes, before + [[None, None]], after + [[None, None]]

    def far_block(side, k):
        planes = [[arrived_tile(side, k, i, c) for c in range(2)] for i in range(edge + 2)]
        c = 1 - side
        flag = planes[0][c]
        planes[0][c] = jnp.where(low, flag, zero) if c else jnp.where(low, zero, flag)
        mine = tables.sent(side, k)
        before, after = [[None, None]], [[None, None]]
        for z in range(edge):
            face = rt_ref[mine, z, :, ends[side]] * flag
            face = jnp.where(low, zero, face) if c else jnp.where(low, face, zero)
            planes[z + 1][c] = planes[z + 1][c] + face
            rims = []
            for i in (edge + 2, edge + 3):
                pair = [arrived_tile(side, k, i, d)[z : z + 1] for d in range(2)]
                rims.append([jnp.broadcast_to(r, (8, LANES)) for r in pair])
            before.append(rims[0])
            after.append(rims[1])
        return planes, before + [[None, None]], after + [[None, None]]

    blocks = []
    for k in range(slabs):
        blocks += [own_block(0, k), own_block(1, k), far_block(0, k), far_block(1, k)]
    count = len(blocks) * 8
    for i in range(edge + 2):
        for q in range(0, len(blocks), 2):
            shifts = [three_shifts(p[i], r[i], s[i]) for p, r, s in blocks[q : q + 2]]
            at = i * count + q * 8
            for dy in range(3):
                for c in range(2):
                    block = jnp.concatenate([shifts[0][dy][c], shifts[1][dy][c]], axis=0)
                    side_ref[dy, at : at + 16, tile_of(c)] = block.astype(BF16)

    for b in range(bricks + 1):
        for z in range(edge):
            for side in range(2):
                edge_ref[b, z, :, tile_of(side)] = rt2_ref[b, z, :, ends[side]]

    def side_window(dy, at, n):
        return side_ref[dy, at : at + n, :]

    result = convolve([side_window], count, edge, band1_ref)
    bias = bias2_ref[0:1, :]
    for z in range(edge):
        value = jnp.maximum(result(0, z) + bias, 0.0)
        for k in range(slabs):
            for side in range(2):
                at = (4 * k + side) * 8
                brick = tables.receiver(side, k)
                inside = jnp.minimum(brick, bricks - 1)
                from_row = pl.multiple_of((z * bricks + inside) * edge, edge)
                new = half(value[at : at + 8] * mask_ref[pl.ds(from_row, edge), ends[side]])
                old = edge_ref[brick, z, :, tile_of(side)]
                new = jnp.where(low, new, old) if side else jnp.where(low, old, new)
                edge_ref[brick, z, :, tile_of(side)] = jnp.where(brick < bricks, new, old)
                at += 16
                far = half(value[at : at + 8]) * arrived_tile(side, k, z + 1, side)
                edge_ref[bricks + 1 + k, z, :, tile_of(1 - side)] = far

    outer = [(tables.rim(b, 0), tables.rim(b, 1)) for b in range(bricks)]

    @pl.when(tables.live())
    def _():
        def own(b, z):
            left, right = edge_ref[outer[b][0], z, :, tile_of(1)], edge_ref[outer[b][1], z, :, tile_of(0)]
            return [left, edge_ref[b, z, :, tile_of(0)], edge_ref[b, z, :, tile_of(1)], right]

        def rim(brick, z):
            return [None, edge_ref[brick, z, :, tile_of(0)], edge_ref[brick, z, :, tile_of(1)], None]

        fill_padded(pad_ref, tables, edge, own, rim, [(0, 1), (2, 3)])

        def low_window(dy, at, n):
            return jnp.concatenate(
                [pad_ref[dy, at : at + n, tile_of(0)], pad2_ref[dy, at : at + n, tile_of(0)]], axis=1
            )

        def high_window(dy, at, n):
            return jnp.concatenate(
                [pad2_ref[dy, at : at + n, tile_of(tiles - 2)], pad_ref[dy, at : at + n, tile_of(1)]],
                axis=1,
            )

        result = convolve([low_window, high_window], rows, edge, band2_ref)
        bias = bias2_ref[1:2, :]
        for side in range(2):
            for z in range(edge):
                keep = mask_ref[z * rows : (z + 1) * rows, ends[side]]
                value = jnp.maximum(result(side, z) + bias, 0.0) * keep
                for b in range(bricks):
                    out_ref[b, z, :, tile_of(side)] = value[b * edge : (b + 1) * edge].astype(BF16)
        choose_parcels(tables, out_ref, fa_ref, fb_ref)


def pick_second(frame_refs):
    ga_ref, gb_ref = frame_refs
    odd = lax.rem(lax.axis_index("frame"), 2) == 1
    return (
        lambda slot: jnp.where(odd, ga_ref[slot], gb_ref[slot]),
        lambda slot: jnp.where(odd, gb_ref[slot], ga_ref[slot]),
    )


def pick_third(frame_refs):
    frame = lax.rem(lax.axis_index("frame"), 3)

    def choose(slot, turn):
        first, second, third = (ref[slot] for ref in frame_refs)
        return jnp.where(turn == 0, first, jnp.where(turn == 1, second, third))

    return (lambda slot: choose(slot, lax.rem(frame + 2, 3)), lambda slot: choose(slot, frame))


def temporal_part(tables, tiles, rt_ref, mask_ref, hid_ref, picks, band, b, put, own_ref=None):
    bricks, edge, _, part = (hid_ref if own_ref is None else own_ref).shape
    from_prior, from_later = picks

    def flat(block):
        return block.astype(F32).reshape(edge * edge, part)

    prior, later = tables.prior_ref[0, b], tables.later_ref[0, b]
    at_prior = jnp.clip(prior, 0, tables.slots - 1)
    at_later = jnp.clip(later, 0, tables.slots - 1)
    before = flat(from_prior(at_prior))
    after = flat(from_later(at_later))
    before = jnp.where(prior >= 0, before, 0.0).astype(BF16)
    after = jnp.where(later >= 0, after, 0.0).astype(BF16)
    fields = (before, after)
    if own_ref is None:
        fields = (before, flat(hid_ref[b]).astype(BF16), after)
    lhs = [
        jnp.concatenate([f[:, tile_of(k)] for f in fields], axis=1)
        for k in range(len(tiles))
    ]
    total = jnp.dot(jnp.concatenate(lhs, axis=0), band, preferred_element_type=F32)
    for k, tile in enumerate(tiles):
        for z in range(edge):
            at = (z * bricks + b) * edge
            keep = mask_ref[at : at + edge, tile_of(tile)]
            row = k * edge * edge + z * edge
            if own_ref is None:
                own = half(rt_ref[b, z, :, tile_of(tile)])
            else:
                own = own_ref[b, z, :, tile_of(k)]
            sums = own + total[row : row + edge]
            put(b, z, k, (keep * sums).astype(BF16))


def middle_out_kernel(*refs):
    tables, refs = Tables(refs[:6]), refs[6:]
    middle_out_body(tables, *refs)


def middle_out_body(
    tables,
    rt_ref,
    mask_ref,
    hid_ref,
    ga_ref,
    gb_ref,
    gc_ref,
    w_ref,
    edges_ref,
    out_ref,
    band_ref,
    own_ref,
):
    depth = w_ref.shape[1]
    blank = jnp.zeros((depth, depth), BF16)
    for i in range(3):
        at = 2 * i * depth
        band_ref[at : at + depth, :] = jnp.concatenate([w_ref[i], blank], axis=1)
        band_ref[at + depth : at + 2 * depth, :] = jnp.concatenate([blank, w_ref[i]], axis=1)
    tiles = rt_ref.shape[-1] // LANES

    def put(b, z, k, value):
        out_ref[b, z, :, tile_of(k)] = value

    band = band_ref[...]
    edge = rt_ref.shape[1]
    for b in range(tables.bricks):
        here = edges_ref[b].astype(F32).reshape(edge * edge, 2 * LANES).astype(BF16)
        lhs = jnp.concatenate([here[:, tile_of(0)], here[:, tile_of(1)]], axis=0)
        total = jnp.dot(lhs, band[2 * depth : 4 * depth, :], preferred_element_type=F32)
        for k, tile in enumerate((0, tiles - 1)):
            for z in range(edge):
                row = (k * edge + z) * edge
                own_ref[b, z, :, tile_of(k)] = (
                    half(rt_ref[b, z, :, tile_of(tile)]) + total[row : row + edge]
                )
        temporal_part(
            tables,
            list(range(1, tiles - 1)),
            rt_ref,
            mask_ref,
            hid_ref,
            pick_third((ga_ref, gb_ref, gc_ref)),
            band,
            b,
            put,
        )


def edge_out_kernel(*refs):
    tables, refs = Tables(refs[:6]), refs[6:]
    edge_out_body(tables, *refs)


def edge_out_body(
    tables,
    mask_ref,
    own_ref,
    ga_ref,
    gb_ref,
    band_ref,
    middle_ref,
    out_hbm,
    held_ref,
    sems,
):
    tiles = mask_ref.shape[-1] // LANES
    wide = tiles * LANES
    copies = [
        pltpu.make_async_copy(
            middle_ref, out_hbm.at[0, :, :, :, LANES : wide - LANES], sems.at[2 * tables.bricks]
        )
    ]
    copies[0].start()

    def put(b, z, k, value):
        held_ref[k, b, z] = value

    third = band_ref.shape[0] // 3
    band = jnp.concatenate([band_ref[0:third, :], band_ref[2 * third :, :]], axis=0)
    for b in range(tables.bricks):
        temporal_part(
            tables,
            [0, tiles - 1],
            None,
            mask_ref,
            None,
            pick_second((ga_ref, gb_ref)),
            band,
            b,
            put,
            own_ref,
        )
        for k, tile in enumerate((0, tiles - 1)):
            copies.append(
                pltpu.make_async_copy(
                    held_ref.at[k, b], out_hbm.at[0, b, :, :, tile_of(tile)], sems.at[2 * b + k]
                )
            )
            copies[-1].start()
    for copy in copies:
        copy.wait()


VMEM = pl.BlockSpec(memory_space=pltpu.VMEM)
HBM = pl.BlockSpec(memory_space=pltpu.HBM)


def in_hbm(*arrays):
    return [pltpu.with_memory_space_constraint(a, pltpu.HBM) for a in arrays]


def cost(flops, moved):
    return pl.CostEstimate(flops=flops, bytes_accessed=moved, transcendentals=0)


def per_device(
    swaps,
    features,
    occupancy,
    w_spatial,
    b_spatial,
    w_temporal,
    face_send,
    face_source,
    send_ahead,
    from_prior,
    send_back,
    from_later,
):
    _, bricks, edge, _, wide = features.shape
    slabs = face_send.shape[1] // 2
    slots = send_ahead.shape[1]
    rows = bricks * edge * edge
    depth = w_spatial.shape[2]
    shape = jax.ShapeDtypeStruct
    space_first, space_second, frame_first, frame_second, thirds = swaps
    parcel = shape((slabs * (edge + 4) * 8, 2 * LANES), BF16)
    field = shape((bricks + 1, edge, edge, wide), F32)
    arguments = (
        face_send,
        face_source,
        send_ahead,
        from_prior,
        send_back,
        from_later,
        occupancy,
        features,
        w_spatial,
        b_spatial,
        w_temporal,
    )
    *table, rolled, mask, parcel_a, parcel_b, w_held, b_held, wt_held = pl.pallas_call(
        pack_kernel,
        name="pack",
        out_shape=tuple(shape(a.shape, a.dtype) for a in arguments[:6])
        + (field, shape((rows, wide), F32), parcel, parcel)
        + tuple(shape(a.shape, a.dtype) for a in arguments[8:]),
        in_specs=[HBM] * 11,
        out_specs=(VMEM,) * 13,
        scratch_shapes=[pltpu.VMEM(a.shape, a.dtype) for a in arguments[6:8]]
        + [pltpu.SemaphoreType.DMA((11,))],
        compiler_params=pltpu.CompilerParams(vmem_limit_bytes=8 << 20),
        cost_estimate=cost(10**8, 10**6),
    )(*in_hbm(*arguments))
    space_a = lax.ppermute(parcel_a, AXES, space_first)
    space_b = lax.ppermute(parcel_b, AXES, space_second)

    half_wide = wide // 2
    band = shape((48 * depth, 2 * LANES), BF16)
    pad_rows = (edge + 2) * bricks * edge
    hidden = shape((bricks, edge, edge, half_wide), BF16)
    sent = shape((slots, edge, edge, half_wide), BF16)
    rolled2, pad2, band1, band2, bias2, middle, *parcels = pl.pallas_call(
        inner_kernel,
        name="inner",
        out_shape=(
            field,
            shape((3, pad_rows, wide - LANES), BF16),
            band,
            band,
            shape((2, LANES), F32),
            hidden,
            sent,
            sent,
            sent,
        ),
        in_specs=[VMEM] * 10,
        out_specs=(VMEM,) * 9,
        scratch_shapes=[pltpu.VMEM((3, pad_rows, wide + LANES), BF16)],
        compiler_params=pltpu.CompilerParams(vmem_limit_bytes=24 << 20),
        cost_estimate=cost(10**9, 4 * 10**6),
    )(*table, rolled, mask, w_held, b_held)
    middles = [swap(parcel, turn) for parcel, turn in zip(parcels, thirds)]

    edges, parcel_a, parcel_b = pl.pallas_call(
        border_kernel,
        name="border",
        out_shape=(hidden, sent, sent),
        in_specs=[VMEM] * 15,
        out_specs=(VMEM,) * 3,
        scratch_shapes=[
            pltpu.VMEM((bricks + 1 + slabs, edge, edge, 2 * LANES), F32),
            pltpu.VMEM((3, (edge + 2) * 32 * slabs, 2 * LANES), BF16),
            pltpu.VMEM((3, pad_rows, 2 * LANES), BF16),
        ],
        compiler_params=pltpu.CompilerParams(vmem_limit_bytes=16 << 20),
        cost_estimate=cost(5 * 10**8, 2 * 10**6),
    )(*table, rolled, mask, rolled2, pad2, band1, band2, bias2, space_a, space_b)
    edge_a = swap(parcel_a, frame_first)
    edge_b = swap(parcel_b, frame_second)

    middle_out, band, own = pl.pallas_call(
        middle_out_kernel,
        name="middle_out",
        out_shape=(hidden, shape((6 * depth, LANES), BF16), shape(hidden.shape, F32)),
        in_specs=[VMEM] * 14,
        out_specs=(VMEM,) * 3,
        compiler_params=pltpu.CompilerParams(vmem_limit_bytes=8 << 20),
        cost_estimate=cost(10**8, 10**6),
    )(*table, rolled, mask, middle, *middles, wt_held, edges)
    return pl.pallas_call(
        edge_out_kernel,
        name="edge_out",
        out_shape=shape(features.shape, BF16),
        in_specs=[VMEM] * 12,
        out_specs=HBM,
        scratch_shapes=[
            pltpu.VMEM((2, bricks, edge, edge, LANES), BF16),
            pltpu.SemaphoreType.DMA((2 * bricks + 1,)),
        ],
        compiler_params=pltpu.CompilerParams(vmem_limit_bytes=8 << 20),
        cost_estimate=cost(10**8, 10**6),
    )(*table, mask, own, edge_a, edge_b, band, middle_out)


def solution(mesh):
    swaps = swap_pairs(mesh.shape["space"], mesh.shape["frame"])
    in_specs = (
        P("frame", "space", None, None, None),
        P("frame", "space", None),
        P(),
        P(),
        P(),
        P("frame", "space"),
        P("frame", "space", None),
        P("frame", "space"),
        P("frame", "space"),
        P("frame", "space"),
        P("frame", "space"),
    )
    out_specs = P("frame", "space", None, None, None)
    return jax.shard_map(
        functools.partial(per_device, swaps),
        mesh=mesh,
        in_specs=in_specs,
        out_specs=out_specs,
        check_vma=False,
    )
```
